32 devices in a mesh: fsdp: 4 (over y, core), ctx: 8 (over z, x).
Axes of the slice: x: 2, y: 2, z: 4, core: 2. Of those that a mesh axis runs over, the one named last changes fastest.
Arguments:
- tokens_in: bfloat16 [4, 2048, 1024], P('fsdp', 'ctx'), may hold values from -6 to 6
- block_ids: int32 [4, 2048], P('fsdp', 'ctx'), may hold values from 0 to 9, never falling along the last dimension, each value on 1 to 256 neighbouring positions
- w_query: bfloat16 [1024, 1024], P(('fsdp', 'ctx')), may hold values from -0.1875 to 0.1875
- w_key: bfloat16 [1024, 1024], P(('fsdp', 'ctx')), may hold values from -0.1875 to 0.1875
- w_value: bfloat16 [1024, 1024], P(('fsdp', 'ctx')), may hold values from -0.1875 to 0.1875
- w_out: bfloat16 [1024, 1024], P(('fsdp', 'ctx')), may hold values from -1.5 to 1.5
- w_up: bfloat16 [1024, 4096], P(('fsdp', 'ctx')), may hold values from -0.1875 to 0.1875
- w_down: bfloat16 [4096, 1024], P(('fsdp', 'ctx')), may hold values from -0.09375 to 0.09375
- norm_gain: bfloat16 [4, 1024], P(None, ('fsdp', 'ctx')), may hold values from 0.5 to 1.5
- cotangent: bfloat16 [4, 2048, 1024], P('fsdp', 'ctx'), may hold values from -6 to 6
Outputs:
- layer_out: bfloat16 [4, 2048, 1024], P('fsdp', 'ctx')
- grad_tokens: bfloat16 [4, 2048, 1024], P('fsdp', 'ctx')
- grad_query: float32 [1024, 1024], P(('fsdp', 'ctx'))
- grad_key: float32 [1024, 1024], P(('fsdp', 'ctx'))
- grad_value: float32 [1024, 1024], P(('fsdp', 'ctx'))
- grad_out: float32 [1024, 1024], P(('fsdp', 'ctx'))
- grad_up: float32 [1024, 4096], P(('fsdp', 'ctx'))
- grad_down: float32 [4096, 1024], P(('fsdp', 'ctx'))
- grad_gain: float32 [4, 1024], P(None, ('fsdp', 'ctx'))
The draws below stay inside these ranges and needn't reach their ends.
Inputs may be any that keep to these rules, and one draw needn't show every extreme that they name: `block_ids`: along each sequence block numbers never fall; every block has 1 to 256 positions and one has exactly 256.
All inputs are finite; a program needn't handle non-finite values.
Results may differ from the reference program's by a relative error of at most 0.018.
Values may be sent and summed in bfloat16 or wider, within the bound.
A program may use at most 256 MiB of HBM per device.

```python
import math
import jax
import jax.numpy as jnp
import numpy as np
from jax import lax

D = 1024
HEADS = 16
HD = 64
FF = 4096
BLOCK = 256
SEQS = 4
LEN = 2048
NBLOCK = 10


def steps_of(key, extent, shards, low, top_value):
    factor_of = 1.0
    for position, blocks in shards:
        draws = jax.random.uniform(jax.random.fold_in(jax.random.fold_in(key, 6), position), (blocks,), jnp.float32, low / len(shards), top_value / len(shards))
        factor_of = factor_of * jnp.repeat(jnp.exp(draws), extent[position] // blocks).reshape((-1,) + (1,) * (len(extent) - 1 - position))
    return factor_of


def length_profile(amount, total, most, lean):
    weights = [(1 << 20) // math.isqrt(grade ** lean) + 1 for grade in range(2, amount + 1)]
    rest, given = total - most - (amount - 1), [1] * (amount - 1)
    while rest > 0:
        movable = [i for i in range(amount - 1) if given[i] < most]
        pool, left = sum([weights[i] for i in movable]), rest
        for i in movable:
            more = min(most - given[i], max(1, left * weights[i] // pool), rest)
            given[i] = given[i] + more
            rest = rest - more
    return np.array([most] + given)


def ragged(stream_key, count, total, limit, slope):
    if count == 2:
        one = jax.random.randint(stream_key, (), max(1, total - limit), min(limit, total - 1) + 1)
        return jnp.stack([one, total - one])
    lengths = jnp.asarray(length_profile(count, total, limit, slope), jnp.int32)
    couples = (count - 1) // 2
    donor, taker = lengths[1:1 + 2 * couples:2], lengths[2:2 + 2 * couples:2]
    room = jnp.minimum(donor - 1, limit - taker)
    shifted = jax.random.randint(jax.random.fold_in(stream_key, 1), (couples,), 0, 1 << 20) % (room + 1)
    lengths = lengths.at[1:1 + 2 * couples:2].set(donor - shifted).at[2:2 + 2 * couples:2].set(taker + shifted)
    return lengths[jax.random.permutation(jax.random.fold_in(stream_key, 2), count)]


def gaussian(own_key, extent, scale, most, cuts=(), held_as=jnp.bfloat16):
    entries = scale * jax.random.normal(own_key, extent, jnp.float32)
    if cuts:
        entries = entries * steps_of(own_key, extent, cuts, -0.22, 0.18)
    return jnp.clip(entries, -most, most).astype(held_as)


def setup_inputs(seed: int = 0) -> dict:
    streams_of = jax.random.split(jax.random.key(seed), 11)
    tokens_in = gaussian(streams_of[0], (SEQS, LEN, D), 1.0, 6.0, ((0, 4), (1, 8)))
    block_ids = jax.vmap(lambda own: jnp.searchsorted(jnp.cumsum(ragged(own, NBLOCK, LEN, BLOCK, 0)), jnp.arange(LEN), side="right"))(jax.random.split(streams_of[1], SEQS)).reshape((SEQS, LEN)).astype(jnp.int32)
    w_query = gaussian(streams_of[2], (D, D), D ** -0.5, 0.1875, ((0, 32),))
    w_key = gaussian(streams_of[3], (D, D), D ** -0.5, 0.1875, ((0, 32),))
    w_value = gaussian(streams_of[4], (D, D), D ** -0.5, 0.1875, ((0, 32),))
    w_out = gaussian(streams_of[5], (D, D), (D // 64) ** -0.5, 1.5, ((0, 32),))
    w_up = gaussian(streams_of[6], (D, FF), D ** -0.5, 0.1875, ((0, 32),))
    w_down = gaussian(streams_of[7], (FF, D), FF ** -0.5, 0.09375, ((0, 32),))
    norm_gain = jnp.clip(1.0 + 0.1 * jax.random.normal(streams_of[8], (4, D), jnp.float32), 0.5, 1.5).astype(jnp.bfloat16)
    cotangent = gaussian(streams_of[9], (SEQS, LEN, D), 1.0, 6.0, ((0, 4), (1, 8)))
    return dict(tokens_in=tokens_in, block_ids=block_ids, w_query=w_query, w_key=w_key, w_value=w_value, w_out=w_out, w_up=w_up, w_down=w_down, norm_gain=norm_gain, cotangent=cotangent)


@jax.custom_vjp
def low(v):
    return lax.optimization_barrier(v.astype(jnp.bfloat16)).astype(jnp.float32)

@jax.custom_vjp
def low_back(v):
    return v

def low_keep(v):
    return (low(v), None)

def low_pass(kept, grad):
    return (grad,)

def back_keep(v):
    return (v, None)

def back_low(kept, grad):
    return (low(grad),)
low.defvjp(low_keep, low_pass)
low_back.defvjp(back_keep, back_low)
EPS = 1e-05
HIGH = lax.Precision.HIGHEST
MASKED = -1e+30

def layer_norm(values, gain):
    centre = values - lax.optimization_barrier(jnp.mean(values, axis=-1, keepdims=True))
    spread = lax.optimization_barrier(jnp.mean(centre * centre, axis=-1, keepdims=True))
    return centre * lax.rsqrt(spread + EPS) * gain

def matmul(left, right):
    return jnp.dot(left, right, precision=HIGH, preferred_element_type=jnp.float32)

def attention(queries, keys, values, blocks):
    length = queries.shape[0]
    block_rows = min(512, length)
    scale = 1.0 / jnp.sqrt(jnp.float32(HD))
    head_keys = keys.reshape(length, HEADS, HD)
    head_values = values.reshape(length, HEADS, HD)

    def one_block(item):
        query_part, block_part = item
        head_queries = query_part.reshape(block_rows, HEADS, HD)
        scores = low_back(jnp.einsum('qhd,khd->hqk', head_queries, head_keys, precision=HIGH) * scale)
        allowed = blocks[None, None, :] <= block_part[None, :, None]
        scores = jnp.where(allowed, scores, MASKED)
        probs = jax.nn.softmax(scores, axis=-1)
        mixed = jnp.einsum('hqk,khd->qhd', low(probs), head_values, precision=HIGH)
        return mixed.reshape(block_rows, HEADS * HD)
    pieces = lax.map(jax.checkpoint(one_block), (queries.reshape(length // block_rows, block_rows, HEADS * HD), blocks.reshape(length // block_rows, block_rows)))
    return pieces.reshape(length, HEADS * HD)

def layer(tokens, w_query, w_key, w_value, w_out, w_up, w_down, gains, blocks):
    normed = low(layer_norm(tokens, gains[0]))
    queries = low_back(low(matmul(normed, w_query)))
    keys = low_back(low(matmul(normed, w_key)))
    values = low_back(low(matmul(normed, w_value)))
    mixed = low_back(low(attention(queries, keys, values, blocks)))
    branch = low_back(matmul(mixed, w_out))
    hidden = tokens + layer_norm(branch, gains[1])
    inner = low(layer_norm(hidden, gains[2]))
    lifted = low_back(matmul(inner, w_up))
    active = low(jax.nn.gelu(lifted, approximate=False))
    lowered = low_back(matmul(active, w_down))
    return hidden + layer_norm(lowered, gains[3])

def reference(tokens_in, block_ids, w_query, w_key, w_value, w_out, w_up, w_down, norm_gain, cotangent):
    params = tuple((weight.astype(jnp.float32) for weight in (w_query, w_key, w_value, w_out, w_up, w_down, norm_gain)))

    def per_sequence(totals, item):
        sequence, blocks, upstream = item

        def forward(inputs, *weights):
            return layer(inputs, *weights, blocks)
        result, pullback = jax.vjp(forward, sequence.astype(jnp.float32), *params)
        grads = pullback(upstream.astype(jnp.float32))
        totals = tuple((total + grad for total, grad in zip(totals, grads[1:])))
        return (totals, (result.astype(jnp.bfloat16), grads[0].astype(jnp.bfloat16)))
    zeros = tuple((jnp.zeros_like(weight) for weight in params))
    totals, outputs = lax.scan(per_sequence, zeros, (tokens_in, block_ids, cotangent))
    return (outputs[0], outputs[1], totals[0], totals[1], totals[2], totals[3], totals[4], totals[5], totals[6])
```

```python
import math

import jax
import jax.numpy as jnp
from jax import lax
from jax.experimental import pallas as pl
from jax.experimental.pallas import tpu as pltpu
from jax.sharding import PartitionSpec as P

HEADS = 16
HD = 64


EPS = 1e-05
MASKED = -1e30


def from_behind(block, axis, distance):
    devices = range(lax.axis_size(axis))
    route = [((i - distance) % len(devices), i) for i in devices]
    return lax.ppermute(block, axis, route)


def layer_norm(values, gain):
    centre = values - jnp.mean(values, axis=-1, keepdims=True)
    spread = jnp.mean(centre * centre, axis=-1, keepdims=True)
    return centre * lax.rsqrt(spread + EPS) * gain


def gelu_exact(values):
    return jax.nn.gelu(values, approximate=False)


def project(left, right):
    return jnp.dot(left, right, preferred_element_type=jnp.float32)


def outer_sum(left, right):
    return lax.dot_general(
        left, right, (((0,), (0,)), ((), ())), preferred_element_type=jnp.float32
    )


def back_project(grad, weight):
    return lax.dot_general(
        grad, weight, (((1,), (1,)), ((), ())), preferred_element_type=jnp.float32
    )


def split_heads(values):
    return values.reshape(values.shape[0], HEADS, HD)


def attend(carry, head_queries, query_blocks, key_rows, key_blocks, scale):
    best, total, accum = carry
    width = key_rows.shape[1] // 2
    keys = split_heads(key_rows[:, :width])
    values = split_heads(key_rows[:, width:])
    scores = (
        jnp.einsum("qhd,khd->hqk", head_queries, keys, preferred_element_type=jnp.float32) * scale
    )
    allowed = key_blocks[None, None, :] <= query_blocks[None, :, None]
    scores = jnp.where(allowed, scores, MASKED)
    newest = jnp.maximum(best, jnp.max(scores, axis=2))
    weights = jnp.where(allowed, jnp.exp(scores - newest[:, :, None]), 0.0)
    factor = jnp.exp(best - newest)
    total = total * factor + jnp.sum(weights, axis=2)
    update = jnp.einsum(
        "hqk,khd->qhd", weights.astype(jnp.bfloat16), values, preferred_element_type=jnp.float32
    )
    accum = accum * jnp.transpose(factor)[:, :, None] + update
    return (newest, total, accum)


def score_grads(
    head_queries, head_grads, log_total, delta, query_blocks, key_rows, key_blocks, scale
):
    width = key_rows.shape[1] // 2
    rows = key_rows.shape[0]
    query_rows = head_queries.shape[0]
    keys = split_heads(key_rows[:, :width])
    values = split_heads(key_rows[:, width:])
    scores = (
        jnp.einsum("qhd,khd->hqk", head_queries, keys, preferred_element_type=jnp.float32) * scale
    )
    allowed = key_blocks[None, None, :] <= query_blocks[None, :, None]
    probs = jnp.where(
        allowed, jnp.exp(jnp.where(allowed, scores, MASKED) - log_total[:, :, None]), 0.0
    )
    grad_values = jnp.einsum(
        "hqk,qhd->khd", probs.astype(jnp.bfloat16), head_grads, preferred_element_type=jnp.float32
    )
    grad_probs = jnp.einsum("qhd,khd->hqk", head_grads, values, preferred_element_type=jnp.float32)
    grad_scores = (probs * (grad_probs - delta[:, :, None])).astype(jnp.bfloat16)
    grad_queries = (
        jnp.einsum("hqk,khd->qhd", grad_scores, keys, preferred_element_type=jnp.float32) * scale
    )
    grad_keys = (
        jnp.einsum("hqk,qhd->khd", grad_scores, head_queries, preferred_element_type=jnp.float32)
        * scale
    )
    joined = jnp.concatenate(
        [grad_keys.reshape(rows, width), grad_values.reshape(rows, width)], axis=1
    )
    return (grad_queries.reshape(query_rows, width), joined)


def guarded(head_queries, head_grads, log_total, delta, query_blocks, key_rows, key_blocks, scale):
    live = jnp.min(key_blocks) <= jnp.max(query_blocks)
    rows, columns = key_rows.shape

    def run(unused):
        return score_grads(
            head_queries, head_grads, log_total, delta, query_blocks, key_rows, key_blocks, scale
        )

    def skip(unused):
        return (
            jnp.zeros((head_queries.shape[0], columns // 2), jnp.float32),
            jnp.zeros((rows, columns), jnp.float32),
        )

    return lax.cond(live, run, skip, 0)


def body(tokens_in, block_ids, w_query, w_key, w_value, w_out, w_up, w_down, norm_gain, cotangent):
    scale = 1.0 / math.sqrt(HD)
    stride = tokens_in.shape[1]
    width = tokens_in.shape[2]
    cycle_size = lax.axis_size("ctx")
    place = lax.axis_index("ctx")
    shards = (w_query, w_key, w_value, w_out, w_up, w_down, norm_gain)
    gathered = (
        lax.all_gather(w_query, ("fsdp", "ctx"), axis=0, tiled=True),
        lax.all_gather(w_key, ("fsdp", "ctx"), axis=0, tiled=True),
        lax.all_gather(w_value, ("fsdp", "ctx"), axis=0, tiled=True),
        lax.all_gather(w_out, ("fsdp", "ctx"), axis=0, tiled=True),
        lax.all_gather(w_up, ("fsdp", "ctx"), axis=0, tiled=True),
        lax.all_gather(w_down, ("fsdp", "ctx"), axis=0, tiled=True),
        lax.all_gather(norm_gain, ("fsdp", "ctx"), axis=1, tiled=True),
    )
    full_query, full_key, full_value, full_out, full_up, full_down, full_gain = gathered
    gains = full_gain.astype(jnp.float32)
    sequence_blocks = lax.all_gather(block_ids, "ctx", axis=1, tiled=True)[0]
    own_blocks = block_ids[0]
    top_block = jnp.max(own_blocks)
    tokens = tokens_in[0].astype(jnp.float32)
    normed = layer_norm(tokens, gains[0]).astype(jnp.bfloat16)
    queries = project(normed, full_query).astype(jnp.bfloat16)
    key_value = jnp.concatenate(
        [project(normed, full_key), project(normed, full_value)], axis=1
    ).astype(jnp.bfloat16)
    head_queries = split_heads(queries)
    start_state = (
        jnp.full((HEADS, stride), MASKED, jnp.float32),
        jnp.zeros((HEADS, stride), jnp.float32),
        jnp.zeros((stride, HEADS, HD), jnp.float32),
    )
    piece = lax.all_gather(key_value, "ctx", axis=0, tiled=True)
    rows = piece.shape[0]
    size = math.gcd(rows, stride)

    def visit(index, state):
        key_rows = lax.dynamic_slice_in_dim(piece, index * size, size, 0)
        key_blocks = lax.dynamic_slice_in_dim(sequence_blocks, index * size, size, 0)
        return lax.cond(
            jnp.min(key_blocks) <= top_block,
            lambda inner: attend(inner, head_queries, own_blocks, key_rows, key_blocks, scale),
            lambda inner: inner,
            state,
        )

    best, total, accum = lax.fori_loop(0, rows // size, visit, start_state)
    mixed = accum / jnp.transpose(total)[:, :, None]
    log_total = best + jnp.log(total)
    mixed_low = mixed.reshape(stride, width).astype(jnp.bfloat16)
    branch = project(mixed_low, full_out)
    hidden = tokens + layer_norm(branch, gains[1])
    inner = layer_norm(hidden, gains[2]).astype(jnp.bfloat16)
    lifted = project(inner, full_up)
    active = gelu_exact(lifted).astype(jnp.bfloat16)
    lowered = project(active, full_down)
    layer_out = (hidden + layer_norm(lowered, gains[3])).astype(jnp.bfloat16)[None]
    regathered = (
        lax.all_gather(shards[0], ("fsdp", "ctx"), axis=0, tiled=True),
        lax.all_gather(shards[1], ("fsdp", "ctx"), axis=0, tiled=True),
        lax.all_gather(shards[2], ("fsdp", "ctx"), axis=0, tiled=True),
        lax.all_gather(shards[3], ("fsdp", "ctx"), axis=0, tiled=True),
        lax.all_gather(shards[4], ("fsdp", "ctx"), axis=0, tiled=True),
        lax.all_gather(shards[5], ("fsdp", "ctx"), axis=0, tiled=True),
        lax.all_gather(shards[6], ("fsdp", "ctx"), axis=1, tiled=True),
    )
    back_query, back_key, back_value, back_out, back_up, back_down, back_gain = regathered
    back_gains = back_gain.astype(jnp.float32)
    upstream = cotangent[0].astype(jnp.float32)
    unused_four, pull_four = jax.vjp(layer_norm, lowered, back_gains[3])
    grad_lowered, gain_four = pull_four(upstream)
    grad_lowered = grad_lowered.astype(jnp.bfloat16)
    grad_down = outer_sum(active, grad_lowered)
    grad_active = back_project(grad_lowered, back_down)
    unused_gelu, pull_gelu = jax.vjp(gelu_exact, lifted)
    grad_lifted = pull_gelu(grad_active)[0].astype(jnp.bfloat16)
    grad_up = outer_sum(inner, grad_lifted)
    grad_inner = back_project(grad_lifted, back_up)
    unused_three, pull_three = jax.vjp(layer_norm, hidden, back_gains[2])
    grad_hidden_branch, gain_three = pull_three(grad_inner)
    grad_hidden = upstream + grad_hidden_branch
    unused_two, pull_two = jax.vjp(layer_norm, branch, back_gains[1])
    grad_branch, gain_two = pull_two(grad_hidden)
    grad_branch = grad_branch.astype(jnp.bfloat16)
    grad_out = outer_sum(mixed_low, grad_branch)
    grad_mixed = back_project(grad_branch, back_out).astype(jnp.bfloat16)
    head_grads = split_heads(grad_mixed)
    delta = jnp.transpose(jnp.sum(head_grads.astype(jnp.float32) * mixed, axis=2))
    query_grad, kv_grad = guarded(
        head_queries, head_grads, log_total, delta, own_blocks, key_value, own_blocks, scale
    )

    def pass_grads(values):
        return from_behind(values.astype(jnp.bfloat16), "ctx", 1).astype(values.dtype)

    def cycle_keys(step, state):
        travel, kv_accum, query_accum = state
        travel = from_behind(travel, "ctx", 1)
        kv_accum = pass_grads(kv_accum)
        source = (place - step) % cycle_size
        key_blocks = lax.dynamic_slice_in_dim(sequence_blocks, source * stride, stride, 0)
        part_query, part_kv = guarded(
            head_queries, head_grads, log_total, delta, own_blocks, travel, key_blocks, scale
        )
        return (travel, kv_accum + part_kv, query_accum + part_query)

    unused_travel, kv_accum, query_grad = lax.fori_loop(
        1, cycle_size, cycle_keys, (key_value, kv_grad, query_grad)
    )
    kv_grad = pass_grads(kv_accum)
    query_low = query_grad.astype(jnp.bfloat16)
    kv_low = kv_grad.astype(jnp.bfloat16)
    key_low = kv_low[:, :width]
    value_low = kv_low[:, width:]
    grad_query = outer_sum(normed, query_low)
    grad_key = outer_sum(normed, key_low)
    grad_value = outer_sum(normed, value_low)
    grad_normed = (
        back_project(query_low, back_query)
        + back_project(key_low, back_key)
        + back_project(value_low, back_value)
    )
    unused_one, pull_one = jax.vjp(layer_norm, tokens, back_gains[0])
    grad_norm_in, gain_one = pull_one(grad_normed)
    grad_tokens = (grad_hidden + grad_norm_in).astype(jnp.bfloat16)[None]
    gain_grads = jnp.stack([gain_one, gain_two, gain_three, gain_four])
    summed = (
        lax.psum_scatter(grad_query, ("fsdp", "ctx"), scatter_dimension=0, tiled=True),
        lax.psum_scatter(grad_key, ("fsdp", "ctx"), scatter_dimension=0, tiled=True),
        lax.psum_scatter(grad_value, ("fsdp", "ctx"), scatter_dimension=0, tiled=True),
        lax.psum_scatter(grad_out, ("fsdp", "ctx"), scatter_dimension=0, tiled=True),
        lax.psum_scatter(grad_up, ("fsdp", "ctx"), scatter_dimension=0, tiled=True),
        lax.psum_scatter(grad_down, ("fsdp", "ctx"), scatter_dimension=0, tiled=True),
        lax.psum_scatter(gain_grads, ("fsdp", "ctx"), scatter_dimension=1, tiled=True),
    )
    return (
        layer_out,
        grad_tokens,
        summed[0],
        summed[1],
        summed[2],
        summed[3],
        summed[4],
        summed[5],
        summed[6],
    )


TILE = 256


def nt(left, right):
    return lax.dot_general(
        left, right, (((1,), (1,)), ((), ())), preferred_element_type=jnp.float32
    )


def nn(left, right):
    return lax.dot_general(
        left, right, (((1,), (0,)), ((), ())), preferred_element_type=jnp.float32
    )


def tn(left, right):
    return lax.dot_general(
        left, right, (((0,), (0,)), ((), ())), preferred_element_type=jnp.float32
    )


def both_heads(rows):
    lane = lax.broadcasted_iota(jnp.int32, rows.shape, 1)
    zero = jnp.zeros_like(rows)
    return jnp.concatenate(
        [jnp.where(lane < HD, rows, zero), jnp.where(lane < HD, zero, rows)], axis=0
    )


def own_lanes(pair):
    half = pair.shape[0] // 2
    lane = lax.broadcasted_iota(jnp.int32, (half, pair.shape[1]), 1)
    return jnp.where(lane < HD, pair[:half], pair[half:])


def attend_kernel(query_ref, key_ref, value_ref, row_ref, col_ref, mixed_ref, log_ref, score_ref):
    tile = pl.program_id(0)
    tiles = pl.num_programs(0)
    wide = 2 * HD
    scaled = both_heads((query_ref[...].astype(jnp.float32) * HD**-0.5).astype(jnp.bfloat16))
    own = row_ref[...]
    own = jnp.concatenate([own, own], axis=0)

    def score(index, best, masked):
        at = pl.multiple_of(index * TILE, TILE)
        part = nt(scaled, key_ref[pl.ds(at, TILE), :])
        if masked:
            part = jnp.where(col_ref[:, pl.ds(at, TILE)] <= own, part, MASKED)
        score_ref[:, pl.ds(at, TILE)] = part
        for lane in range(0, TILE, wide):
            best = jnp.maximum(best, part[:, lane : lane + wide])
        return best

    best = jnp.full((2 * TILE, wide), MASKED, jnp.float32)
    best = lax.fori_loop(0, tile, lambda i, b: score(i, b, False), best)
    stop = jnp.minimum(tile + 2, tiles)
    best = lax.fori_loop(tile, stop, lambda i, b: score(i, b, True), best)
    best = jnp.max(best, axis=1, keepdims=True)

    def weigh(index, carry):
        total, accum = carry
        at = pl.multiple_of(index * TILE, TILE)
        weights = jnp.exp(score_ref[:, pl.ds(at, TILE)] - best)
        for lane in range(0, TILE, wide):
            total = total + weights[:, lane : lane + wide]
        return (total, accum + nn(weights.astype(jnp.bfloat16), value_ref[pl.ds(at, TILE), :]))

    zero = jnp.zeros((2 * TILE, wide), jnp.float32)
    total, accum = lax.fori_loop(0, stop, weigh, (zero, zero))
    total = jnp.sum(total, axis=1, keepdims=True)
    mixed_ref[...] = own_lanes(accum / total)
    log_total = jnp.broadcast_to(best + jnp.log(total), (2 * TILE, wide))
    log_ref[0] = jnp.transpose(log_total)[:8]


def attention_forward(joined, blocks):
    rows = joined.shape[0]
    wide = 2 * HD
    tiles = rows // TILE
    return pl.pallas_call(
        attend_kernel,
        grid=(tiles,),
        out_shape=(
            jax.ShapeDtypeStruct((rows, wide), jnp.float32),
            jax.ShapeDtypeStruct((tiles, 8, 2 * TILE), jnp.float32),
        ),
        in_specs=[
            pl.BlockSpec((TILE, wide), lambda t: (t, 0)),
            pl.BlockSpec((rows, wide), lambda t: (0, 1)),
            pl.BlockSpec((rows, wide), lambda t: (0, 2)),
            pl.BlockSpec((TILE, 1), lambda t: (t, 0)),
            pl.BlockSpec((1, rows), lambda t: (0, 0)),
        ],
        out_specs=(
            pl.BlockSpec((TILE, wide), lambda t: (t, 0)),
            pl.BlockSpec((1, 8, 2 * TILE), lambda t: (t, 0, 0)),
        ),
        scratch_shapes=[pltpu.VMEM((2 * TILE, rows), jnp.float32)],
        name="attention_forward",
    )(joined, joined, joined, blocks.reshape(rows, 1), blocks.reshape(1, rows))


def grads_kernel(
    query_ref, key_ref, value_ref, grad_ref, mixed_ref, log_ref, row_ref, col_ref, out_ref, key_sum, value_sum
):
    tile = pl.program_id(0)
    tiles = pl.num_programs(0)
    wide = 2 * HD

    @pl.when(tile == 0)
    def _():
        key_sum[...] = jnp.zeros_like(key_sum)
        value_sum[...] = jnp.zeros_like(value_sum)

    scaled = both_heads((query_ref[...].astype(jnp.float32) * HD**-0.5).astype(jnp.bfloat16))
    grads = both_heads(grad_ref[...])
    products = grad_ref[...].astype(jnp.float32) * mixed_ref[...]
    products = jnp.transpose(products)
    delta = jnp.concatenate(
        [
            jnp.sum(products[:HD], axis=0, keepdims=True),
            jnp.sum(products[HD:], axis=0, keepdims=True),
        ],
        axis=1,
    )
    log_total = log_ref[0, :1]
    own = col_ref[...]
    own = jnp.concatenate([own, own], axis=1)

    def step(index, accum, masked):
        at = pl.multiple_of(index * TILE, TILE)
        here = pl.ds(at, TILE)
        keys = key_ref[here, :]
        scores = nt(keys, scaled)
        if masked:
            scores = jnp.where(row_ref[here, :] <= own, scores, MASKED)
        probs = jnp.exp(scores - log_total)
        value_sum[here, :] += nn(probs.astype(jnp.bfloat16), grads)
        grad_scores = (probs * (nt(value_ref[here, :], grads) - delta)).astype(jnp.bfloat16)
        key_sum[here, :] += nn(grad_scores, scaled)
        return accum + tn(grad_scores, keys)

    accum = jnp.zeros((2 * TILE, wide), jnp.float32)
    accum = lax.fori_loop(0, tile, lambda i, a: step(i, a, False), accum)
    stop = jnp.minimum(tile + 2, tiles)
    accum = lax.fori_loop(tile, stop, lambda i, a: step(i, a, True), accum)
    at = pl.multiple_of(tile * TILE, TILE)
    out_ref[pl.ds(at, TILE), :wide] = (own_lanes(accum) * HD**-0.5).astype(jnp.bfloat16)

    @pl.when(tile == tiles - 1)
    def _():
        out_ref[:, wide : 2 * wide] = key_sum[...].astype(jnp.bfloat16)
        out_ref[:, 2 * wide :] = value_sum[...].astype(jnp.bfloat16)


def attention_backward(joined, grad_mixed, mixed, log_total, blocks):
    rows = joined.shape[0]
    wide = 2 * HD
    tiles = rows // TILE
    return pl.pallas_call(
        grads_kernel,
        grid=(tiles,),
        out_shape=jax.ShapeDtypeStruct((rows, 3 * wide), jnp.bfloat16),
        in_specs=[
            pl.BlockSpec((TILE, wide), lambda t: (t, 0)),
            pl.BlockSpec((rows, wide), lambda t: (0, 1)),
            pl.BlockSpec((rows, wide), lambda t: (0, 2)),
            pl.BlockSpec((TILE, wide), lambda t: (t, 0)),
            pl.BlockSpec((TILE, wide), lambda t: (t, 0)),
            pl.BlockSpec((1, 8, 2 * TILE), lambda t: (t, 0, 0)),
            pl.BlockSpec((rows, 1), lambda t: (0, 0)),
            pl.BlockSpec((1, TILE), lambda t: (0, t)),
        ],
        out_specs=pl.BlockSpec((rows, 3 * wide), lambda t: (0, 0)),
        scratch_shapes=[
            pltpu.VMEM((rows, wide), jnp.float32),
            pltpu.VMEM((rows, wide), jnp.float32),
        ],
        name="attention_backward",
    )(
        joined,
        joined,
        joined,
        grad_mixed,
        mixed,
        log_total,
        blocks.reshape(rows, 1),
        blocks.reshape(1, rows),
    )


def to_heads(rows, groups, count):
    tokens = rows.shape[0]
    wide = rows.shape[1] // (groups * count)
    split = rows.reshape(tokens, count, groups, wide).transpose(2, 0, 1, 3)
    split = split.reshape(groups, tokens, count * wide)
    whole = lax.all_to_all(split, "ctx", 0, 0, tiled=True)
    return whole.reshape(groups * tokens, count * wide)


def to_tokens(rows, groups, count):
    tokens = rows.shape[0] // groups
    wide = rows.shape[1] // count
    split = lax.all_to_all(rows.reshape(groups, tokens, count * wide), "ctx", 0, 0, tiled=True)
    split = split.reshape(groups, tokens, count, wide).transpose(1, 2, 0, 3)
    return split.reshape(tokens, count * groups * wide)


def scatter_sum(grad):
    return lax.psum_scatter(
        grad.astype(jnp.bfloat16), ("fsdp", "ctx"), scatter_dimension=0, tiled=True
    ).astype(jnp.float32)


def fast_body(
    tokens_in, block_ids, w_query, w_key, w_value, w_out, w_up, w_down, norm_gain, cotangent
):
    axes = ("fsdp", "ctx")
    width = tokens_in.shape[2]
    groups = lax.axis_size("ctx")
    full_gain = lax.all_gather(norm_gain, axes, axis=1, tiled=True)
    full_qkv = lax.all_gather(
        jnp.concatenate([w_query, w_key, w_value], axis=1), axes, axis=0, tiled=True
    )
    blocks = lax.all_gather(block_ids, "ctx", axis=1, tiled=True)[0]
    full_out = lax.all_gather(w_out, axes, axis=0, tiled=True)
    full_up = lax.all_gather(w_up, axes, axis=0, tiled=True)
    full_down = lax.all_gather(w_down, axes, axis=0, tiled=True)
    gains = full_gain.astype(jnp.float32)
    tokens = tokens_in[0].astype(jnp.float32)
    normed = layer_norm(tokens, gains[0]).astype(jnp.bfloat16)
    joined = to_heads(project(normed, full_qkv).astype(jnp.bfloat16), groups, 3)
    mixed, log_total = attention_forward(joined, blocks)
    mixed_low = to_tokens(mixed.astype(jnp.bfloat16), groups, 1)
    branch = project(mixed_low, full_out)
    hidden = tokens + layer_norm(branch, gains[1])
    inner = layer_norm(hidden, gains[2]).astype(jnp.bfloat16)
    lifted = project(inner, full_up)
    active = gelu_exact(lifted).astype(jnp.bfloat16)
    lowered = project(active, full_down)
    layer_out = (hidden + layer_norm(lowered, gains[3])).astype(jnp.bfloat16)[None]
    upstream = cotangent[0].astype(jnp.float32)
    unused_four, pull_four = jax.vjp(layer_norm, lowered, gains[3])
    grad_lowered, gain_four = pull_four(upstream)
    grad_lowered = grad_lowered.astype(jnp.bfloat16)
    grad_down = scatter_sum(outer_sum(active, grad_lowered))
    grad_active = back_project(grad_lowered, full_down)
    unused_gelu, pull_gelu = jax.vjp(gelu_exact, lifted)
    grad_lifted = pull_gelu(grad_active)[0].astype(jnp.bfloat16)
    grad_up = scatter_sum(outer_sum(inner, grad_lifted))
    grad_inner = back_project(grad_lifted, full_up)
    unused_three, pull_three = jax.vjp(layer_norm, hidden, gains[2])
    grad_hidden_branch, gain_three = pull_three(grad_inner)
    grad_hidden = upstream + grad_hidden_branch
    unused_two, pull_two = jax.vjp(layer_norm, branch, gains[1])
    grad_branch, gain_two = pull_two(grad_hidden)
    grad_branch = grad_branch.astype(jnp.bfloat16)
    grad_out = scatter_sum(outer_sum(mixed_low, grad_branch))
    grad_mixed = back_project(grad_branch, full_out).astype(jnp.bfloat16)
    grad_joined = attention_backward(
        joined, to_heads(grad_mixed, groups, 1), mixed, log_total, blocks
    )
    grad_qkv = to_tokens(grad_joined, groups, 3)
    grad_three = scatter_sum(outer_sum(normed, grad_qkv))
    grad_normed = back_project(grad_qkv, full_qkv)
    unused_one, pull_one = jax.vjp(layer_norm, tokens, gains[0])
    grad_norm_in, gain_one = pull_one(grad_normed)
    grad_tokens = (grad_hidden + grad_norm_in).astype(jnp.bfloat16)[None]
    gain_grads = jnp.stack([gain_one, gain_two, gain_three, gain_four])
    gain_sum = lax.psum_scatter(gain_grads, axes, scatter_dimension=1, tiled=True)
    return (
        layer_out,
        grad_tokens,
        grad_three[:, :width],
        grad_three[:, width : 2 * width],
        grad_three[:, 2 * width :],
        grad_out,
        grad_up,
        grad_down,
        gain_sum,
    )


def pick(mesh):
    return fast_body if mesh.shape["ctx"] * 2 == HEADS else body


def solution(mesh):
    placed = (
        P("fsdp", "ctx", None),
        P("fsdp", "ctx"),
        P(("fsdp", "ctx"), None),
        P(("fsdp", "ctx"), None),
        P(("fsdp", "ctx"), None),
        P(("fsdp", "ctx"), None),
        P(("fsdp", "ctx"), None),
        P(("fsdp", "ctx"), None),
        P(None, ("fsdp", "ctx")),
        P("fsdp", "ctx", None),
    )
    return jax.shard_map(
        pick(mesh),
        mesh=mesh,
        in_specs=placed,
        out_specs=(
            P("fsdp", "ctx", None),
            P("fsdp", "ctx", None),
            P(("fsdp", "ctx"), None),
            P(("fsdp", "ctx"), None),
            P(("fsdp", "ctx"), None),
            P(("fsdp", "ctx"), None),
            P(("fsdp", "ctx"), None),
            P(("fsdp", "ctx"), None),
            P(None, ("fsdp", "ctx")),
        ),
        check_vma=False,
    )
```

```python
import functools
import math

import jax
import jax.numpy as jnp
from jax import lax
from jax.experimental import pallas as pl
from jax.experimental.pallas import tpu as pltpu
from jax.sharding import PartitionSpec as P

HEADS = 16
HD = 64


EPS = 1e-05
MASKED = -1e30


def from_behind(block, axis, distance):
    devices = range(lax.axis_size(axis))
    route = [((i - distance) % len(devices), i) for i in devices]
    return lax.ppermute(block, axis, route)


def layer_norm(values, gain):
    centre = values - jnp.mean(values, axis=-1, keepdims=True)
    spread = jnp.mean(centre * centre, axis=-1, keepdims=True)
    return centre * lax.rsqrt(spread + EPS) * gain


def gelu_exact(values):
    return jax.nn.gelu(values, approximate=False)


def project(left, right):
    return jnp.dot(left, right, preferred_element_type=jnp.float32)


def outer_sum(left, right):
    return lax.dot_general(
        left, right, (((0,), (0,)), ((), ())), preferred_element_type=jnp.float32
    )


def back_project(grad, weight):
    return lax.dot_general(
        grad, weight, (((1,), (1,)), ((), ())), preferred_element_type=jnp.float32
    )


def split_heads(values):
    return values.reshape(values.shape[0], HEADS, HD)


def attend(carry, head_queries, query_blocks, key_rows, key_blocks, scale):
    best, total, accum = carry
    width = key_rows.shape[1] // 2
    keys = split_heads(key_rows[:, :width])
    values = split_heads(key_rows[:, width:])
    scores = (
        jnp.einsum("qhd,khd->hqk", head_queries, keys, preferred_element_type=jnp.float32) * scale
    )
    allowed = key_blocks[None, None, :] <= query_blocks[None, :, None]
    scores = jnp.where(allowed, scores, MASKED)
    newest = jnp.maximum(best, jnp.max(scores, axis=2))
    weights = jnp.where(allowed, jnp.exp(scores - newest[:, :, None]), 0.0)
    factor = jnp.exp(best - newest)
    total = total * factor + jnp.sum(weights, axis=2)
    update = jnp.einsum(
        "hqk,khd->qhd", weights.astype(jnp.bfloat16), values, preferred_element_type=jnp.float32
    )
    accum = accum * jnp.transpose(factor)[:, :, None] + update
    return (newest, total, accum)


def score_grads(
    head_queries, head_grads, log_total, delta, query_blocks, key_rows, key_blocks, scale
):
    width = key_rows.shape[1] // 2
    rows = key_rows.shape[0]
    query_rows = head_queries.shape[0]
    keys = split_heads(key_rows[:, :width])
    values = split_heads(key_rows[:, width:])
    scores = (
        jnp.einsum("qhd,khd->hqk", head_queries, keys, preferred_element_type=jnp.float32) * scale
    )
    allowed = key_blocks[None, None, :] <= query_blocks[None, :, None]
    probs = jnp.where(
        allowed, jnp.exp(jnp.where(allowed, scores, MASKED) - log_total[:, :, None]), 0.0
    )
    grad_values = jnp.einsum(
        "hqk,qhd->khd", probs.astype(jnp.bfloat16), head_grads, preferred_element_type=jnp.float32
    )
    grad_probs = jnp.einsum("qhd,khd->hqk", head_grads, values, preferred_element_type=jnp.float32)
    grad_scores = (probs * (grad_probs - delta[:, :, None])).astype(jnp.bfloat16)
    grad_queries = (
        jnp.einsum("hqk,khd->qhd", grad_scores, keys, preferred_element_type=jnp.float32) * scale
    )
    grad_keys = (
        jnp.einsum("hqk,qhd->khd", grad_scores, head_queries, preferred_element_type=jnp.float32)
        * scale
    )
    joined = jnp.concatenate(
        [grad_keys.reshape(rows, width), grad_values.reshape(rows, width)], axis=1
    )
    return (grad_queries.reshape(query_rows, width), joined)


def guarded(head_queries, head_grads, log_total, delta, query_blocks, key_rows, key_blocks, scale):
    live = jnp.min(key_blocks) <= jnp.max(query_blocks)
    rows, columns = key_rows.shape

    def run(unused):
        return score_grads(
            head_queries, head_grads, log_total, delta, query_blocks, key_rows, key_blocks, scale
        )

    def skip(unused):
        return (
            jnp.zeros((head_queries.shape[0], columns // 2), jnp.float32),
            jnp.zeros((rows, columns), jnp.float32),
        )

    return lax.cond(live, run, skip, 0)


def body(tokens_in, block_ids, w_query, w_key, w_value, w_out, w_up, w_down, norm_gain, cotangent):
    scale = 1.0 / math.sqrt(HD)
    stride = tokens_in.shape[1]
    width = tokens_in.shape[2]
    cycle_size = lax.axis_size("ctx")
    place = lax.axis_index("ctx")
    shards = (w_query, w_key, w_value, w_out, w_up, w_down, norm_gain)
    gathered = (
        lax.all_gather(w_query, ("fsdp", "ctx"), axis=0, tiled=True),
        lax.all_gather(w_key, ("fsdp", "ctx"), axis=0, tiled=True),
        lax.all_gather(w_value, ("fsdp", "ctx"), axis=0, tiled=True),
        lax.all_gather(w_out, ("fsdp", "ctx"), axis=0, tiled=True),
        lax.all_gather(w_up, ("fsdp", "ctx"), axis=0, tiled=True),
        lax.all_gather(w_down, ("fsdp", "ctx"), axis=0, tiled=True),
        lax.all_gather(norm_gain, ("fsdp", "ctx"), axis=1, tiled=True),
    )
    full_query, full_key, full_value, full_out, full_up, full_down, full_gain = gathered
    gains = full_gain.astype(jnp.float32)
    sequence_blocks = lax.all_gather(block_ids, "ctx", axis=1, tiled=True)[0]
    own_blocks = block_ids[0]
    top_block = jnp.max(own_blocks)
    tokens = tokens_in[0].astype(jnp.float32)
    normed = layer_norm(tokens, gains[0]).astype(jnp.bfloat16)
    queries = project(normed, full_query).astype(jnp.bfloat16)
    key_value = jnp.concatenate(
        [project(normed, full_key), project(normed, full_value)], axis=1
    ).astype(jnp.bfloat16)
    head_queries = split_heads(queries)
    start_state = (
        jnp.full((HEADS, stride), MASKED, jnp.float32),
        jnp.zeros((HEADS, stride), jnp.float32),
        jnp.zeros((stride, HEADS, HD), jnp.float32),
    )
    piece = lax.all_gather(key_value, "ctx", axis=0, tiled=True)
    rows = piece.shape[0]
    size = math.gcd(rows, stride)

    def visit(index, state):
        key_rows = lax.dynamic_slice_in_dim(piece, index * size, size, 0)
        key_blocks = lax.dynamic_slice_in_dim(sequence_blocks, index * size, size, 0)
        return lax.cond(
            jnp.min(key_blocks) <= top_block,
            lambda inner: attend(inner, head_queries, own_blocks, key_rows, key_blocks, scale),
            lambda inner: inner,
            state,
        )

    best, total, accum = lax.fori_loop(0, rows // size, visit, start_state)
    mixed = accum / jnp.transpose(total)[:, :, None]
    log_total = best + jnp.log(total)
    mixed_low = mixed.reshape(stride, width).astype(jnp.bfloat16)
    branch = project(mixed_low, full_out)
    hidden = tokens + layer_norm(branch, gains[1])
    inner = layer_norm(hidden, gains[2]).astype(jnp.bfloat16)
    lifted = project(inner, full_up)
    active = gelu_exact(lifted).astype(jnp.bfloat16)
    lowered = project(active, full_down)
    layer_out = (hidden + layer_norm(lowered, gains[3])).astype(jnp.bfloat16)[None]
    regathered = (
        lax.all_gather(shards[0], ("fsdp", "ctx"), axis=0, tiled=True),
        lax.all_gather(shards[1], ("fsdp", "ctx"), axis=0, tiled=True),
        lax.all_gather(shards[2], ("fsdp", "ctx"), axis=0, tiled=True),
        lax.all_gather(shards[3], ("fsdp", "ctx"), axis=0, tiled=True),
        lax.all_gather(shards[4], ("fsdp", "ctx"), axis=0, tiled=True),
        lax.all_gather(shards[5], ("fsdp", "ctx"), axis=0, tiled=True),
        lax.all_gather(shards[6], ("fsdp", "ctx"), axis=1, tiled=True),
    )
    back_query, back_key, back_value, back_out, back_up, back_down, back_gain = regathered
    back_gains = back_gain.astype(jnp.float32)
    upstream = cotangent[0].astype(jnp.float32)
    unused_four, pull_four = jax.vjp(layer_norm, lowered, back_gains[3])
    grad_lowered, gain_four = pull_four(upstream)
    grad_lowered = grad_lowered.astype(jnp.bfloat16)
    grad_down = outer_sum(active, grad_lowered)
    grad_active = back_project(grad_lowered, back_down)
    unused_gelu, pull_gelu = jax.vjp(gelu_exact, lifted)
    grad_lifted = pull_gelu(grad_active)[0].astype(jnp.bfloat16)
    grad_up = outer_sum(inner, grad_lifted)
    grad_inner = back_project(grad_lifted, back_up)
    unused_three, pull_three = jax.vjp(layer_norm, hidden, back_gains[2])
    grad_hidden_branch, gain_three = pull_three(grad_inner)
    grad_hidden = upstream + grad_hidden_branch
    unused_two, pull_two = jax.vjp(layer_norm, branch, back_gains[1])
    grad_branch, gain_two = pull_two(grad_hidden)
    grad_branch = grad_branch.astype(jnp.bfloat16)
    grad_out = outer_sum(mixed_low, grad_branch)
    grad_mixed = back_project(grad_branch, back_out).astype(jnp.bfloat16)
    head_grads = split_heads(grad_mixed)
    delta = jnp.transpose(jnp.sum(head_grads.astype(jnp.float32) * mixed, axis=2))
    query_grad, kv_grad = guarded(
        head_queries, head_grads, log_total, delta, own_blocks, key_value, own_blocks, scale
    )

    def pass_grads(values):
        return from_behind(values.astype(jnp.bfloat16), "ctx", 1).astype(values.dtype)

    def cycle_keys(step, state):
        travel, kv_accum, query_accum = state
        travel = from_behind(travel, "ctx", 1)
        kv_accum = pass_grads(kv_accum)
        source = (place - step) % cycle_size
        key_blocks = lax.dynamic_slice_in_dim(sequence_blocks, source * stride, stride, 0)
        part_query, part_kv = guarded(
            head_queries, head_grads, log_total, delta, own_blocks, travel, key_blocks, scale
        )
        return (travel, kv_accum + part_kv, query_accum + part_query)

    unused_travel, kv_accum, query_grad = lax.fori_loop(
        1, cycle_size, cycle_keys, (key_value, kv_grad, query_grad)
    )
    kv_grad = pass_grads(kv_accum)
    query_low = query_grad.astype(jnp.bfloat16)
    kv_low = kv_grad.astype(jnp.bfloat16)
    key_low = kv_low[:, :width]
    value_low = kv_low[:, width:]
    grad_query = outer_sum(normed, query_low)
    grad_key = outer_sum(normed, key_low)
    grad_value = outer_sum(normed, value_low)
    grad_normed = (
        back_project(query_low, back_query)
        + back_project(key_low, back_key)
        + back_project(value_low, back_value)
    )
    unused_one, pull_one = jax.vjp(layer_norm, tokens, back_gains[0])
    grad_norm_in, gain_one = pull_one(grad_normed)
    grad_tokens = (grad_hidden + grad_norm_in).astype(jnp.bfloat16)[None]
    gain_grads = jnp.stack([gain_one, gain_two, gain_three, gain_four])
    summed = (
        lax.psum_scatter(grad_query, ("fsdp", "ctx"), scatter_dimension=0, tiled=True),
        lax.psum_scatter(grad_key, ("fsdp", "ctx"), scatter_dimension=0, tiled=True),
        lax.psum_scatter(grad_value, ("fsdp", "ctx"), scatter_dimension=0, tiled=True),
        lax.psum_scatter(grad_out, ("fsdp", "ctx"), scatter_dimension=0, tiled=True),
        lax.psum_scatter(grad_up, ("fsdp", "ctx"), scatter_dimension=0, tiled=True),
        lax.psum_scatter(grad_down, ("fsdp", "ctx"), scatter_dimension=0, tiled=True),
        lax.psum_scatter(gain_grads, ("fsdp", "ctx"), scatter_dimension=1, tiled=True),
    )
    return (
        layer_out,
        grad_tokens,
        summed[0],
        summed[1],
        summed[2],
        summed[3],
        summed[4],
        summed[5],
        summed[6],
    )


MESH = pl.DeviceIdType.MESH
SLAB = 32
LANES = 1024


def places():
    fsdp, ctx = lax.axis_index("fsdp"), lax.axis_index("ctx")
    return lax.div(fsdp, 2), lax.rem(fsdp, 2), lax.div(ctx, 2), lax.rem(ctx, 2)


def at_place(y, core, z, x):
    return (y * 2 + core, z * 2 + x)


def meet(devices):
    barrier = pltpu.get_barrier_semaphore()
    for device in devices:
        pl.semaphore_signal(barrier, inc=1, device_id=device, device_id_type=MESH)
    pl.semaphore_wait(barrier, len(devices))


def sum_kernel(views, lines, *refs):
    grads, gain_ref = refs[:lines], refs[lines]
    out_ref, gain_out, own, zero, first_x, first_y, second, third = refs[lines + 1 : lines + 9]
    g_own, g_zero, g_first, g_second, g_third, load, send, arrive = refs[lines + 9 :]
    y, core, z, x = places()
    partner = at_place(y, 1 - core, z, x)
    beside = at_place(y, core, z, 1 - x)
    across = at_place(1 - y, core, z, x)
    rank = [lax.rem(z + d, 4) for d in (1, 2, 3)]
    others = [at_place(y, core, r, x) for r in rank]
    meet([partner, beside, across] + others)
    count = len(views) + 1
    last = len(views)

    def pick(k, side):
        if k == last:
            return gain_ref.at[:, side]
        ref, part = views[k]
        return grads[ref].at[(slice(None), side, slice(None), slice(None)) + part]

    def remote(src, dst, k, phase, device):
        return pltpu.make_async_remote_copy(
            src_ref=src,
            dst_ref=dst,
            send_sem=send.at[k, phase],
            recv_sem=arrive.at[k, phase],
            device_id=device,
            device_id_type=MESH,
        )

    def add(total, landed, pairs, rows):
        def one(i, unused):
            into, out_of = pairs(i)
            total[into] = total[into] + landed[out_of]
            return unused

        lax.fori_loop(0, rows, one, 0)

    def steps(k):
        if k == last:
            return g_own, g_zero, g_first, g_second, g_third
        return own.at[k], zero.at[k], (first_y if k % 2 else first_x).at[k // 2], second.at[k], third.at[k]

    def phase_zero(k):
        return remote(pick(k, 1 - core), steps(k)[1], k, 0, partner)

    def loading(k):
        return pltpu.make_async_copy(pick(k, core), steps(k)[0], load.at[k])

    def phase_one(k):
        total = steps(k)[0]
        if k % 2:
            return remote(total.at[1 - y], steps(k)[2], k, 1, across)
        return remote(total.at[:, :, 1 - x], steps(k)[2], k, 1, beside)

    def phase_two(k):
        total = steps(k)[0]
        if k % 2:
            return remote(total.at[y, :, 1 - x], steps(k)[3], k, 2, beside)
        return remote(total.at[1 - y, :, x], steps(k)[3], k, 2, across)

    def phase_three(k):
        total = steps(k)[0]
        return [
            remote(total.at[y, r, x], steps(k)[4].at[2 - d], k, 3 + d, others[d])
            for d, r in enumerate(rank)
        ]

    def after_zero(k):
        loading(k).wait()
        phase_zero(k).wait()
        total, landed = steps(k)[:2]
        split = lambda i: (lax.div(i, 8), lax.rem(lax.div(i, 2), 4), lax.rem(i, 2))
        add(total, landed, lambda i: (split(i), split(i)), 16)
        phase_one(k).start()

    def after_one(k):
        phase_one(k).wait()
        total, landed = steps(k)[0], steps(k)[2]
        if k % 2:
            add(total, landed, lambda i: ((y, lax.div(i, 2), lax.rem(i, 2)), (lax.div(i, 2), lax.rem(i, 2))), 8)
        else:
            add(total, landed, lambda i: ((lax.div(i, 4), lax.rem(i, 4), x), (lax.div(i, 4), lax.rem(i, 4))), 8)
        phase_two(k).start()

    def after_two(k):
        phase_two(k).wait()
        total, landed = steps(k)[0], steps(k)[3]
        add(total, landed, lambda i: ((y, i, x), (i,)), 4)
        for copy in phase_three(k):
            copy.start()

    def after_three(k):
        for copy in phase_three(k):
            copy.wait()
        total, landed = steps(k)[0], steps(k)[4]
        value = total[y, z, x].astype(jnp.float32)
        for d in range(3):
            value = value + landed[d].astype(jnp.float32)
        if k == last:
            gain_out[...] = value
        else:
            out_ref[k] = value

    for k in range(count):
        loading(k).start()
        phase_zero(k).start()
    for step in range(count + 3):
        for lag, run in enumerate((after_zero, after_one, after_two, after_three)):
            if 0 <= step - lag < count:
                run(step - lag)


def sum_over_devices(grads, gain, collective_id):
    shaped, views = [], []
    for ref, grad in enumerate(grads):
        rows, columns = grad.shape
        if columns == LANES:
            parts = rows // (32 * SLAB)
            shaped.append(grad.reshape(2, 2, 4, 2, parts, SLAB, LANES))
            views += [(ref, (part,)) for part in range(parts)]
        else:
            parts = columns // LANES
            shaped.append(grad.reshape(2, 2, 4, 2, SLAB, columns))
            views += [(ref, (slice(None), pl.ds(part * LANES, LANES))) for part in range(parts)]
    count = len(views)
    low = jnp.bfloat16
    slab = (SLAB, LANES)
    any_spec = pl.BlockSpec(memory_space=pl.ANY)
    out, gain_out = pl.pallas_call(
        functools.partial(sum_kernel, views, len(grads)),
        out_shape=(
            jax.ShapeDtypeStruct((count,) + slab, jnp.float32),
            jax.ShapeDtypeStruct((8, 128), jnp.float32),
        ),
        in_specs=[any_spec] * (len(grads) + 1),
        out_specs=(pl.BlockSpec(memory_space=pltpu.VMEM), pl.BlockSpec(memory_space=pltpu.VMEM)),
        scratch_shapes=[
            pltpu.VMEM((count, 2, 4, 2) + slab, low),
            pltpu.VMEM((count, 2, 4, 2) + slab, low),
            pltpu.VMEM(((count + 1) // 2, 2, 4) + slab, low),
            pltpu.VMEM(((count + 1) // 2, 4, 2) + slab, low),
            pltpu.VMEM((count, 4) + slab, low),
            pltpu.VMEM((count, 3) + slab, low),
            pltpu.VMEM((2, 4, 2, 8, 128), jnp.float32),
            pltpu.VMEM((2, 4, 2, 8, 128), jnp.float32),
            pltpu.VMEM(((4, 2) if count % 2 else (2, 4)) + (8, 128), jnp.float32),
            pltpu.VMEM((4, 8, 128), jnp.float32),
            pltpu.VMEM((3, 8, 128), jnp.float32),
            pltpu.SemaphoreType.DMA((count + 1,)),
            pltpu.SemaphoreType.DMA((count + 1, 6)),
            pltpu.SemaphoreType.DMA((count + 1, 6)),
        ],
        compiler_params=pltpu.CompilerParams(
            collective_id=collective_id, has_side_effects=True, vmem_limit_bytes=60 * 2**20
        ),
        name="sum_over_devices",
    )(*shaped, gain)
    return out, gain_out


TILE = 256


def nt(left, right):
    return lax.dot_general(
        left, right, (((1,), (1,)), ((), ())), preferred_element_type=jnp.float32
    )


def nn(left, right):
    return lax.dot_general(
        left, right, (((1,), (0,)), ((), ())), preferred_element_type=jnp.float32
    )


def tn(left, right):
    return lax.dot_general(
        left, right, (((0,), (0,)), ((), ())), preferred_element_type=jnp.float32
    )


def both_heads(rows):
    lane = lax.broadcasted_iota(jnp.int32, rows.shape, 1)
    zero = jnp.zeros_like(rows)
    return jnp.concatenate(
        [jnp.where(lane < HD, rows, zero), jnp.where(lane < HD, zero, rows)], axis=0
    )


def own_lanes(pair):
    half = pair.shape[0] // 2
    lane = lax.broadcasted_iota(jnp.int32, (half, pair.shape[1]), 1)
    return jnp.where(lane < HD, pair[:half], pair[half:])


def attend_kernel(query_ref, key_ref, value_ref, row_ref, col_ref, mixed_ref, log_ref, score_ref):
    tile = pl.program_id(0)
    tiles = pl.num_programs(0)
    wide = 2 * HD
    scaled = both_heads((query_ref[...].astype(jnp.float32) * HD**-0.5).astype(jnp.bfloat16))
    own = row_ref[...]
    own = jnp.concatenate([own, own], axis=0)

    def score(index, best, masked):
        at = pl.multiple_of(index * TILE, TILE)
        part = nt(scaled, key_ref[pl.ds(at, TILE), :])
        if masked:
            part = jnp.where(col_ref[:, pl.ds(at, TILE)] <= own, part, MASKED)
        score_ref[:, pl.ds(at, TILE)] = part
        for lane in range(0, TILE, wide):
            best = jnp.maximum(best, part[:, lane : lane + wide])
        return best

    best = jnp.full((2 * TILE, wide), MASKED, jnp.float32)
    best = lax.fori_loop(0, tile, lambda i, b: score(i, b, False), best)
    stop = jnp.minimum(tile + 2, tiles)
    best = lax.fori_loop(tile, stop, lambda i, b: score(i, b, True), best)
    best = jnp.max(best, axis=1, keepdims=True)

    def weigh(index, carry):
        total, accum = carry
        at = pl.multiple_of(index * TILE, TILE)
        weights = jnp.exp(score_ref[:, pl.ds(at, TILE)] - best)
        for lane in range(0, TILE, wide):
            total = total + weights[:, lane : lane + wide]
        return (total, accum + nn(weights.astype(jnp.bfloat16), value_ref[pl.ds(at, TILE), :]))

    zero = jnp.zeros((2 * TILE, wide), jnp.float32)
    total, accum = lax.fori_loop(0, stop, weigh, (zero, zero))
    total = jnp.sum(total, axis=1, keepdims=True)
    mixed_ref[...] = own_lanes(accum / total)
    log_total = jnp.broadcast_to(best + jnp.log(total), (2 * TILE, wide))
    log_ref[0] = jnp.transpose(log_total)[:8]


def attention_forward(joined, blocks):
    rows = joined.shape[0]
    wide = 2 * HD
    tiles = rows // TILE
    return pl.pallas_call(
        attend_kernel,
        grid=(tiles,),
        out_shape=(
            jax.ShapeDtypeStruct((rows, wide), jnp.float32),
            jax.ShapeDtypeStruct((tiles, 8, 2 * TILE), jnp.float32),
        ),
        in_specs=[
            pl.BlockSpec((TILE, wide), lambda t: (t, 0)),
            pl.BlockSpec((rows, wide), lambda t: (0, 1)),
            pl.BlockSpec((rows, wide), lambda t: (0, 2)),
            pl.BlockSpec((TILE, 1), lambda t: (t, 0)),
            pl.BlockSpec((1, rows), lambda t: (0, 0)),
        ],
        out_specs=(
            pl.BlockSpec((TILE, wide), lambda t: (t, 0)),
            pl.BlockSpec((1, 8, 2 * TILE), lambda t: (t, 0, 0)),
        ),
        scratch_shapes=[pltpu.VMEM((2 * TILE, rows), jnp.float32)],
        name="attention_forward",
    )(joined, joined, joined, blocks.reshape(rows, 1), blocks.reshape(1, rows))


def grads_kernel(
    query_ref, key_ref, value_ref, grad_ref, mixed_ref, log_ref, row_ref, col_ref, out_ref, key_sum, value_sum
):
    tile = pl.program_id(0)
    tiles = pl.num_programs(0)
    wide = 2 * HD

    @pl.when(tile == 0)
    def _():
        key_sum[...] = jnp.zeros_like(key_sum)
        value_sum[...] = jnp.zeros_like(value_sum)

    scaled = both_heads((query_ref[...].astype(jnp.float32) * HD**-0.5).astype(jnp.bfloat16))
    grads = both_heads(grad_ref[...])
    products = grad_ref[...].astype(jnp.float32) * mixed_ref[...]
    products = jnp.transpose(products)
    delta = jnp.concatenate(
        [
            jnp.sum(products[:HD], axis=0, keepdims=True),
            jnp.sum(products[HD:], axis=0, keepdims=True),
        ],
        axis=1,
    )
    log_total = log_ref[0, :1]
    own = col_ref[...]
    own = jnp.concatenate([own, own], axis=1)

    def step(index, accum, masked):
        at = pl.multiple_of(index * TILE, TILE)
        here = pl.ds(at, TILE)
        keys = key_ref[here, :]
        scores = nt(keys, scaled)
        if masked:
            scores = jnp.where(row_ref[here, :] <= own, scores, MASKED)
        probs = jnp.exp(scores - log_total)
        value_sum[here, :] += nn(probs.astype(jnp.bfloat16), grads)
        grad_scores = (probs * (nt(value_ref[here, :], grads) - delta)).astype(jnp.bfloat16)
        key_sum[here, :] += nn(grad_scores, scaled)
        return accum + tn(grad_scores, keys)

    accum = jnp.zeros((2 * TILE, wide), jnp.float32)
    accum = lax.fori_loop(0, tile, lambda i, a: step(i, a, False), accum)
    stop = jnp.minimum(tile + 2, tiles)
    accum = lax.fori_loop(tile, stop, lambda i, a: step(i, a, True), accum)
    at = pl.multiple_of(tile * TILE, TILE)
    out_ref[pl.ds(at, TILE), :wide] = (own_lanes(accum) * HD**-0.5).astype(jnp.bfloat16)

    @pl.when(tile == tiles - 1)
    def _():
        out_ref[:, wide : 2 * wide] = key_sum[...].astype(jnp.bfloat16)
        out_ref[:, 2 * wide :] = value_sum[...].astype(jnp.bfloat16)


def attention_backward(joined, grad_mixed, mixed, log_total, blocks):
    rows = joined.shape[0]
    wide = 2 * HD
    tiles = rows // TILE
    return pl.pallas_call(
        grads_kernel,
        grid=(tiles,),
        out_shape=jax.ShapeDtypeStruct((rows, 3 * wide), jnp.bfloat16),
        in_specs=[
            pl.BlockSpec((TILE, wide), lambda t: (t, 0)),
            pl.BlockSpec((rows, wide), lambda t: (0, 1)),
            pl.BlockSpec((rows, wide), lambda t: (0, 2)),
            pl.BlockSpec((TILE, wide), lambda t: (t, 0)),
            pl.BlockSpec((TILE, wide), lambda t: (t, 0)),
            pl.BlockSpec((1, 8, 2 * TILE), lambda t: (t, 0, 0)),
            pl.BlockSpec((rows, 1), lambda t: (0, 0)),
            pl.BlockSpec((1, TILE), lambda t: (0, t)),
        ],
        out_specs=pl.BlockSpec((rows, 3 * wide), lambda t: (0, 0)),
        scratch_shapes=[
            pltpu.VMEM((rows, wide), jnp.float32),
            pltpu.VMEM((rows, wide), jnp.float32),
        ],
        name="attention_backward",
    )(
        joined,
        joined,
        joined,
        grad_mixed,
        mixed,
        log_total,
        blocks.reshape(rows, 1),
        blocks.reshape(1, rows),
    )


def to_heads(rows, groups, count):
    tokens = rows.shape[0]
    wide = rows.shape[1] // (groups * count)
    split = rows.reshape(tokens, count, groups, wide).transpose(2, 0, 1, 3)
    split = split.reshape(groups, tokens, count * wide)
    whole = lax.all_to_all(split, "ctx", 0, 0, tiled=True)
    return whole.reshape(groups * tokens, count * wide)


def to_tokens(rows, groups, count):
    tokens = rows.shape[0] // groups
    wide = rows.shape[1] // count
    split = lax.all_to_all(rows.reshape(groups, tokens, count * wide), "ctx", 0, 0, tiled=True)
    split = split.reshape(groups, tokens, count, wide).transpose(1, 2, 0, 3)
    return split.reshape(tokens, count * groups * wide)


def fast_body(
    tokens_in, block_ids, w_query, w_key, w_value, w_out, w_up, w_down, norm_gain, cotangent
):
    axes = ("fsdp", "ctx")
    width = tokens_in.shape[2]
    groups = lax.axis_size("ctx")
    full_gain = lax.all_gather(norm_gain, axes, axis=1, tiled=True)
    full_qkv = lax.all_gather(
        jnp.concatenate([w_query, w_key, w_value], axis=1), axes, axis=0, tiled=True
    )
    blocks = lax.all_gather(block_ids, "ctx", axis=1, tiled=True)[0]
    full_out = lax.all_gather(w_out, axes, axis=0, tiled=True)
    full_up = lax.all_gather(w_up, axes, axis=0, tiled=True)
    full_down = lax.all_gather(w_down, axes, axis=0, tiled=True)
    gains = full_gain.astype(jnp.float32)
    tokens = tokens_in[0].astype(jnp.float32)
    normed = layer_norm(tokens, gains[0]).astype(jnp.bfloat16)
    joined = to_heads(project(normed, full_qkv).astype(jnp.bfloat16), groups, 3)
    mixed, log_total = attention_forward(joined, blocks)
    mixed_low = to_tokens(mixed.astype(jnp.bfloat16), groups, 1)
    branch = project(mixed_low, full_out)
    hidden = tokens + layer_norm(branch, gains[1])
    inner = layer_norm(hidden, gains[2]).astype(jnp.bfloat16)
    lifted = project(inner, full_up)
    active = gelu_exact(lifted).astype(jnp.bfloat16)
    lowered = project(active, full_down)
    layer_out = (hidden + layer_norm(lowered, gains[3])).astype(jnp.bfloat16)[None]
    upstream = cotangent[0].astype(jnp.float32)
    unused_four, pull_four = jax.vjp(layer_norm, lowered, gains[3])
    grad_lowered, gain_four = pull_four(upstream)
    grad_lowered = grad_lowered.astype(jnp.bfloat16)
    grad_down = outer_sum(active, grad_lowered).astype(jnp.bfloat16)
    grad_active = back_project(grad_lowered, full_down)
    unused_gelu, pull_gelu = jax.vjp(gelu_exact, lifted)
    grad_lifted = pull_gelu(grad_active)[0].astype(jnp.bfloat16)
    grad_up = outer_sum(inner, grad_lifted).astype(jnp.bfloat16)
    grad_inner = back_project(grad_lifted, full_up)
    unused_three, pull_three = jax.vjp(layer_norm, hidden, gains[2])
    grad_hidden_branch, gain_three = pull_three(grad_inner)
    grad_hidden = upstream + grad_hidden_branch
    unused_two, pull_two = jax.vjp(layer_norm, branch, gains[1])
    grad_branch, gain_two = pull_two(grad_hidden)
    grad_branch = grad_branch.astype(jnp.bfloat16)
    grad_out = outer_sum(mixed_low, grad_branch).astype(jnp.bfloat16)
    grad_mixed = back_project(grad_branch, full_out).astype(jnp.bfloat16)
    grad_joined = attention_backward(
        joined, to_heads(grad_mixed, groups, 1), mixed, log_total, blocks
    )
    grad_qkv = to_tokens(grad_joined, groups, 3)
    grad_three = outer_sum(normed, grad_qkv).astype(jnp.bfloat16)
    grad_normed = back_project(grad_qkv, full_qkv)
    unused_one, pull_one = jax.vjp(layer_norm, tokens, gains[0])
    grad_norm_in, gain_one = pull_one(grad_normed)
    grad_tokens = (grad_hidden + grad_norm_in).astype(jnp.bfloat16)[None]
    gain_grads = jnp.stack([gain_one, gain_two, gain_three, gain_four])
    sums, gain_sum = sum_over_devices(
        [grad_three, grad_out, grad_up, grad_down], by_owner(gain_grads), 3
    )
    return (
        layer_out,
        grad_tokens,
        sums[0],
        sums[1],
        sums[2],
        sums[3],
        sums[4:8].transpose(1, 0, 2).reshape(w_up.shape),
        sums[8:].reshape(w_down.shape),
        gain_sum[0].reshape(norm_gain.shape),
    )


def by_owner(gain_grads):
    kinds, width = gain_grads.shape
    rows = gain_grads.reshape(kinds, 32, width // 32).transpose(1, 0, 2).reshape(32, 1, -1)
    return jnp.pad(rows, ((0, 0), (0, 7), (0, 0))).reshape(2, 2, 4, 2, 8, rows.shape[-1])


def pick(mesh):
    return fast_body if mesh.shape["ctx"] * 2 == HEADS else body


def solution(mesh):
    placed = (
        P("fsdp", "ctx", None),
        P("fsdp", "ctx"),
        P(("fsdp", "ctx"), None),
        P(("fsdp", "ctx"), None),
        P(("fsdp", "ctx"), None),
        P(("fsdp", "ctx"), None),
        P(("fsdp", "ctx"), None),
        P(("fsdp", "ctx"), None),
        P(None, ("fsdp", "ctx")),
        P("fsdp", "ctx", None),
    )
    return jax.shard_map(
        pick(mesh),
        mesh=mesh,
        in_specs=placed,
        out_specs=(
            P("fsdp", "ctx", None),
            P("fsdp", "ctx", None),
            P(("fsdp", "ctx"), None),
            P(("fsdp", "ctx"), None),
            P(("fsdp", "ctx"), None),
            P(("fsdp", "ctx"), None),
            P(("fsdp", "ctx"), None),
            P(("fsdp", "ctx"), None),
            P(None, ("fsdp", "ctx")),
        ),
        check_vma=False,
    )
```

```python
import functools
import math

import jax
import jax.numpy as jnp
from jax import lax
from jax.experimental import pallas as pl
from jax.experimental.pallas import tpu as pltpu
from jax.sharding import PartitionSpec as P

HEADS = 16
HD = 64


EPS = 1e-05
MASKED = -1e30


def from_behind(block, axis, distance):
    devices = range(lax.axis_size(axis))
    route = [((i - distance) % len(devices), i) for i in devices]
    return lax.ppermute(block, axis, route)


def layer_norm(values, gain):
    centre = values - jnp.mean(values, axis=-1, keepdims=True)
    spread = jnp.mean(centre * centre, axis=-1, keepdims=True)
    return centre * lax.rsqrt(spread + EPS) * gain


def gelu_exact(values):
    return jax.nn.gelu(values, approximate=False)


def project(left, right):
    return jnp.dot(left, right, preferred_element_type=jnp.float32)


def outer_sum(left, right):
    return lax.dot_general(
        left, right, (((0,), (0,)), ((), ())), preferred_element_type=jnp.float32
    )


def back_project(grad, weight):
    return lax.dot_general(
        grad, weight, (((1,), (1,)), ((), ())), preferred_element_type=jnp.float32
    )


def split_heads(values):
    return values.reshape(values.shape[0], HEADS, HD)


def attend(carry, head_queries, query_blocks, key_rows, key_blocks, scale):
    best, total, accum = carry
    width = key_rows.shape[1] // 2
    keys = split_heads(key_rows[:, :width])
    values = split_heads(key_rows[:, width:])
    scores = (
        jnp.einsum("qhd,khd->hqk", head_queries, keys, preferred_element_type=jnp.float32) * scale
    )
    allowed = key_blocks[None, None, :] <= query_blocks[None, :, None]
    scores = jnp.where(allowed, scores, MASKED)
    newest = jnp.maximum(best, jnp.max(scores, axis=2))
    weights = jnp.where(allowed, jnp.exp(scores - newest[:, :, None]), 0.0)
    factor = jnp.exp(best - newest)
    total = total * factor + jnp.sum(weights, axis=2)
    update = jnp.einsum(
        "hqk,khd->qhd", weights.astype(jnp.bfloat16), values, preferred_element_type=jnp.float32
    )
    accum = accum * jnp.transpose(factor)[:, :, None] + update
    return (newest, total, accum)


def score_grads(
    head_queries, head_grads, log_total, delta, query_blocks, key_rows, key_blocks, scale
):
    width = key_rows.shape[1] // 2
    rows = key_rows.shape[0]
    query_rows = head_queries.shape[0]
    keys = split_heads(key_rows[:, :width])
    values = split_heads(key_rows[:, width:])
    scores = (
        jnp.einsum("qhd,khd->hqk", head_queries, keys, preferred_element_type=jnp.float32) * scale
    )
    allowed = key_blocks[None, None, :] <= query_blocks[None, :, None]
    probs = jnp.where(
        allowed, jnp.exp(jnp.where(allowed, scores, MASKED) - log_total[:, :, None]), 0.0
    )
    grad_values = jnp.einsum(
        "hqk,qhd->khd", probs.astype(jnp.bfloat16), head_grads, preferred_element_type=jnp.float32
    )
    grad_probs = jnp.einsum("qhd,khd->hqk", head_grads, values, preferred_element_type=jnp.float32)
    grad_scores = (probs * (grad_probs - delta[:, :, None])).astype(jnp.bfloat16)
    grad_queries = (
        jnp.einsum("hqk,khd->qhd", grad_scores, keys, preferred_element_type=jnp.float32) * scale
    )
    grad_keys = (
        jnp.einsum("hqk,qhd->khd", grad_scores, head_queries, preferred_element_type=jnp.float32)
        * scale
    )
    joined = jnp.concatenate(
        [grad_keys.reshape(rows, width), grad_values.reshape(rows, width)], axis=1
    )
    return (grad_queries.reshape(query_rows, width), joined)


def guarded(head_queries, head_grads, log_total, delta, query_blocks, key_rows, key_blocks, scale):
    live = jnp.min(key_blocks) <= jnp.max(query_blocks)
    rows, columns = key_rows.shape

    def run(unused):
        return score_grads(
            head_queries, head_grads, log_total, delta, query_blocks, key_rows, key_blocks, scale
        )

    def skip(unused):
        return (
            jnp.zeros((head_queries.shape[0], columns // 2), jnp.float32),
            jnp.zeros((rows, columns), jnp.float32),
        )

    return lax.cond(live, run, skip, 0)


def body(tokens_in, block_ids, w_query, w_key, w_value, w_out, w_up, w_down, norm_gain, cotangent):
    scale = 1.0 / math.sqrt(HD)
    stride = tokens_in.shape[1]
    width = tokens_in.shape[2]
    cycle_size = lax.axis_size("ctx")
    place = lax.axis_index("ctx")
    shards = (w_query, w_key, w_value, w_out, w_up, w_down, norm_gain)
    gathered = (
        lax.all_gather(w_query, ("fsdp", "ctx"), axis=0, tiled=True),
        lax.all_gather(w_key, ("fsdp", "ctx"), axis=0, tiled=True),
        lax.all_gather(w_value, ("fsdp", "ctx"), axis=0, tiled=True),
        lax.all_gather(w_out, ("fsdp", "ctx"), axis=0, tiled=True),
        lax.all_gather(w_up, ("fsdp", "ctx"), axis=0, tiled=True),
        lax.all_gather(w_down, ("fsdp", "ctx"), axis=0, tiled=True),
        lax.all_gather(norm_gain, ("fsdp", "ctx"), axis=1, tiled=True),
    )
    full_query, full_key, full_value, full_out, full_up, full_down, full_gain = gathered
    gains = full_gain.astype(jnp.float32)
    sequence_blocks = lax.all_gather(block_ids, "ctx", axis=1, tiled=True)[0]
    own_blocks = block_ids[0]
    top_block = jnp.max(own_blocks)
    tokens = tokens_in[0].astype(jnp.float32)
    normed = layer_norm(tokens, gains[0]).astype(jnp.bfloat16)
    queries = project(normed, full_query).astype(jnp.bfloat16)
    key_value = jnp.concatenate(
        [project(normed, full_key), project(normed, full_value)], axis=1
    ).astype(jnp.bfloat16)
    head_queries = split_heads(queries)
    start_state = (
        jnp.full((HEADS, stride), MASKED, jnp.float32),
        jnp.zeros((HEADS, stride), jnp.float32),
        jnp.zeros((stride, HEADS, HD), jnp.float32),
    )
    piece = lax.all_gather(key_value, "ctx", axis=0, tiled=True)
    rows = piece.shape[0]
    size = math.gcd(rows, stride)

    def visit(index, state):
        key_rows = lax.dynamic_slice_in_dim(piece, index * size, size, 0)
        key_blocks = lax.dynamic_slice_in_dim(sequence_blocks, index * size, size, 0)
        return lax.cond(
            jnp.min(key_blocks) <= top_block,
            lambda inner: attend(inner, head_queries, own_blocks, key_rows, key_blocks, scale),
            lambda inner: inner,
            state,
        )

    best, total, accum = lax.fori_loop(0, rows // size, visit, start_state)
    mixed = accum / jnp.transpose(total)[:, :, None]
    log_total = best + jnp.log(total)
    mixed_low = mixed.reshape(stride, width).astype(jnp.bfloat16)
    branch = project(mixed_low, full_out)
    hidden = tokens + layer_norm(branch, gains[1])
    inner = layer_norm(hidden, gains[2]).astype(jnp.bfloat16)
    lifted = project(inner, full_up)
    active = gelu_exact(lifted).astype(jnp.bfloat16)
    lowered = project(active, full_down)
    layer_out = (hidden + layer_norm(lowered, gains[3])).astype(jnp.bfloat16)[None]
    regathered = (
        lax.all_gather(shards[0], ("fsdp", "ctx"), axis=0, tiled=True),
        lax.all_gather(shards[1], ("fsdp", "ctx"), axis=0, tiled=True),
        lax.all_gather(shards[2], ("fsdp", "ctx"), axis=0, tiled=True),
        lax.all_gather(shards[3], ("fsdp", "ctx"), axis=0, tiled=True),
        lax.all_gather(shards[4], ("fsdp", "ctx"), axis=0, tiled=True),
        lax.all_gather(shards[5], ("fsdp", "ctx"), axis=0, tiled=True),
        lax.all_gather(shards[6], ("fsdp", "ctx"), axis=1, tiled=True),
    )
    back_query, back_key, back_value, back_out, back_up, back_down, back_gain = regathered
    back_gains = back_gain.astype(jnp.float32)
    upstream = cotangent[0].astype(jnp.float32)
    unused_four, pull_four = jax.vjp(layer_norm, lowered, back_gains[3])
    grad_lowered, gain_four = pull_four(upstream)
    grad_lowered = grad_lowered.astype(jnp.bfloat16)
    grad_down = outer_sum(active, grad_lowered)
    grad_active = back_project(grad_lowered, back_down)
    unused_gelu, pull_gelu = jax.vjp(gelu_exact, lifted)
    grad_lifted = pull_gelu(grad_active)[0].astype(jnp.bfloat16)
    grad_up = outer_sum(inner, grad_lifted)
    grad_inner = back_project(grad_lifted, back_up)
    unused_three, pull_three = jax.vjp(layer_norm, hidden, back_gains[2])
    grad_hidden_branch, gain_three = pull_three(grad_inner)
    grad_hidden = upstream + grad_hidden_branch
    unused_two, pull_two = jax.vjp(layer_norm, branch, back_gains[1])
    grad_branch, gain_two = pull_two(grad_hidden)
    grad_branch = grad_branch.astype(jnp.bfloat16)
    grad_out = outer_sum(mixed_low, grad_branch)
    grad_mixed = back_project(grad_branch, back_out).astype(jnp.bfloat16)
    head_grads = split_heads(grad_mixed)
    delta = jnp.transpose(jnp.sum(head_grads.astype(jnp.float32) * mixed, axis=2))
    query_grad, kv_grad = guarded(
        head_queries, head_grads, log_total, delta, own_blocks, key_value, own_blocks, scale
    )

    def pass_grads(values):
        return from_behind(values.astype(jnp.bfloat16), "ctx", 1).astype(values.dtype)

    def cycle_keys(step, state):
        travel, kv_accum, query_accum = state
        travel = from_behind(travel, "ctx", 1)
        kv_accum = pass_grads(kv_accum)
        source = (place - step) % cycle_size
        key_blocks = lax.dynamic_slice_in_dim(sequence_blocks, source * stride, stride, 0)
        part_query, part_kv = guarded(
            head_queries, head_grads, log_total, delta, own_blocks, travel, key_blocks, scale
        )
        return (travel, kv_accum + part_kv, query_accum + part_query)

    unused_travel, kv_accum, query_grad = lax.fori_loop(
        1, cycle_size, cycle_keys, (key_value, kv_grad, query_grad)
    )
    kv_grad = pass_grads(kv_accum)
    query_low = query_grad.astype(jnp.bfloat16)
    kv_low = kv_grad.astype(jnp.bfloat16)
    key_low = kv_low[:, :width]
    value_low = kv_low[:, width:]
    grad_query = outer_sum(normed, query_low)
    grad_key = outer_sum(normed, key_low)
    grad_value = outer_sum(normed, value_low)
    grad_normed = (
        back_project(query_low, back_query)
        + back_project(key_low, back_key)
        + back_project(value_low, back_value)
    )
    unused_one, pull_one = jax.vjp(layer_norm, tokens, back_gains[0])
    grad_norm_in, gain_one = pull_one(grad_normed)
    grad_tokens = (grad_hidden + grad_norm_in).astype(jnp.bfloat16)[None]
    gain_grads = jnp.stack([gain_one, gain_two, gain_three, gain_four])
    summed = (
        lax.psum_scatter(grad_query, ("fsdp", "ctx"), scatter_dimension=0, tiled=True),
        lax.psum_scatter(grad_key, ("fsdp", "ctx"), scatter_dimension=0, tiled=True),
        lax.psum_scatter(grad_value, ("fsdp", "ctx"), scatter_dimension=0, tiled=True),
        lax.psum_scatter(grad_out, ("fsdp", "ctx"), scatter_dimension=0, tiled=True),
        lax.psum_scatter(grad_up, ("fsdp", "ctx"), scatter_dimension=0, tiled=True),
        lax.psum_scatter(grad_down, ("fsdp", "ctx"), scatter_dimension=0, tiled=True),
        lax.psum_scatter(gain_grads, ("fsdp", "ctx"), scatter_dimension=1, tiled=True),
    )
    return (
        layer_out,
        grad_tokens,
        summed[0],
        summed[1],
        summed[2],
        summed[3],
        summed[4],
        summed[5],
        summed[6],
    )


MESH = pl.DeviceIdType.MESH
SLAB = 32
LANES = 1024


def places():
    fsdp, ctx = lax.axis_index("fsdp"), lax.axis_index("ctx")
    return lax.div(fsdp, 2), lax.rem(fsdp, 2), lax.div(ctx, 2), lax.rem(ctx, 2)


def at_place(y, core, z, x):
    return (y * 2 + core, z * 2 + x)


def meet(devices):
    barrier = pltpu.get_barrier_semaphore()
    for device in devices:
        pl.semaphore_signal(barrier, inc=1, device_id=device, device_id_type=MESH)
    pl.semaphore_wait(barrier, len(devices))


def sum_kernel(views, lines, *refs):
    grads, gain_ref = refs[:lines], refs[lines]
    out_ref, gain_out, own, zero, first_x, first_y, second, third = refs[lines + 1 : lines + 9]
    g_own, g_zero, g_first, g_second, g_third, load, send, arrive = refs[lines + 9 :]
    y, core, z, x = places()
    partner = at_place(y, 1 - core, z, x)
    beside = at_place(y, core, z, 1 - x)
    across = at_place(1 - y, core, z, x)
    rank = [lax.rem(z + d, 4) for d in (1, 2, 3)]
    others = [at_place(y, core, r, x) for r in rank]
    meet([partner, beside, across] + others)
    count = len(views) + 1
    last = len(views)

    def pick(k, side):
        if k == last:
            return gain_ref.at[:, side]
        ref, part = views[k]
        return grads[ref].at[(slice(None), side, slice(None), slice(None)) + part]

    def remote(src, dst, k, phase, device):
        return pltpu.make_async_remote_copy(
            src_ref=src,
            dst_ref=dst,
            send_sem=send.at[k, phase],
            recv_sem=arrive.at[k, phase],
            device_id=device,
            device_id_type=MESH,
        )

    def add(total, landed, pairs, rows):
        def one(i, unused):
            into, out_of = pairs(i)
            total[into] = total[into] + landed[out_of]
            return unused

        lax.fori_loop(0, rows, one, 0)

    def steps(k):
        if k == last:
            return g_own, g_zero, g_first, g_second, g_third
        return own.at[k], zero.at[k], (first_y if k % 2 else first_x).at[k // 2], second.at[k], third.at[k]

    def phase_zero(k):
        return remote(pick(k, 1 - core), steps(k)[1], k, 0, partner)

    def loading(k):
        return pltpu.make_async_copy(pick(k, core), steps(k)[0], load.at[k])

    def phase_one(k):
        total = steps(k)[0]
        if k % 2:
            return remote(total.at[1 - y], steps(k)[2], k, 1, across)
        return remote(total.at[:, :, 1 - x], steps(k)[2], k, 1, beside)

    def phase_two(k):
        total = steps(k)[0]
        if k % 2:
            return remote(total.at[y, :, 1 - x], steps(k)[3], k, 2, beside)
        return remote(total.at[1 - y, :, x], steps(k)[3], k, 2, across)

    def phase_three(k):
        total = steps(k)[0]
        return [
            remote(total.at[y, r, x], steps(k)[4].at[2 - d], k, 3 + d, others[d])
            for d, r in enumerate(rank)
        ]

    def after_zero(k):
        loading(k).wait()
        phase_zero(k).wait()
        total, landed = steps(k)[:2]
        split = lambda i: (lax.div(i, 8), lax.rem(lax.div(i, 2), 4), lax.rem(i, 2))
        add(total, landed, lambda i: (split(i), split(i)), 16)
        phase_one(k).start()

    def after_one(k):
        phase_one(k).wait()
        total, landed = steps(k)[0], steps(k)[2]
        if k % 2:
            add(total, landed, lambda i: ((y, lax.div(i, 2), lax.rem(i, 2)), (lax.div(i, 2), lax.rem(i, 2))), 8)
        else:
            add(total, landed, lambda i: ((lax.div(i, 4), lax.rem(i, 4), x), (lax.div(i, 4), lax.rem(i, 4))), 8)
        phase_two(k).start()

    def after_two(k):
        phase_two(k).wait()
        total, landed = steps(k)[0], steps(k)[3]
        add(total, landed, lambda i: ((y, i, x), (i,)), 4)
        for copy in phase_three(k):
            copy.start()

    def after_three(k):
        for copy in phase_three(k):
            copy.wait()
        total, landed = steps(k)[0], steps(k)[4]
        value = total[y, z, x].astype(jnp.float32)
        for d in range(3):
            value = value + landed[d].astype(jnp.float32)
        if k == last:
            gain_out[...] = value
        else:
            out_ref[k] = value

    for k in range(count):
        loading(k).start()
        phase_zero(k).start()
    for step in range(count + 3):
        for lag, run in enumerate((after_zero, after_one, after_two, after_three)):
            if 0 <= step - lag < count:
                run(step - lag)


def sum_over_devices(grads, gain, collective_id):
    shaped, views = [], []
    for ref, grad in enumerate(grads):
        rows, columns = grad.shape
        if columns == LANES:
            parts = rows // (32 * SLAB)
            shaped.append(grad.reshape(2, 2, 4, 2, parts, SLAB, LANES))
            views += [(ref, (part,)) for part in range(parts)]
        else:
            parts = columns // LANES
            shaped.append(grad.reshape(2, 2, 4, 2, SLAB, columns))
            views += [(ref, (slice(None), pl.ds(part * LANES, LANES))) for part in range(parts)]
    count = len(views)
    low = jnp.bfloat16
    slab = (SLAB, LANES)
    any_spec = pl.BlockSpec(memory_space=pl.ANY)
    out, gain_out = pl.pallas_call(
        functools.partial(sum_kernel, views, len(grads)),
        out_shape=(
            jax.ShapeDtypeStruct((count,) + slab, jnp.float32),
            jax.ShapeDtypeStruct((8, 128), jnp.float32),
        ),
        in_specs=[any_spec] * (len(grads) + 1),
        out_specs=(pl.BlockSpec(memory_space=pltpu.VMEM), pl.BlockSpec(memory_space=pltpu.VMEM)),
        scratch_shapes=[
            pltpu.VMEM((count, 2, 4, 2) + slab, low),
            pltpu.VMEM((count, 2, 4, 2) + slab, low),
            pltpu.VMEM(((count + 1) // 2, 2, 4) + slab, low),
            pltpu.VMEM(((count + 1) // 2, 4, 2) + slab, low),
            pltpu.VMEM((count, 4) + slab, low),
            pltpu.VMEM((count, 3) + slab, low),
            pltpu.VMEM((2, 4, 2, 8, 128), jnp.float32),
            pltpu.VMEM((2, 4, 2, 8, 128), jnp.float32),
            pltpu.VMEM(((4, 2) if count % 2 else (2, 4)) + (8, 128), jnp.float32),
            pltpu.VMEM((4, 8, 128), jnp.float32),
            pltpu.VMEM((3, 8, 128), jnp.float32),
            pltpu.SemaphoreType.DMA((count + 1,)),
            pltpu.SemaphoreType.DMA((count + 1, 6)),
            pltpu.SemaphoreType.DMA((count + 1, 6)),
        ],
        compiler_params=pltpu.CompilerParams(
            collective_id=collective_id, has_side_effects=True, vmem_limit_bytes=60 * 2**20
        ),
        name="sum_over_devices",
    )(*shaped, gain)
    return out, gain_out


def gather_schedule(chunks, send, arrive, keep):
    y, core, z, x = places()
    partner = at_place(y, 1 - core, z, x)
    beside = at_place(y, core, z, 1 - x)
    across = at_place(1 - y, core, z, x)
    rank = [lax.rem(z + d, 4) for d in (1, 2, 3)]
    others = [at_place(y, core, r, x) for r in rank]
    count = len(chunks)
    every = slice(None)

    def remote(src, dst, k, phase, device):
        return pltpu.make_async_remote_copy(
            src_ref=src,
            dst_ref=dst,
            send_sem=send.at[k, phase],
            recv_sem=arrive.at[k, phase],
            device_id=device,
            device_id_type=MESH,
        )

    def keeping(k):
        own, whole = chunks[k]
        return pltpu.make_async_copy(own, whole(y, core, z, x), keep.at[k])

    def along_z(k):
        own, whole = chunks[k]
        return [remote(own, whole(y, core, z, x), k, 3 + d, others[d]) for d in range(3)]

    def hop(k, phase):
        whole = chunks[k][1]
        if phase == 0:
            part, device = whole(y, core, every, x), (across if k % 2 else beside)
        elif k % 2:
            part, device = whole(every, core, every, x), beside
        else:
            part, device = whole(y, core, every, every), across
        return remote(part, part, k, phase, device)

    def over(k):
        part = chunks[k][1](every, core, every, every)
        return remote(part, part, k, 2, partner)

    def begin():
        for k in range(count):
            keeping(k).start()
            for copy in along_z(k):
                copy.start()

    def after_z(k):
        keeping(k).wait()
        for copy in along_z(k):
            copy.wait()
        hop(k, 0).start()

    def after_first(k):
        hop(k, 0).wait()
        hop(k, 1).start()

    def after_second(k):
        hop(k, 1).wait()
        over(k).start()

    def after_over(k):
        over(k).wait()

    steps = [begin]
    for step in range(count + 3):
        for lag, run in enumerate((after_z, after_first, after_second, after_over)):
            if 0 <= step - lag < count:
                steps.append(functools.partial(run, step - lag))
    return steps


def weight_chunks(shards, wholes):
    chunks = []
    for own, whole in zip(shards, wholes):
        columns = own.shape[1]
        if len(whole.shape) == 7:
            for part in range(whole.shape[4]):
                chunks.append(
                    (own.at[pl.ds(part * SLAB, SLAB)], lambda *p, w=whole, n=part: w.at[p + (n,)])
                )
        elif columns > LANES:
            for part in range(columns // LANES):
                at = pl.ds(part * LANES, LANES)
                chunks.append(
                    (own.at[:, at], lambda *p, w=whole, n=at: w.at[p + (slice(None), n)])
                )
        else:
            chunks.append((own, lambda *p, w=whole: w.at[p]))
    return chunks


def whole_shape(shard):
    rows, columns = shard.shape
    if rows > SLAB and columns == LANES:
        return jax.ShapeDtypeStruct((2, 2, 4, 2, rows // SLAB, SLAB, columns), shard.dtype)
    return jax.ShapeDtypeStruct((2, 2, 4, 2, rows, columns), shard.dtype)


def gather_kernel(count, *refs):
    shards, wholes = refs[:count], refs[count : 2 * count]
    send, arrive, keep = refs[2 * count :]
    y, core, z, x = places()
    meet(
        [at_place(y, 1 - core, z, x), at_place(y, core, z, 1 - x), at_place(1 - y, core, z, x)]
        + [at_place(y, core, lax.rem(z + d, 4), x) for d in (1, 2, 3)]
    )
    for step in gather_schedule(weight_chunks(shards, wholes), send, arrive, keep):
        step()


def gather_over_devices(shards, collective_id):
    shapes = [whole_shape(shard) for shard in shards]
    count = sum(max(1, shard.size // (SLAB * LANES)) for shard in shards)
    any_spec = pl.BlockSpec(memory_space=pl.ANY)
    wholes = pl.pallas_call(
        functools.partial(gather_kernel, len(shards)),
        out_shape=shapes,
        in_specs=[pl.BlockSpec(memory_space=pltpu.VMEM)] * len(shards),
        out_specs=[any_spec] * len(shards),
        scratch_shapes=[
            pltpu.SemaphoreType.DMA((count, 6)),
            pltpu.SemaphoreType.DMA((count, 6)),
            pltpu.SemaphoreType.DMA((count,)),
        ],
        compiler_params=pltpu.CompilerParams(
            collective_id=collective_id, has_side_effects=True, vmem_limit_bytes=60 * 2**20
        ),
        name="gather_over_devices",
    )(*shards)
    return [whole.reshape(-1, whole.shape[-1]) for whole in wholes]


def same_column(offset):
    return lax.rem(lax.axis_index("ctx") + offset, lax.axis_size("ctx"))


def greet(devices):
    meet(devices + [(lax.axis_index("fsdp"), same_column(o)) for o in range(1, 8)])


def to_column(src, dst, send, arrive, place):
    return pltpu.make_async_remote_copy(
        src_ref=src,
        dst_ref=dst,
        send_sem=send,
        recv_sem=arrive,
        device_id=(lax.axis_index("fsdp"), place),
        device_id_type=MESH,
    )


def rows_of(index):
    return pl.ds(pl.multiple_of(index * TILE, TILE), TILE)


def lanes_of(index, start=0):
    return pl.ds(pl.multiple_of(start + index * 2 * HD, 2 * HD), 2 * HD)


def spread_steps(steps, tiles, first, per_tile):
    before, rest = steps[:first], steps[first:]
    beside = [rest[t * per_tile : (t + 1) * per_tile] for t in range(tiles)]
    return before, beside, rest[tiles * per_tile :]


def forward_kernel(count, *refs):
    joined_in, row_ref, col_ref = refs[:3]
    shards, refs = refs[3 : 3 + count], refs[3 + count :]
    joined, mixed_ref, log_ref, mixed_in = refs[:4]
    wholes, refs = refs[4 : 4 + count], refs[4 + count :]
    score_ref, low_ref, q_send, q_arrive, m_send, m_arrive, send, arrive, keep = refs
    y, core, z, x = places()
    me = lax.axis_index("ctx")
    tiles = 8
    wide = 2 * HD
    width = HEADS * HD
    greet([at_place(y, 1 - core, z, x), at_place(1 - y, core, z, x)])

    def outward(offset, part):
        place = same_column(offset)
        src = joined_in.at[:, lanes_of(place, part * width)]
        dst = joined.at[part, rows_of(me)]
        if offset == 0:
            return pltpu.make_async_copy(src, dst, q_arrive.at[0, part])
        return to_column(src, dst, q_send.at[offset, part], q_arrive.at[offset, part], place)

    for offset in (4, 3, 5, 2, 6, 1, 7, 0):
        for part in range(3):
            outward(offset, part).start()
    steps = gather_schedule(weight_chunks(shards, wholes), send, arrive, keep)
    before, beside, after = spread_steps(steps, tiles, 3, 2)
    for step in before:
        step()

    def receive(source):
        offset = lax.rem(me + 8 - source, 8)
        for part in range(3):
            dst = joined.at[part, rows_of(source)]

            @pl.when(offset == 0)
            def _():
                outward(0, part).wait()

            @pl.when(offset != 0)
            def _():
                to_column(
                    dst, dst, q_send.at[offset, part], q_arrive.at[offset, part], source
                ).wait_recv()

    def back(tile):
        return to_column(
            low_ref.at[tile], mixed_in.at[:, lanes_of(me)], m_send.at[tile], m_arrive.at[me], tile
        )

    def back_here():
        return pltpu.make_async_copy(
            low_ref.at[me], mixed_in.at[:, lanes_of(me)], m_arrive.at[me]
        )

    receive(jnp.int32(0))

    def one_tile(tile, unused):
        @pl.when(tile < tiles - 1)
        def _():
            receive(tile + 1)

        scaled = both_heads(
            (joined[0, rows_of(tile)].astype(jnp.float32) * HD**-0.5).astype(jnp.bfloat16)
        )
        own = row_ref[rows_of(tile), :]
        own = jnp.concatenate([own, own], axis=0)

        def score(index, best, masked):
            here = rows_of(index)
            part = nt(scaled, joined[1, here])
            if masked:
                part = jnp.where(col_ref[:, here] <= own, part, MASKED)
            score_ref[:, here] = part
            for lane in range(0, TILE, wide):
                best = jnp.maximum(best, part[:, lane : lane + wide])
            return best

        best = jnp.full((2 * TILE, wide), MASKED, jnp.float32)
        best = lax.fori_loop(0, tile, lambda i, b: score(i, b, False), best)
        stop = jnp.minimum(tile + 2, tiles)
        best = lax.fori_loop(tile, stop, lambda i, b: score(i, b, True), best)
        best = jnp.max(best, axis=1, keepdims=True)

        def weigh(index, carry):
            total, accum = carry
            here = rows_of(index)
            weights = jnp.exp(score_ref[:, here] - best)
            for lane in range(0, TILE, wide):
                total = total + weights[:, lane : lane + wide]
            return (total, accum + nn(weights.astype(jnp.bfloat16), joined[2, here]))

        zero = jnp.zeros((2 * TILE, wide), jnp.float32)
        total, accum = lax.fori_loop(0, stop, weigh, (zero, zero))
        total = jnp.sum(total, axis=1, keepdims=True)
        mixed = own_lanes(accum / total)
        mixed_ref[rows_of(tile), :] = mixed
        low_ref[tile] = mixed.astype(jnp.bfloat16)
        log_total = jnp.broadcast_to(best + jnp.log(total), (2 * TILE, wide))
        log_ref[tile] = jnp.transpose(log_total)[:8]

        @pl.when(tile != me)
        def _():
            back(tile).start()

        @pl.when(tile == me)
        def _():
            back_here().start()

        for turn in range(tiles):
            if beside[turn]:

                @pl.when(tile == turn)
                def _():
                    for step in beside[turn]:
                        step()

        return unused

    lax.fori_loop(0, tiles, one_tile, 0)
    for step in after:
        step()
    for offset in range(1, 8):
        for part in range(3):
            outward(offset, part).wait_send()
        place = same_column(offset)
        back(place).wait_send()
        lane = mixed_in.at[:, lanes_of(place)]
        to_column(lane, lane, m_send.at[place], m_arrive.at[place], place).wait_recv()
    back_here().wait()


def attention_forward(joined, blocks, shards, collective_id):
    tokens = joined.shape[0]
    rows = tokens * 8
    wide = 2 * HD
    low = jnp.bfloat16
    chunks = sum(shard.size // (SLAB * LANES) for shard in shards)
    vmem = pl.BlockSpec(memory_space=pltpu.VMEM)
    any_spec = pl.BlockSpec(memory_space=pl.ANY)
    results = pl.pallas_call(
        functools.partial(forward_kernel, len(shards)),
        out_shape=[
            jax.ShapeDtypeStruct((3, rows, wide), low),
            jax.ShapeDtypeStruct((rows, wide), jnp.float32),
            jax.ShapeDtypeStruct((8, 8, 2 * TILE), jnp.float32),
            jax.ShapeDtypeStruct((tokens, HEADS * HD), low),
        ]
        + [whole_shape(shard) for shard in shards],
        in_specs=[vmem] * (3 + len(shards)),
        out_specs=[vmem] * 4 + [any_spec] * len(shards),
        scratch_shapes=[
            pltpu.VMEM((2 * TILE, rows), jnp.float32),
            pltpu.VMEM((8, TILE, wide), low),
            pltpu.SemaphoreType.DMA((8, 3)),
            pltpu.SemaphoreType.DMA((8, 3)),
            pltpu.SemaphoreType.DMA((8,)),
            pltpu.SemaphoreType.DMA((8,)),
            pltpu.SemaphoreType.DMA((chunks, 6)),
            pltpu.SemaphoreType.DMA((chunks, 6)),
            pltpu.SemaphoreType.DMA((chunks,)),
        ],
        compiler_params=pltpu.CompilerParams(
            collective_id=collective_id, has_side_effects=True, vmem_limit_bytes=60 * 2**20
        ),
        name="attention_forward",
    )(joined, blocks.reshape(rows, 1), blocks.reshape(1, rows), *shards)
    wholes = [whole.reshape(-1, whole.shape[-1]) for whole in results[4:]]
    return results[0], results[1], results[2], results[3], wholes


TILE = 256


def nt(left, right):
    return lax.dot_general(
        left, right, (((1,), (1,)), ((), ())), preferred_element_type=jnp.float32
    )


def nn(left, right):
    return lax.dot_general(
        left, right, (((1,), (0,)), ((), ())), preferred_element_type=jnp.float32
    )


def tn(left, right):
    return lax.dot_general(
        left, right, (((0,), (0,)), ((), ())), preferred_element_type=jnp.float32
    )


def both_heads(rows):
    lane = lax.broadcasted_iota(jnp.int32, rows.shape, 1)
    zero = jnp.zeros_like(rows)
    return jnp.concatenate(
        [jnp.where(lane < HD, rows, zero), jnp.where(lane < HD, zero, rows)], axis=0
    )


def own_lanes(pair):
    half = pair.shape[0] // 2
    lane = lax.broadcasted_iota(jnp.int32, (half, pair.shape[1]), 1)
    return jnp.where(lane < HD, pair[:half], pair[half:])


def grads_kernel(
    query_ref, key_ref, value_ref, grad_ref, mixed_ref, log_ref, row_ref, col_ref, out_ref, key_sum, value_sum
):
    tile = pl.program_id(0)
    tiles = pl.num_programs(0)
    wide = 2 * HD

    @pl.when(tile == 0)
    def _():
        key_sum[...] = jnp.zeros_like(key_sum)
        value_sum[...] = jnp.zeros_like(value_sum)

    scaled = both_heads((query_ref[...].astype(jnp.float32) * HD**-0.5).astype(jnp.bfloat16))
    grads = both_heads(grad_ref[...])
    products = grad_ref[...].astype(jnp.float32) * mixed_ref[...]
    products = jnp.transpose(products)
    delta = jnp.concatenate(
        [
            jnp.sum(products[:HD], axis=0, keepdims=True),
            jnp.sum(products[HD:], axis=0, keepdims=True),
        ],
        axis=1,
    )
    log_total = log_ref[0, :1]
    own = col_ref[...]
    own = jnp.concatenate([own, own], axis=1)

    def step(index, accum, masked):
        at = pl.multiple_of(index * TILE, TILE)
        here = pl.ds(at, TILE)
        keys = key_ref[here, :]
        scores = nt(keys, scaled)
        if masked:
            scores = jnp.where(row_ref[here, :] <= own, scores, MASKED)
        probs = jnp.exp(scores - log_total)
        value_sum[here, :] += nn(probs.astype(jnp.bfloat16), grads)
        grad_scores = (probs * (nt(value_ref[here, :], grads) - delta)).astype(jnp.bfloat16)
        key_sum[here, :] += nn(grad_scores, scaled)
        return accum + tn(grad_scores, keys)

    accum = jnp.zeros((2 * TILE, wide), jnp.float32)
    accum = lax.fori_loop(0, tile, lambda i, a: step(i, a, False), accum)
    stop = jnp.minimum(tile + 2, tiles)
    accum = lax.fori_loop(tile, stop, lambda i, a: step(i, a, True), accum)
    at = pl.multiple_of(tile * TILE, TILE)
    out_ref[pl.ds(at, TILE), :wide] = (own_lanes(accum) * HD**-0.5).astype(jnp.bfloat16)

    @pl.when(tile == tiles - 1)
    def _():
        out_ref[:, wide : 2 * wide] = key_sum[...].astype(jnp.bfloat16)
        out_ref[:, 2 * wide :] = value_sum[...].astype(jnp.bfloat16)


def attention_backward(joined, grad_mixed, mixed, log_total, blocks):
    rows = joined.shape[1]
    wide = 2 * HD
    tiles = rows // TILE
    return pl.pallas_call(
        grads_kernel,
        grid=(tiles,),
        out_shape=jax.ShapeDtypeStruct((rows, 3 * wide), jnp.bfloat16),
        in_specs=[
            pl.BlockSpec((None, TILE, wide), lambda t: (0, t, 0)),
            pl.BlockSpec((None, rows, wide), lambda t: (1, 0, 0)),
            pl.BlockSpec((None, rows, wide), lambda t: (2, 0, 0)),
            pl.BlockSpec((TILE, wide), lambda t: (t, 0)),
            pl.BlockSpec((TILE, wide), lambda t: (t, 0)),
            pl.BlockSpec((1, 8, 2 * TILE), lambda t: (t, 0, 0)),
            pl.BlockSpec((rows, 1), lambda t: (0, 0)),
            pl.BlockSpec((1, TILE), lambda t: (0, t)),
        ],
        out_specs=pl.BlockSpec((rows, 3 * wide), lambda t: (0, 0)),
        scratch_shapes=[
            pltpu.VMEM((rows, wide), jnp.float32),
            pltpu.VMEM((rows, wide), jnp.float32),
        ],
        name="attention_backward",
    )(
        joined,
        joined,
        joined,
        grad_mixed,
        mixed,
        log_total,
        blocks.reshape(rows, 1),
        blocks.reshape(1, rows),
    )


def to_heads(rows, groups, count):
    tokens = rows.shape[0]
    wide = rows.shape[1] // (groups * count)
    split = rows.reshape(tokens, count, groups, wide).transpose(2, 0, 1, 3)
    split = split.reshape(groups, tokens, count * wide)
    whole = lax.all_to_all(split, "ctx", 0, 0, tiled=True)
    return whole.reshape(groups * tokens, count * wide)


def to_tokens(rows, groups, count):
    tokens = rows.shape[0] // groups
    wide = rows.shape[1] // count
    split = lax.all_to_all(rows.reshape(groups, tokens, count * wide), "ctx", 0, 0, tiled=True)
    split = split.reshape(groups, tokens, count, wide).transpose(1, 2, 0, 3)
    return split.reshape(tokens, count * groups * wide)


def fast_body(
    tokens_in, block_ids, w_query, w_key, w_value, w_out, w_up, w_down, norm_gain, cotangent
):
    width = tokens_in.shape[2]
    groups = lax.axis_size("ctx")
    kinds = norm_gain.shape[0]
    small = jnp.concatenate(
        [norm_gain.astype(jnp.float32).reshape(1, -1), block_ids.astype(jnp.float32).reshape(-1, 128)]
    )
    small = jnp.pad(small, ((0, 8 - small.shape[0]), (0, 0)))
    smalls, full_query, full_key, full_value = gather_over_devices(
        [small, w_query, w_key, w_value], 1
    )
    smalls = smalls.reshape(32, 8, 128)
    gains = smalls[:, 0].reshape(32, kinds, -1).transpose(1, 0, 2).reshape(kinds, width)
    blocks = lax.dynamic_slice_in_dim(smalls, lax.axis_index("fsdp") * groups, groups, 0)
    blocks = blocks[:, 1:3].reshape(-1).astype(jnp.int32)
    tokens = tokens_in[0].astype(jnp.float32)
    normed = layer_norm(tokens, gains[0]).astype(jnp.bfloat16)
    queries = jnp.concatenate(
        [project(normed, w).astype(jnp.bfloat16) for w in (full_query, full_key, full_value)], axis=1
    )
    joined, mixed, log_total, mixed_low, wholes = attention_forward(
        queries, blocks, [w_out, w_up, w_down], 2
    )
    full_out, full_up, full_down = wholes
    branch = project(mixed_low, full_out)
    hidden = tokens + layer_norm(branch, gains[1])
    inner = layer_norm(hidden, gains[2]).astype(jnp.bfloat16)
    lifted = project(inner, full_up)
    active = gelu_exact(lifted).astype(jnp.bfloat16)
    lowered = project(active, full_down)
    layer_out = (hidden + layer_norm(lowered, gains[3])).astype(jnp.bfloat16)[None]
    upstream = cotangent[0].astype(jnp.float32)
    unused_four, pull_four = jax.vjp(layer_norm, lowered, gains[3])
    grad_lowered, gain_four = pull_four(upstream)
    grad_lowered = grad_lowered.astype(jnp.bfloat16)
    grad_down = outer_sum(active, grad_lowered).astype(jnp.bfloat16)
    grad_active = back_project(grad_lowered, full_down)
    unused_gelu, pull_gelu = jax.vjp(gelu_exact, lifted)
    grad_lifted = pull_gelu(grad_active)[0].astype(jnp.bfloat16)
    grad_up = outer_sum(inner, grad_lifted).astype(jnp.bfloat16)
    grad_inner = back_project(grad_lifted, full_up)
    unused_three, pull_three = jax.vjp(layer_norm, hidden, gains[2])
    grad_hidden_branch, gain_three = pull_three(grad_inner)
    grad_hidden = upstream + grad_hidden_branch
    unused_two, pull_two = jax.vjp(layer_norm, branch, gains[1])
    grad_branch, gain_two = pull_two(grad_hidden)
    grad_branch = grad_branch.astype(jnp.bfloat16)
    grad_out = outer_sum(mixed_low, grad_branch).astype(jnp.bfloat16)
    grad_mixed = back_project(grad_branch, full_out).astype(jnp.bfloat16)
    grad_joined = attention_backward(
        joined, to_heads(grad_mixed, groups, 1), mixed, log_total, blocks
    )
    grad_qkv = to_tokens(grad_joined, groups, 3)
    grad_three = outer_sum(normed, grad_qkv).astype(jnp.bfloat16)
    grad_normed = (
        back_project(grad_qkv[:, :width], full_query)
        + back_project(grad_qkv[:, width : 2 * width], full_key)
        + back_project(grad_qkv[:, 2 * width :], full_value)
    )
    unused_one, pull_one = jax.vjp(layer_norm, tokens, gains[0])
    grad_norm_in, gain_one = pull_one(grad_normed)
    grad_tokens = (grad_hidden + grad_norm_in).astype(jnp.bfloat16)[None]
    gain_grads = jnp.stack([gain_one, gain_two, gain_three, gain_four])
    sums, gain_sum = sum_over_devices(
        [grad_three, grad_out, grad_up, grad_down], by_owner(gain_grads), 3
    )
    return (
        layer_out,
        grad_tokens,
        sums[0],
        sums[1],
        sums[2],
        sums[3],
        sums[4:8].transpose(1, 0, 2).reshape(w_up.shape),
        sums[8:].reshape(w_down.shape),
        gain_sum[0].reshape(norm_gain.shape),
    )


def by_owner(gain_grads):
    kinds, width = gain_grads.shape
    rows = gain_grads.reshape(kinds, 32, width // 32).transpose(1, 0, 2).reshape(32, 1, -1)
    return jnp.pad(rows, ((0, 0), (0, 7), (0, 0))).reshape(2, 2, 4, 2, 8, rows.shape[-1])


def pick(mesh):
    return fast_body if mesh.shape["ctx"] * 2 == HEADS else body


def solution(mesh):
    placed = (
        P("fsdp", "ctx", None),
        P("fsdp", "ctx"),
        P(("fsdp", "ctx"), None),
        P(("fsdp", "ctx"), None),
        P(("fsdp", "ctx"), None),
        P(("fsdp", "ctx"), None),
        P(("fsdp", "ctx"), None),
        P(("fsdp", "ctx"), None),
        P(None, ("fsdp", "ctx")),
        P("fsdp", "ctx", None),
    )
    return jax.shard_map(
        pick(mesh),
        mesh=mesh,
        in_specs=placed,
        out_specs=(
            P("fsdp", "ctx", None),
            P("fsdp", "ctx", None),
            P(("fsdp", "ctx"), None),
            P(("fsdp", "ctx"), None),
            P(("fsdp", "ctx"), None),
            P(("fsdp", "ctx"), None),
            P(("fsdp", "ctx"), None),
            P(("fsdp", "ctx"), None),
            P(None, ("fsdp", "ctx")),
        ),
        check_vma=False,
    )
```

```python
import functools
import math

import jax
import jax.numpy as jnp
from jax import lax
from jax.experimental import pallas as pl
from jax.experimental.pallas import tpu as pltpu
from jax.sharding import PartitionSpec as P

HEADS = 16
HD = 64


EPS = 1e-05
MASKED = -1e30


def from_behind(block, axis, distance):
    devices = range(lax.axis_size(axis))
    route = [((i - distance) % len(devices), i) for i in devices]
    return lax.ppermute(block, axis, route)


def layer_norm(values, gain):
    centre = values - jnp.mean(values, axis=-1, keepdims=True)
    spread = jnp.mean(centre * centre, axis=-1, keepdims=True)
    return centre * lax.rsqrt(spread + EPS) * gain


def gelu_exact(values):
    return jax.nn.gelu(values, approximate=False)


def project(left, right):
    return jnp.dot(left, right, preferred_element_type=jnp.float32)


def outer_sum(left, right):
    return lax.dot_general(
        left, right, (((0,), (0,)), ((), ())), preferred_element_type=jnp.float32
    )


def back_project(grad, weight):
    return lax.dot_general(
        grad, weight, (((1,), (1,)), ((), ())), preferred_element_type=jnp.float32
    )


def split_heads(values):
    return values.reshape(values.shape[0], HEADS, HD)


def attend(carry, head_queries, query_blocks, key_rows, key_blocks, scale):
    best, total, accum = carry
    width = key_rows.shape[1] // 2
    keys = split_heads(key_rows[:, :width])
    values = split_heads(key_rows[:, width:])
    scores = (
        jnp.einsum("qhd,khd->hqk", head_queries, keys, preferred_element_type=jnp.float32) * scale
    )
    allowed = key_blocks[None, None, :] <= query_blocks[None, :, None]
    scores = jnp.where(allowed, scores, MASKED)
    newest = jnp.maximum(best, jnp.max(scores, axis=2))
    weights = jnp.where(allowed, jnp.exp(scores - newest[:, :, None]), 0.0)
    factor = jnp.exp(best - newest)
    total = total * factor + jnp.sum(weights, axis=2)
    update = jnp.einsum(
        "hqk,khd->qhd", weights.astype(jnp.bfloat16), values, preferred_element_type=jnp.float32
    )
    accum = accum * jnp.transpose(factor)[:, :, None] + update
    return (newest, total, accum)


def score_grads(
    head_queries, head_grads, log_total, delta, query_blocks, key_rows, key_blocks, scale
):
    width = key_rows.shape[1] // 2
    rows = key_rows.shape[0]
    query_rows = head_queries.shape[0]
    keys = split_heads(key_rows[:, :width])
    values = split_heads(key_rows[:, width:])
    scores = (
        jnp.einsum("qhd,khd->hqk", head_queries, keys, preferred_element_type=jnp.float32) * scale
    )
    allowed = key_blocks[None, None, :] <= query_blocks[None, :, None]
    probs = jnp.where(
        allowed, jnp.exp(jnp.where(allowed, scores, MASKED) - log_total[:, :, None]), 0.0
    )
    grad_values = jnp.einsum(
        "hqk,qhd->khd", probs.astype(jnp.bfloat16), head_grads, preferred_element_type=jnp.float32
    )
    grad_probs = jnp.einsum("qhd,khd->hqk", head_grads, values, preferred_element_type=jnp.float32)
    grad_scores = (probs * (grad_probs - delta[:, :, None])).astype(jnp.bfloat16)
    grad_queries = (
        jnp.einsum("hqk,khd->qhd", grad_scores, keys, preferred_element_type=jnp.float32) * scale
    )
    grad_keys = (
        jnp.einsum("hqk,qhd->khd", grad_scores, head_queries, preferred_element_type=jnp.float32)
        * scale
    )
    joined = jnp.concatenate(
        [grad_keys.reshape(rows, width), grad_values.reshape(rows, width)], axis=1
    )
    return (grad_queries.reshape(query_rows, width), joined)


def guarded(head_queries, head_grads, log_total, delta, query_blocks, key_rows, key_blocks, scale):
    live = jnp.min(key_blocks) <= jnp.max(query_blocks)
    rows, columns = key_rows.shape

    def run(unused):
        return score_grads(
            head_queries, head_grads, log_total, delta, query_blocks, key_rows, key_blocks, scale
        )

    def skip(unused):
        return (
            jnp.zeros((head_queries.shape[0], columns // 2), jnp.float32),
            jnp.zeros((rows, columns), jnp.float32),
        )

    return lax.cond(live, run, skip, 0)


def body(tokens_in, block_ids, w_query, w_key, w_value, w_out, w_up, w_down, norm_gain, cotangent):
    scale = 1.0 / math.sqrt(HD)
    stride = tokens_in.shape[1]
    width = tokens_in.shape[2]
    cycle_size = lax.axis_size("ctx")
    place = lax.axis_index("ctx")
    shards = (w_query, w_key, w_value, w_out, w_up, w_down, norm_gain)
    gathered = (
        lax.all_gather(w_query, ("fsdp", "ctx"), axis=0, tiled=True),
        lax.all_gather(w_key, ("fsdp", "ctx"), axis=0, tiled=True),
        lax.all_gather(w_value, ("fsdp", "ctx"), axis=0, tiled=True),
        lax.all_gather(w_out, ("fsdp", "ctx"), axis=0, tiled=True),
        lax.all_gather(w_up, ("fsdp", "ctx"), axis=0, tiled=True),
        lax.all_gather(w_down, ("fsdp", "ctx"), axis=0, tiled=True),
        lax.all_gather(norm_gain, ("fsdp", "ctx"), axis=1, tiled=True),
    )
    full_query, full_key, full_value, full_out, full_up, full_down, full_gain = gathered
    gains = full_gain.astype(jnp.float32)
    sequence_blocks = lax.all_gather(block_ids, "ctx", axis=1, tiled=True)[0]
    own_blocks = block_ids[0]
    top_block = jnp.max(own_blocks)
    tokens = tokens_in[0].astype(jnp.float32)
    normed = layer_norm(tokens, gains[0]).astype(jnp.bfloat16)
    queries = project(normed, full_query).astype(jnp.bfloat16)
    key_value = jnp.concatenate(
        [project(normed, full_key), project(normed, full_value)], axis=1
    ).astype(jnp.bfloat16)
    head_queries = split_heads(queries)
    start_state = (
        jnp.full((HEADS, stride), MASKED, jnp.float32),
        jnp.zeros((HEADS, stride), jnp.float32),
        jnp.zeros((stride, HEADS, HD), jnp.float32),
    )
    piece = lax.all_gather(key_value, "ctx", axis=0, tiled=True)
    rows = piece.shape[0]
    size = math.gcd(rows, stride)

    def visit(index, state):
        key_rows = lax.dynamic_slice_in_dim(piece, index * size, size, 0)
        key_blocks = lax.dynamic_slice_in_dim(sequence_blocks, index * size, size, 0)
        return lax.cond(
            jnp.min(key_blocks) <= top_block,
            lambda inner: attend(inner, head_queries, own_blocks, key_rows, key_blocks, scale),
            lambda inner: inner,
            state,
        )

    best, total, accum = lax.fori_loop(0, rows // size, visit, start_state)
    mixed = accum / jnp.transpose(total)[:, :, None]
    log_total = best + jnp.log(total)
    mixed_low = mixed.reshape(stride, width).astype(jnp.bfloat16)
    branch = project(mixed_low, full_out)
    hidden = tokens + layer_norm(branch, gains[1])
    inner = layer_norm(hidden, gains[2]).astype(jnp.bfloat16)
    lifted = project(inner, full_up)
    active = gelu_exact(lifted).astype(jnp.bfloat16)
    lowered = project(active, full_down)
    layer_out = (hidden + layer_norm(lowered, gains[3])).astype(jnp.bfloat16)[None]
    regathered = (
        lax.all_gather(shards[0], ("fsdp", "ctx"), axis=0, tiled=True),
        lax.all_gather(shards[1], ("fsdp", "ctx"), axis=0, tiled=True),
        lax.all_gather(shards[2], ("fsdp", "ctx"), axis=0, tiled=True),
        lax.all_gather(shards[3], ("fsdp", "ctx"), axis=0, tiled=True),
        lax.all_gather(shards[4], ("fsdp", "ctx"), axis=0, tiled=True),
        lax.all_gather(shards[5], ("fsdp", "ctx"), axis=0, tiled=True),
        lax.all_gather(shards[6], ("fsdp", "ctx"), axis=1, tiled=True),
    )
    back_query, back_key, back_value, back_out, back_up, back_down, back_gain = regathered
    back_gains = back_gain.astype(jnp.float32)
    upstream = cotangent[0].astype(jnp.float32)
    unused_four, pull_four = jax.vjp(layer_norm, lowered, back_gains[3])
    grad_lowered, gain_four = pull_four(upstream)
    grad_lowered = grad_lowered.astype(jnp.bfloat16)
    grad_down = outer_sum(active, grad_lowered)
    grad_active = back_project(grad_lowered, back_down)
    unused_gelu, pull_gelu = jax.vjp(gelu_exact, lifted)
    grad_lifted = pull_gelu(grad_active)[0].astype(jnp.bfloat16)
    grad_up = outer_sum(inner, grad_lifted)
    grad_inner = back_project(grad_lifted, back_up)
    unused_three, pull_three = jax.vjp(layer_norm, hidden, back_gains[2])
    grad_hidden_branch, gain_three = pull_three(grad_inner)
    grad_hidden = upstream + grad_hidden_branch
    unused_two, pull_two = jax.vjp(layer_norm, branch, back_gains[1])
    grad_branch, gain_two = pull_two(grad_hidden)
    grad_branch = grad_branch.astype(jnp.bfloat16)
    grad_out = outer_sum(mixed_low, grad_branch)
    grad_mixed = back_project(grad_branch, back_out).astype(jnp.bfloat16)
    head_grads = split_heads(grad_mixed)
    delta = jnp.transpose(jnp.sum(head_grads.astype(jnp.float32) * mixed, axis=2))
    query_grad, kv_grad = guarded(
        head_queries, head_grads, log_total, delta, own_blocks, key_value, own_blocks, scale
    )

    def pass_grads(values):
        return from_behind(values.astype(jnp.bfloat16), "ctx", 1).astype(values.dtype)

    def cycle_keys(step, state):
        travel, kv_accum, query_accum = state
        travel = from_behind(travel, "ctx", 1)
        kv_accum = pass_grads(kv_accum)
        source = (place - step) % cycle_size
        key_blocks = lax.dynamic_slice_in_dim(sequence_blocks, source * stride, stride, 0)
        part_query, part_kv = guarded(
            head_queries, head_grads, log_total, delta, own_blocks, travel, key_blocks, scale
        )
        return (travel, kv_accum + part_kv, query_accum + part_query)

    unused_travel, kv_accum, query_grad = lax.fori_loop(
        1, cycle_size, cycle_keys, (key_value, kv_grad, query_grad)
    )
    kv_grad = pass_grads(kv_accum)
    query_low = query_grad.astype(jnp.bfloat16)
    kv_low = kv_grad.astype(jnp.bfloat16)
    key_low = kv_low[:, :width]
    value_low = kv_low[:, width:]
    grad_query = outer_sum(normed, query_low)
    grad_key = outer_sum(normed, key_low)
    grad_value = outer_sum(normed, value_low)
    grad_normed = (
        back_project(query_low, back_query)
        + back_project(key_low, back_key)
        + back_project(value_low, back_value)
    )
    unused_one, pull_one = jax.vjp(layer_norm, tokens, back_gains[0])
    grad_norm_in, gain_one = pull_one(grad_normed)
    grad_tokens = (grad_hidden + grad_norm_in).astype(jnp.bfloat16)[None]
    gain_grads = jnp.stack([gain_one, gain_two, gain_three, gain_four])
    summed = (
        lax.psum_scatter(grad_query, ("fsdp", "ctx"), scatter_dimension=0, tiled=True),
        lax.psum_scatter(grad_key, ("fsdp", "ctx"), scatter_dimension=0, tiled=True),
        lax.psum_scatter(grad_value, ("fsdp", "ctx"), scatter_dimension=0, tiled=True),
        lax.psum_scatter(grad_out, ("fsdp", "ctx"), scatter_dimension=0, tiled=True),
        lax.psum_scatter(grad_up, ("fsdp", "ctx"), scatter_dimension=0, tiled=True),
        lax.psum_scatter(grad_down, ("fsdp", "ctx"), scatter_dimension=0, tiled=True),
        lax.psum_scatter(gain_grads, ("fsdp", "ctx"), scatter_dimension=1, tiled=True),
    )
    return (
        layer_out,
        grad_tokens,
        summed[0],
        summed[1],
        summed[2],
        summed[3],
        summed[4],
        summed[5],
        summed[6],
    )


MESH = pl.DeviceIdType.MESH
SLAB = 32
LANES = 1024


def places():
    fsdp, ctx = lax.axis_index("fsdp"), lax.axis_index("ctx")
    return lax.div(fsdp, 2), lax.rem(fsdp, 2), lax.div(ctx, 2), lax.rem(ctx, 2)


def at_place(y, core, z, x):
    return (y * 2 + core, z * 2 + x)


def meet(devices):
    barrier = pltpu.get_barrier_semaphore()
    for device in devices:
        pl.semaphore_signal(barrier, inc=1, device_id=device, device_id_type=MESH)
    pl.semaphore_wait(barrier, len(devices))


def sum_kernel(views, lines, *refs):
    grads, gain_ref = refs[:lines], refs[lines]
    out_ref, gain_out, own, zero, first_x, first_y, second, third = refs[lines + 1 : lines + 9]
    g_own, g_zero, g_first, g_second, g_third, load, send, arrive = refs[lines + 9 :]
    y, core, z, x = places()
    partner = at_place(y, 1 - core, z, x)
    beside = at_place(y, core, z, 1 - x)
    across = at_place(1 - y, core, z, x)
    rank = [lax.rem(z + d, 4) for d in (1, 2, 3)]
    others = [at_place(y, core, r, x) for r in rank]
    meet([partner, beside, across] + others)
    count = len(views) + 1
    last = len(views)

    def pick(k, side):
        if k == last:
            return gain_ref.at[:, side]
        ref, part = views[k]
        return grads[ref].at[(slice(None), side, slice(None), slice(None)) + part]

    def remote(src, dst, k, phase, device):
        return pltpu.make_async_remote_copy(
            src_ref=src,
            dst_ref=dst,
            send_sem=send.at[k, phase],
            recv_sem=arrive.at[k, phase],
            device_id=device,
            device_id_type=MESH,
        )

    def add(total, landed, pairs, rows):
        def one(i, unused):
            into, out_of = pairs(i)
            total[into] = total[into] + landed[out_of]
            return unused

        lax.fori_loop(0, rows, one, 0)

    def steps(k):
        if k == last:
            return g_own, g_zero, g_first, g_second, g_third
        return own.at[k], zero.at[k], (first_y if k % 2 else first_x).at[k // 2], second.at[k], third.at[k]

    def phase_zero(k):
        return remote(pick(k, 1 - core), steps(k)[1], k, 0, partner)

    def loading(k):
        return pltpu.make_async_copy(pick(k, core), steps(k)[0], load.at[k])

    def phase_one(k):
        total = steps(k)[0]
        if k % 2:
            return remote(total.at[1 - y], steps(k)[2], k, 1, across)
        return remote(total.at[:, :, 1 - x], steps(k)[2], k, 1, beside)

    def phase_two(k):
        total = steps(k)[0]
        if k % 2:
            return remote(total.at[y, :, 1 - x], steps(k)[3], k, 2, beside)
        return remote(total.at[1 - y, :, x], steps(k)[3], k, 2, across)

    def phase_three(k):
        total = steps(k)[0]
        return [
            remote(total.at[y, r, x], steps(k)[4].at[2 - d], k, 3 + d, others[d])
            for d, r in enumerate(rank)
        ]

    def after_zero(k):
        loading(k).wait()
        phase_zero(k).wait()
        total, landed = steps(k)[:2]
        split = lambda i: (lax.div(i, 8), lax.rem(lax.div(i, 2), 4), lax.rem(i, 2))
        add(total, landed, lambda i: (split(i), split(i)), 16)
        phase_one(k).start()

    def after_one(k):
        phase_one(k).wait()
        total, landed = steps(k)[0], steps(k)[2]
        if k % 2:
            add(total, landed, lambda i: ((y, lax.div(i, 2), lax.rem(i, 2)), (lax.div(i, 2), lax.rem(i, 2))), 8)
        else:
            add(total, landed, lambda i: ((lax.div(i, 4), lax.rem(i, 4), x), (lax.div(i, 4), lax.rem(i, 4))), 8)
        phase_two(k).start()

    def after_two(k):
        phase_two(k).wait()
        total, landed = steps(k)[0], steps(k)[3]
        add(total, landed, lambda i: ((y, i, x), (i,)), 4)
        for copy in phase_three(k):
            copy.start()

    def after_three(k):
        for copy in phase_three(k):
            copy.wait()
        total, landed = steps(k)[0], steps(k)[4]
        value = total[y, z, x].astype(jnp.float32)
        for d in range(3):
            value = value + landed[d].astype(jnp.float32)
        if k == last:
            gain_out[...] = value
        else:
            out_ref[k] = value

    for k in range(count):
        loading(k).start()
        phase_zero(k).start()
    for step in range(count + 3):
        for lag, run in enumerate((after_zero, after_one, after_two, after_three)):
            if 0 <= step - lag < count:
                run(step - lag)


def sum_over_devices(grads, gain, collective_id):
    shaped, views = [], []
    for ref, grad in enumerate(grads):
        rows, columns = grad.shape
        if columns == LANES:
            parts = rows // (32 * SLAB)
            shaped.append(grad.reshape(2, 2, 4, 2, parts, SLAB, LANES))
            views += [(ref, (part,)) for part in range(parts)]
        else:
            parts = columns // LANES
            shaped.append(grad.reshape(2, 2, 4, 2, SLAB, columns))
            views += [(ref, (slice(None), pl.ds(part * LANES, LANES))) for part in range(parts)]
    count = len(views)
    low = jnp.bfloat16
    slab = (SLAB, LANES)
    any_spec = pl.BlockSpec(memory_space=pl.ANY)
    out, gain_out = pl.pallas_call(
        functools.partial(sum_kernel, views, len(grads)),
        out_shape=(
            jax.ShapeDtypeStruct((count,) + slab, jnp.float32),
            jax.ShapeDtypeStruct((8, 128), jnp.float32),
        ),
        in_specs=[any_spec] * (len(grads) + 1),
        out_specs=(pl.BlockSpec(memory_space=pltpu.VMEM), pl.BlockSpec(memory_space=pltpu.VMEM)),
        scratch_shapes=[
            pltpu.VMEM((count, 2, 4, 2) + slab, low),
            pltpu.VMEM((count, 2, 4, 2) + slab, low),
            pltpu.VMEM(((count + 1) // 2, 2, 4) + slab, low),
            pltpu.VMEM(((count + 1) // 2, 4, 2) + slab, low),
            pltpu.VMEM((count, 4) + slab, low),
            pltpu.VMEM((count, 3) + slab, low),
            pltpu.VMEM((2, 4, 2, 8, 128), jnp.float32),
            pltpu.VMEM((2, 4, 2, 8, 128), jnp.float32),
            pltpu.VMEM(((4, 2) if count % 2 else (2, 4)) + (8, 128), jnp.float32),
            pltpu.VMEM((4, 8, 128), jnp.float32),
            pltpu.VMEM((3, 8, 128), jnp.float32),
            pltpu.SemaphoreType.DMA((count + 1,)),
            pltpu.SemaphoreType.DMA((count + 1, 6)),
            pltpu.SemaphoreType.DMA((count + 1, 6)),
        ],
        compiler_params=pltpu.CompilerParams(
            collective_id=collective_id, has_side_effects=True, vmem_limit_bytes=60 * 2**20
        ),
        name="sum_over_devices",
    )(*shaped, gain)
    return out, gain_out


WINDOW = 4
ORDERS = ("zxy", "zyx")


def gather_schedule(chunks, send, arrive, keep):
    here = dict(zip(("y", "core", "z", "x"), places()))
    count = len(chunks)
    slots = {"x": 0, "y": 1, "core": 2, "z": 3}

    def copies(k, stage):
        own, whole = chunks[k]
        order = tuple(ORDERS[k % len(ORDERS)]) + ("core",)
        axis, done = order[stage], order[:stage]
        part = whole(*(slice(None) if a in done else here[a] for a in here))
        made = []
        for distance in range(1, 4 if axis == "z" else 2):
            there = dict(here)
            there[axis] = lax.rem(here[axis] + distance, 4 if axis == "z" else 2)
            made.append(
                pltpu.make_async_remote_copy(
                    src_ref=part if stage else own,
                    dst_ref=part,
                    send_sem=send.at[k, slots[axis] + distance - 1],
                    recv_sem=arrive.at[k, slots[axis] + distance - 1],
                    device_id=at_place(*there.values()),
                    device_id_type=MESH,
                )
            )
        return made

    def keeping(k):
        own, whole = chunks[k]
        return pltpu.make_async_copy(own, whole(*here.values()), keep.at[k])

    def enter(k):
        keeping(k).start()
        for copy in copies(k, 0):
            copy.start()

    def begin():
        for k in range(min(WINDOW, count)):
            enter(k)

    def after(k, stage):
        if stage == 0:
            if k + WINDOW < count:
                enter(k + WINDOW)
            keeping(k).wait()
        for copy in copies(k, stage):
            copy.wait()
        if stage < 3:
            for copy in copies(k, stage + 1):
                copy.start()

    steps = [begin]
    for step in range(count + 3):
        for stage in range(4):
            if 0 <= step - stage < count:
                steps.append(functools.partial(after, step - stage, stage))
    return steps


def weight_chunks(shards, wholes):
    chunks = []
    for own, whole in zip(shards, wholes):
        columns = own.shape[1]
        if len(whole.shape) == 7:
            for part in range(whole.shape[4]):
                chunks.append(
                    (own.at[pl.ds(part * SLAB, SLAB)], lambda *p, w=whole, n=part: w.at[p + (n,)])
                )
        elif columns > LANES:
            for part in range(columns // LANES):
                at = pl.ds(part * LANES, LANES)
                chunks.append(
                    (own.at[:, at], lambda *p, w=whole, n=at: w.at[p + (slice(None), n)])
                )
        else:
            chunks.append((own, lambda *p, w=whole: w.at[p]))
    return chunks


def whole_shape(shard):
    rows, columns = shard.shape
    if rows > SLAB and columns == LANES:
        return jax.ShapeDtypeStruct((2, 2, 4, 2, rows // SLAB, SLAB, columns), shard.dtype)
    return jax.ShapeDtypeStruct((2, 2, 4, 2, rows, columns), shard.dtype)


def gather_kernel(count, *refs):
    shards, wholes = refs[:count], refs[count : 2 * count]
    send, arrive, keep = refs[2 * count :]
    y, core, z, x = places()
    meet(
        [at_place(y, 1 - core, z, x), at_place(y, core, z, 1 - x), at_place(1 - y, core, z, x)]
        + [at_place(y, core, lax.rem(z + d, 4), x) for d in (1, 2, 3)]
    )
    for step in gather_schedule(weight_chunks(shards, wholes), send, arrive, keep):
        step()


def gather_over_devices(shards, collective_id):
    shapes = [whole_shape(shard) for shard in shards]
    count = sum(max(1, shard.size // (SLAB * LANES)) for shard in shards)
    any_spec = pl.BlockSpec(memory_space=pl.ANY)
    wholes = pl.pallas_call(
        functools.partial(gather_kernel, len(shards)),
        out_shape=shapes,
        in_specs=[pl.BlockSpec(memory_space=pltpu.VMEM)] * len(shards),
        out_specs=[any_spec] * len(shards),
        scratch_shapes=[
            pltpu.SemaphoreType.DMA((count, 6)),
            pltpu.SemaphoreType.DMA((count, 6)),
            pltpu.SemaphoreType.DMA((count,)),
        ],
        compiler_params=pltpu.CompilerParams(
            collective_id=collective_id, has_side_effects=True, vmem_limit_bytes=60 * 2**20
        ),
        name="gather_over_devices",
    )(*shards)
    return [whole.reshape(-1, whole.shape[-1]) for whole in wholes]


FIRST = 3


def same_column(offset):
    return lax.rem(lax.axis_index("ctx") + offset, lax.axis_size("ctx"))


def greet(devices):
    meet(devices + [(lax.axis_index("fsdp"), same_column(o)) for o in range(1, 8)])


def to_column(src, dst, send, arrive, place):
    return pltpu.make_async_remote_copy(
        src_ref=src,
        dst_ref=dst,
        send_sem=send,
        recv_sem=arrive,
        device_id=(lax.axis_index("fsdp"), place),
        device_id_type=MESH,
    )


def rows_of(index):
    return pl.ds(pl.multiple_of(index * TILE, TILE), TILE)


def lanes_of(index, start=0):
    return pl.ds(pl.multiple_of(start + index * 2 * HD, 2 * HD), 2 * HD)


def spread_steps(steps, tiles, first, per_tile):
    before, rest = steps[:first], steps[first:]
    beside = [rest[t * per_tile : (t + 1) * per_tile] for t in range(tiles)]
    return before, beside, rest[tiles * per_tile :]


def forward_kernel(count, *refs):
    joined_in, row_ref, col_ref = refs[:3]
    shards, refs = refs[3 : 3 + count], refs[3 + count :]
    joined, mixed_ref, log_ref, mixed_in = refs[:4]
    wholes, refs = refs[4 : 4 + count], refs[4 + count :]
    score_ref, low_ref, q_send, q_arrive, m_send, m_arrive, send, arrive, keep = refs
    y, core, z, x = places()
    me = lax.axis_index("ctx")
    tiles = 8
    wide = 2 * HD
    width = HEADS * HD
    greet([at_place(y, 1 - core, z, x), at_place(1 - y, core, z, x)])

    def outward(offset, part):
        place = same_column(offset)
        src = joined_in.at[:, lanes_of(place, part * width)]
        dst = joined.at[part, rows_of(me)]
        if offset == 0:
            return pltpu.make_async_copy(src, dst, q_arrive.at[0, part])
        return to_column(src, dst, q_send.at[offset, part], q_arrive.at[offset, part], place)

    for offset in (4, 3, 5, 2, 6, 1, 7, 0):
        for part in range(3):
            outward(offset, part).start()
    steps = gather_schedule(weight_chunks(shards, wholes), send, arrive, keep)
    before, beside, after = spread_steps(steps, tiles, FIRST, 2)
    for step in before:
        step()

    def receive(source):
        offset = lax.rem(me + 8 - source, 8)
        for part in range(3):
            dst = joined.at[part, rows_of(source)]

            @pl.when(offset == 0)
            def _():
                outward(0, part).wait()

            @pl.when(offset != 0)
            def _():
                to_column(
                    dst, dst, q_send.at[offset, part], q_arrive.at[offset, part], source
                ).wait_recv()

    def back(tile):
        return to_column(
            low_ref.at[tile], mixed_in.at[:, lanes_of(me)], m_send.at[tile], m_arrive.at[me], tile
        )

    def back_here():
        return pltpu.make_async_copy(
            low_ref.at[me], mixed_in.at[:, lanes_of(me)], m_arrive.at[me]
        )

    receive(jnp.int32(0))

    def one_tile(tile, unused):
        @pl.when(tile < tiles - 1)
        def _():
            receive(tile + 1)

        scaled = both_heads(
            (joined[0, rows_of(tile)].astype(jnp.float32) * HD**-0.5).astype(jnp.bfloat16)
        )
        own = row_ref[rows_of(tile), :]
        own = jnp.concatenate([own, own], axis=0)

        def score(index, best, masked):
            here = rows_of(index)
            part = nt(scaled, joined[1, here])
            if masked:
                part = jnp.where(col_ref[:, here] <= own, part, MASKED)
            score_ref[:, here] = part
            for lane in range(0, TILE, wide):
                best = jnp.maximum(best, part[:, lane : lane + wide])
            return best

        best = jnp.full((2 * TILE, wide), MASKED, jnp.float32)
        best = lax.fori_loop(0, tile, lambda i, b: score(i, b, False), best)
        stop = jnp.minimum(tile + 2, tiles)
        best = lax.fori_loop(tile, stop, lambda i, b: score(i, b, True), best)
        best = jnp.max(best, axis=1, keepdims=True)

        def weigh(index, carry):
            total, accum = carry
            here = rows_of(index)
            weights = jnp.exp(score_ref[:, here] - best)
            for lane in range(0, TILE, wide):
                total = total + weights[:, lane : lane + wide]
            return (total, accum + nn(weights.astype(jnp.bfloat16), joined[2, here]))

        zero = jnp.zeros((2 * TILE, wide), jnp.float32)
        total, accum = lax.fori_loop(0, stop, weigh, (zero, zero))
        total = jnp.sum(total, axis=1, keepdims=True)
        mixed = own_lanes(accum / total)
        mixed_ref[rows_of(tile), :] = mixed
        low_ref[tile] = mixed.astype(jnp.bfloat16)
        log_total = jnp.broadcast_to(best + jnp.log(total), (2 * TILE, wide))
        log_ref[tile] = jnp.transpose(log_total)[:8]

        @pl.when(tile != me)
        def _():
            back(tile).start()

        @pl.when(tile == me)
        def _():
            back_here().start()

        for turn in range(tiles):
            if beside[turn]:

                @pl.when(tile == turn)
                def _():
                    for step in beside[turn]:
                        step()

        return unused

    lax.fori_loop(0, tiles, one_tile, 0)
    for step in after:
        step()
    for offset in range(1, 8):
        for part in range(3):
            outward(offset, part).wait_send()
        place = same_column(offset)
        back(place).wait_send()
        lane = mixed_in.at[:, lanes_of(place)]
        to_column(lane, lane, m_send.at[place], m_arrive.at[place], place).wait_recv()
    back_here().wait()


def attention_forward(joined, blocks, shards, collective_id):
    tokens = joined.shape[0]
    rows = tokens * 8
    wide = 2 * HD
    low = jnp.bfloat16
    chunks = sum(shard.size // (SLAB * LANES) for shard in shards)
    vmem = pl.BlockSpec(memory_space=pltpu.VMEM)
    any_spec = pl.BlockSpec(memory_space=pl.ANY)
    results = pl.pallas_call(
        functools.partial(forward_kernel, len(shards)),
        out_shape=[
            jax.ShapeDtypeStruct((3, rows, wide), low),
            jax.ShapeDtypeStruct((rows, wide), jnp.float32),
            jax.ShapeDtypeStruct((8, 8, 2 * TILE), jnp.float32),
            jax.ShapeDtypeStruct((tokens, HEADS * HD), low),
        ]
        + [whole_shape(shard) for shard in shards],
        in_specs=[vmem] * (3 + len(shards)),
        out_specs=[vmem] * 4 + [any_spec] * len(shards),
        scratch_shapes=[
            pltpu.VMEM((2 * TILE, rows), jnp.float32),
            pltpu.VMEM((8, TILE, wide), low),
            pltpu.SemaphoreType.DMA((8, 3)),
            pltpu.SemaphoreType.DMA((8, 3)),
            pltpu.SemaphoreType.DMA((8,)),
            pltpu.SemaphoreType.DMA((8,)),
            pltpu.SemaphoreType.DMA((max(chunks, 1), 6)),
            pltpu.SemaphoreType.DMA((max(chunks, 1), 6)),
            pltpu.SemaphoreType.DMA((max(chunks, 1),)),
        ],
        compiler_params=pltpu.CompilerParams(
            collective_id=collective_id, has_side_effects=True, vmem_limit_bytes=60 * 2**20
        ),
        name="attention_forward",
    )(joined, blocks.reshape(rows, 1), blocks.reshape(1, rows), *shards)
    wholes = [whole.reshape(-1, whole.shape[-1]) for whole in results[4:]]
    return results[0], results[1], results[2], results[3], wholes


def backward_kernel(
    grad_in, joined, mixed_ref, log_ref, row_ref, col_ref, out_ref,
    grad_ref, key_sum, value_sum, low_ref, g_send, g_arrive, o_send, o_arrive,
):
    me = lax.axis_index("ctx")
    tiles = 8
    wide = 2 * HD
    width = HEADS * HD
    greet([])

    def outward(offset):
        place = same_column(offset)
        src, dst = grad_in.at[:, lanes_of(place)], grad_ref.at[rows_of(me)]
        if offset == 0:
            return pltpu.make_async_copy(src, dst, g_arrive.at[0])
        return to_column(src, dst, g_send.at[offset], g_arrive.at[offset], place)

    for offset in range(8):
        outward(offset).start()
    key_sum[...] = jnp.zeros_like(key_sum)
    value_sum[...] = jnp.zeros_like(value_sum)

    def receive(source):
        offset = lax.rem(me + 8 - source, 8)

        @pl.when(offset == 0)
        def _():
            outward(0).wait()

        @pl.when(offset != 0)
        def _():
            dst = grad_ref.at[rows_of(source)]
            to_column(dst, dst, g_send.at[offset], g_arrive.at[offset], source).wait_recv()

    def back(tile, part):
        return to_column(
            low_ref.at[part, tile],
            out_ref.at[:, lanes_of(me, part * width)],
            o_send.at[part, tile],
            o_arrive.at[part, me],
            tile,
        )

    def back_here(part):
        return pltpu.make_async_copy(
            low_ref.at[part, me], out_ref.at[:, lanes_of(me, part * width)], o_arrive.at[part, me]
        )

    def deliver(tile, parts):
        @pl.when(tile != me)
        def _():
            for part in parts:
                back(tile, part).start()

        @pl.when(tile == me)
        def _():
            for part in parts:
                back_here(part).start()

    def finish_keys(tile):
        low_ref[1, tile] = key_sum[rows_of(tile), :].astype(jnp.bfloat16)
        low_ref[2, tile] = value_sum[rows_of(tile), :].astype(jnp.bfloat16)
        deliver(tile, (1, 2))

    def one_tile(turn, unused):
        tile = tiles - 1 - turn
        receive(tile)
        scaled = both_heads(
            (joined[0, rows_of(tile)].astype(jnp.float32) * HD**-0.5).astype(jnp.bfloat16)
        )
        grads = both_heads(grad_ref[rows_of(tile), :])
        products = grad_ref[rows_of(tile), :].astype(jnp.float32) * mixed_ref[rows_of(tile), :]
        products = jnp.transpose(products)
        delta = jnp.concatenate(
            [
                jnp.sum(products[:HD], axis=0, keepdims=True),
                jnp.sum(products[HD:], axis=0, keepdims=True),
            ],
            axis=1,
        )
        log_total = log_ref[tile, :1]
        own = col_ref[:, rows_of(tile)]
        own = jnp.concatenate([own, own], axis=1)

        def step(index, accum, masked):
            here = rows_of(index)
            keys = joined[1, here]
            scores = nt(keys, scaled)
            if masked:
                scores = jnp.where(row_ref[here, :] <= own, scores, MASKED)
            probs = jnp.exp(scores - log_total)
            value_sum[here, :] += nn(probs.astype(jnp.bfloat16), grads)
            grad_scores = (probs * (nt(joined[2, here], grads) - delta)).astype(jnp.bfloat16)
            key_sum[here, :] += nn(grad_scores, scaled)
            return accum + tn(grad_scores, keys)

        accum = jnp.zeros((2 * TILE, wide), jnp.float32)
        accum = lax.fori_loop(0, tile, lambda i, a: step(i, a, False), accum)
        stop = jnp.minimum(tile + 2, tiles)
        accum = lax.fori_loop(tile, stop, lambda i, a: step(i, a, True), accum)
        low_ref[0, tile] = (own_lanes(accum) * HD**-0.5).astype(jnp.bfloat16)
        deliver(tile, (0,))

        @pl.when(tile < tiles - 1)
        def _():
            finish_keys(tile + 1)

        return unused

    lax.fori_loop(0, tiles, one_tile, 0)
    finish_keys(jnp.int32(0))
    for offset in range(1, 8):
        outward(offset).wait_send()
        place = same_column(offset)
        for part in range(3):
            back(place, part).wait_send()
            lane = out_ref.at[:, lanes_of(place, part * width)]
            to_column(
                lane, lane, o_send.at[part, place], o_arrive.at[part, place], place
            ).wait_recv()
    for part in range(3):
        back_here(part).wait()


def attention_backward(grad_mixed, joined, mixed, log_total, blocks, collective_id):
    tokens, width = grad_mixed.shape
    rows = joined.shape[1]
    wide = 2 * HD
    low = jnp.bfloat16
    vmem = pl.BlockSpec(memory_space=pltpu.VMEM)
    return pl.pallas_call(
        backward_kernel,
        out_shape=jax.ShapeDtypeStruct((tokens, 3 * width), low),
        in_specs=[vmem] * 6,
        out_specs=vmem,
        scratch_shapes=[
            pltpu.VMEM((rows, wide), low),
            pltpu.VMEM((rows, wide), jnp.float32),
            pltpu.VMEM((rows, wide), jnp.float32),
            pltpu.VMEM((3, 8, TILE, wide), low),
            pltpu.SemaphoreType.DMA((8,)),
            pltpu.SemaphoreType.DMA((8,)),
            pltpu.SemaphoreType.DMA((3, 8)),
            pltpu.SemaphoreType.DMA((3, 8)),
        ],
        compiler_params=pltpu.CompilerParams(
            collective_id=collective_id, has_side_effects=True, vmem_limit_bytes=60 * 2**20
        ),
        name="attention_backward",
    )(grad_mixed, joined, mixed, log_total, blocks.reshape(rows, 1), blocks.reshape(1, rows))


FF_BLOCK = 512


def feed_kernel(
    inner_ref, hidden_ref, upstream_ref, gain_ref, up_ref, down_ref,
    out_ref, grad_inner_ref, gain_grad_ref, grad_up_ref, grad_down_ref,
    turned_ref, slope_ref, active_ref, lowered_ref, grad_ref,
):
    step = pl.program_id(0)
    blocks = slope_ref.shape[0]

    @pl.when(step == 0)
    def _():
        lowered_ref[...] = jnp.zeros_like(lowered_ref)
        grad_inner_ref[...] = jnp.zeros_like(grad_inner_ref)
        turned_ref[...] = jnp.transpose(inner_ref[...])

    @pl.when(step < blocks)
    def _():
        lifted = nn(inner_ref[...], up_ref[...])
        share = 0.5 + 0.5 * lax.erf(lifted * 0.5**0.5)
        slope_ref[step] = share + lifted * jnp.exp(lifted * lifted * -0.5) * (2 * math.pi) ** -0.5
        active = (lifted * share).astype(jnp.bfloat16)
        active_ref[step] = active
        lowered_ref[...] += nn(active, down_ref[...])

    @pl.when(step == blocks - 1)
    def _():
        lowered = lowered_ref[...]
        centre = lowered - jnp.mean(lowered, axis=-1, keepdims=True)
        inverse = lax.rsqrt(jnp.mean(centre * centre, axis=-1, keepdims=True) + EPS)
        unit = centre * inverse
        gain = gain_ref[...]
        out_ref[...] = (hidden_ref[...] + unit * gain).astype(jnp.bfloat16)
        upstream = upstream_ref[...].astype(jnp.float32)
        gain_grad_ref[...] = jnp.sum(upstream * unit, axis=0, keepdims=True)
        scaled = upstream * gain
        mean = jnp.mean(scaled, axis=-1, keepdims=True)
        along = jnp.mean(scaled * unit, axis=-1, keepdims=True)
        grad_ref[...] = ((scaled - mean - unit * along) * inverse).astype(jnp.bfloat16)

    @pl.when(step >= blocks)
    def _():
        block = step - blocks
        grad = grad_ref[...]
        grad_lifted = (nt(grad, down_ref[...]) * slope_ref[block]).astype(jnp.bfloat16)
        grad_up_ref[...] = nn(turned_ref[...], grad_lifted).astype(jnp.bfloat16)
        grad_down_ref[...] = tn(active_ref[block], grad).astype(jnp.bfloat16)
        grad_inner_ref[...] += nt(grad_lifted, up_ref[...])


def feed_forward(inner, hidden, upstream, gain, full_up, full_down):
    tokens, width = inner.shape
    blocks = full_up.shape[1] // FF_BLOCK
    low = jnp.bfloat16
    whole = pl.BlockSpec((tokens, width), lambda i: (0, 0))
    row = pl.BlockSpec((1, width), lambda i: (0, 0))
    at = lambda i: lax.rem(i, blocks)
    late = lambda i: jnp.maximum(i - blocks, 0)
    return pl.pallas_call(
        feed_kernel,
        grid=(2 * blocks,),
        out_shape=(
            jax.ShapeDtypeStruct((tokens, width), low),
            jax.ShapeDtypeStruct((tokens, width), jnp.float32),
            jax.ShapeDtypeStruct((1, width), jnp.float32),
            jax.ShapeDtypeStruct(full_up.shape, low),
            jax.ShapeDtypeStruct(full_down.shape, low),
        ),
        in_specs=[
            whole,
            whole,
            whole,
            row,
            pl.BlockSpec((width, FF_BLOCK), lambda i: (0, at(i))),
            pl.BlockSpec((FF_BLOCK, width), lambda i: (at(i), 0)),
        ],
        out_specs=(
            whole,
            whole,
            row,
            pl.BlockSpec((width, FF_BLOCK), lambda i: (0, late(i))),
            pl.BlockSpec((FF_BLOCK, width), lambda i: (late(i), 0)),
        ),
        scratch_shapes=[
            pltpu.VMEM((width, tokens), low),
            pltpu.VMEM((blocks, tokens, FF_BLOCK), jnp.float32),
            pltpu.VMEM((blocks, tokens, FF_BLOCK), low),
            pltpu.VMEM((tokens, width), jnp.float32),
            pltpu.VMEM((tokens, width), low),
        ],
        compiler_params=pltpu.CompilerParams(vmem_limit_bytes=60 * 2**20),
        name="feed_forward",
    )(inner, hidden, upstream, gain, full_up, full_down)


EARLY = 3


TILE = 256


def nt(left, right):
    return lax.dot_general(
        left, right, (((1,), (1,)), ((), ())), preferred_element_type=jnp.float32
    )


def nn(left, right):
    return lax.dot_general(
        left, right, (((1,), (0,)), ((), ())), preferred_element_type=jnp.float32
    )


def tn(left, right):
    return lax.dot_general(
        left, right, (((0,), (0,)), ((), ())), preferred_element_type=jnp.float32
    )


def both_heads(rows):
    lane = lax.broadcasted_iota(jnp.int32, rows.shape, 1)
    zero = jnp.zeros_like(rows)
    return jnp.concatenate(
        [jnp.where(lane < HD, rows, zero), jnp.where(lane < HD, zero, rows)], axis=0
    )


def own_lanes(pair):
    half = pair.shape[0] // 2
    lane = lax.broadcasted_iota(jnp.int32, (half, pair.shape[1]), 1)
    return jnp.where(lane < HD, pair[:half], pair[half:])


def fast_body(
    tokens_in, block_ids, w_query, w_key, w_value, w_out, w_up, w_down, norm_gain, cotangent
):
    width = tokens_in.shape[2]
    groups = lax.axis_size("ctx")
    kinds = norm_gain.shape[0]
    small = jnp.concatenate(
        [norm_gain.astype(jnp.float32).reshape(1, -1), block_ids.astype(jnp.float32).reshape(-1, 128)]
    )
    small = jnp.pad(small, ((0, 8 - small.shape[0]), (0, 0)))
    early, late = [w_out, w_up, w_down][:EARLY], [w_out, w_up, w_down][EARLY:]
    smalls, full_query, full_key, full_value, *first = gather_over_devices(
        [small, w_query, w_key, w_value] + early, 1
    )
    smalls = smalls.reshape(32, 8, 128)
    gains = smalls[:, 0].reshape(32, kinds, -1).transpose(1, 0, 2).reshape(kinds, width)
    blocks = lax.dynamic_slice_in_dim(smalls, lax.axis_index("fsdp") * groups, groups, 0)
    blocks = blocks[:, 1:3].reshape(-1).astype(jnp.int32)
    tokens = tokens_in[0].astype(jnp.float32)
    normed = layer_norm(tokens, gains[0]).astype(jnp.bfloat16)
    queries = jnp.concatenate(
        [project(normed, w).astype(jnp.bfloat16) for w in (full_query, full_key, full_value)], axis=1
    )
    joined, mixed, log_total, mixed_low, wholes = attention_forward(
        queries, blocks, late, 2
    )
    full_out, full_up, full_down = first + wholes
    branch = project(mixed_low, full_out)
    hidden = tokens + layer_norm(branch, gains[1])
    inner = layer_norm(hidden, gains[2]).astype(jnp.bfloat16)
    upstream = cotangent[0].astype(jnp.float32)
    layer_out, grad_inner, gain_four, grad_up, grad_down = feed_forward(
        inner, hidden, cotangent[0], gains[3:], full_up, full_down
    )
    layer_out, gain_four = layer_out[None], gain_four[0]
    unused_three, pull_three = jax.vjp(layer_norm, hidden, gains[2])
    grad_hidden_branch, gain_three = pull_three(grad_inner)
    grad_hidden = upstream + grad_hidden_branch
    unused_two, pull_two = jax.vjp(layer_norm, branch, gains[1])
    grad_branch, gain_two = pull_two(grad_hidden)
    grad_branch = grad_branch.astype(jnp.bfloat16)
    grad_out = outer_sum(mixed_low, grad_branch).astype(jnp.bfloat16)
    grad_mixed = back_project(grad_branch, full_out).astype(jnp.bfloat16)
    grad_qkv = attention_backward(grad_mixed, joined, mixed, log_total, blocks, 4)
    grad_three = outer_sum(normed, grad_qkv).astype(jnp.bfloat16)
    grad_normed = (
        back_project(grad_qkv[:, :width], full_query)
        + back_project(grad_qkv[:, width : 2 * width], full_key)
        + back_project(grad_qkv[:, 2 * width :], full_value)
    )
    unused_one, pull_one = jax.vjp(layer_norm, tokens, gains[0])
    grad_norm_in, gain_one = pull_one(grad_normed)
    grad_tokens = (grad_hidden + grad_norm_in).astype(jnp.bfloat16)[None]
    gain_grads = jnp.stack([gain_one, gain_two, gain_three, gain_four])
    sums, gain_sum = sum_over_devices(
        [grad_three, grad_out, grad_up, grad_down], by_owner(gain_grads), 3
    )
    return (
        layer_out,
        grad_tokens,
        sums[0],
        sums[1],
        sums[2],
        sums[3],
        sums[4:8].transpose(1, 0, 2).reshape(w_up.shape),
        sums[8:].reshape(w_down.shape),
        gain_sum[0].reshape(norm_gain.shape),
    )


def by_owner(gain_grads):
    kinds, width = gain_grads.shape
    rows = gain_grads.reshape(kinds, 32, width // 32).transpose(1, 0, 2).reshape(32, 1, -1)
    return jnp.pad(rows, ((0, 0), (0, 7), (0, 0))).reshape(2, 2, 4, 2, 8, rows.shape[-1])


def pick(mesh):
    return fast_body if mesh.shape["ctx"] * 2 == HEADS else body


def solution(mesh):
    placed = (
        P("fsdp", "ctx", None),
        P("fsdp", "ctx"),
        P(("fsdp", "ctx"), None),
        P(("fsdp", "ctx"), None),
        P(("fsdp", "ctx"), None),
        P(("fsdp", "ctx"), None),
        P(("fsdp", "ctx"), None),
        P(("fsdp", "ctx"), None),
        P(None, ("fsdp", "ctx")),
        P("fsdp", "ctx", None),
    )
    return jax.shard_map(
        pick(mesh),
        mesh=mesh,
        in_specs=placed,
        out_specs=(
            P("fsdp", "ctx", None),
            P("fsdp", "ctx", None),
            P(("fsdp", "ctx"), None),
            P(("fsdp", "ctx"), None),
            P(("fsdp", "ctx"), None),
            P(("fsdp", "ctx"), None),
            P(("fsdp", "ctx"), None),
            P(("fsdp", "ctx"), None),
            P(None, ("fsdp", "ctx")),
        ),
        check_vma=False,
    )
```

```python
import functools
import math

import jax
import jax.numpy as jnp
from jax import lax
from jax.experimental import pallas as pl
from jax.experimental.pallas import tpu as pltpu
from jax.sharding import PartitionSpec as P

HEADS = 16
HD = 64


EPS = 1e-05
MASKED = -1e30


def from_behind(block, axis, distance):
    devices = range(lax.axis_size(axis))
    route = [((i - distance) % len(devices), i) for i in devices]
    return lax.ppermute(block, axis, route)


def layer_norm(values, gain):
    centre = values - jnp.mean(values, axis=-1, keepdims=True)
    spread = jnp.mean(centre * centre, axis=-1, keepdims=True)
    return centre * lax.rsqrt(spread + EPS) * gain


def gelu_exact(values):
    return jax.nn.gelu(values, approximate=False)


def project(left, right):
    return jnp.dot(left, right, preferred_element_type=jnp.float32)


def outer_sum(left, right):
    return lax.dot_general(
        left, right, (((0,), (0,)), ((), ())), preferred_element_type=jnp.float32
    )


def back_project(grad, weight):
    return lax.dot_general(
        grad, weight, (((1,), (1,)), ((), ())), preferred_element_type=jnp.float32
    )


def split_heads(values):
    return values.reshape(values.shape[0], HEADS, HD)


def attend(carry, head_queries, query_blocks, key_rows, key_blocks, scale):
    best, total, accum = carry
    width = key_rows.shape[1] // 2
    keys = split_heads(key_rows[:, :width])
    values = split_heads(key_rows[:, width:])
    scores = (
        jnp.einsum("qhd,khd->hqk", head_queries, keys, preferred_element_type=jnp.float32) * scale
    )
    allowed = key_blocks[None, None, :] <= query_blocks[None, :, None]
    scores = jnp.where(allowed, scores, MASKED)
    newest = jnp.maximum(best, jnp.max(scores, axis=2))
    weights = jnp.where(allowed, jnp.exp(scores - newest[:, :, None]), 0.0)
    factor = jnp.exp(best - newest)
    total = total * factor + jnp.sum(weights, axis=2)
    update = jnp.einsum(
        "hqk,khd->qhd", weights.astype(jnp.bfloat16), values, preferred_element_type=jnp.float32
    )
    accum = accum * jnp.transpose(factor)[:, :, None] + update
    return (newest, total, accum)


def score_grads(
    head_queries, head_grads, log_total, delta, query_blocks, key_rows, key_blocks, scale
):
    width = key_rows.shape[1] // 2
    rows = key_rows.shape[0]
    query_rows = head_queries.shape[0]
    keys = split_heads(key_rows[:, :width])
    values = split_heads(key_rows[:, width:])
    scores = (
        jnp.einsum("qhd,khd->hqk", head_queries, keys, preferred_element_type=jnp.float32) * scale
    )
    allowed = key_blocks[None, None, :] <= query_blocks[None, :, None]
    probs = jnp.where(
        allowed, jnp.exp(jnp.where(allowed, scores, MASKED) - log_total[:, :, None]), 0.0
    )
    grad_values = jnp.einsum(
        "hqk,qhd->khd", probs.astype(jnp.bfloat16), head_grads, preferred_element_type=jnp.float32
    )
    grad_probs = jnp.einsum("qhd,khd->hqk", head_grads, values, preferred_element_type=jnp.float32)
    grad_scores = (probs * (grad_probs - delta[:, :, None])).astype(jnp.bfloat16)
    grad_queries = (
        jnp.einsum("hqk,khd->qhd", grad_scores, keys, preferred_element_type=jnp.float32) * scale
    )
    grad_keys = (
        jnp.einsum("hqk,qhd->khd", grad_scores, head_queries, preferred_element_type=jnp.float32)
        * scale
    )
    joined = jnp.concatenate(
        [grad_keys.reshape(rows, width), grad_values.reshape(rows, width)], axis=1
    )
    return (grad_queries.reshape(query_rows, width), joined)


def guarded(head_queries, head_grads, log_total, delta, query_blocks, key_rows, key_blocks, scale):
    live = jnp.min(key_blocks) <= jnp.max(query_blocks)
    rows, columns = key_rows.shape

    def run(unused):
        return score_grads(
            head_queries, head_grads, log_total, delta, query_blocks, key_rows, key_blocks, scale
        )

    def skip(unused):
        return (
            jnp.zeros((head_queries.shape[0], columns // 2), jnp.float32),
            jnp.zeros((rows, columns), jnp.float32),
        )

    return lax.cond(live, run, skip, 0)


def body(tokens_in, block_ids, w_query, w_key, w_value, w_out, w_up, w_down, norm_gain, cotangent):
    scale = 1.0 / math.sqrt(HD)
    stride = tokens_in.shape[1]
    width = tokens_in.shape[2]
    cycle_size = lax.axis_size("ctx")
    place = lax.axis_index("ctx")
    shards = (w_query, w_key, w_value, w_out, w_up, w_down, norm_gain)
    gathered = (
        lax.all_gather(w_query, ("fsdp", "ctx"), axis=0, tiled=True),
        lax.all_gather(w_key, ("fsdp", "ctx"), axis=0, tiled=True),
        lax.all_gather(w_value, ("fsdp", "ctx"), axis=0, tiled=True),
        lax.all_gather(w_out, ("fsdp", "ctx"), axis=0, tiled=True),
        lax.all_gather(w_up, ("fsdp", "ctx"), axis=0, tiled=True),
        lax.all_gather(w_down, ("fsdp", "ctx"), axis=0, tiled=True),
        lax.all_gather(norm_gain, ("fsdp", "ctx"), axis=1, tiled=True),
    )
    full_query, full_key, full_value, full_out, full_up, full_down, full_gain = gathered
    gains = full_gain.astype(jnp.float32)
    sequence_blocks = lax.all_gather(block_ids, "ctx", axis=1, tiled=True)[0]
    own_blocks = block_ids[0]
    top_block = jnp.max(own_blocks)
    tokens = tokens_in[0].astype(jnp.float32)
    normed = layer_norm(tokens, gains[0]).astype(jnp.bfloat16)
    queries = project(normed, full_query).astype(jnp.bfloat16)
    key_value = jnp.concatenate(
        [project(normed, full_key), project(normed, full_value)], axis=1
    ).astype(jnp.bfloat16)
    head_queries = split_heads(queries)
    start_state = (
        jnp.full((HEADS, stride), MASKED, jnp.float32),
        jnp.zeros((HEADS, stride), jnp.float32),
        jnp.zeros((stride, HEADS, HD), jnp.float32),
    )
    piece = lax.all_gather(key_value, "ctx", axis=0, tiled=True)
    rows = piece.shape[0]
    size = math.gcd(rows, stride)

    def visit(index, state):
        key_rows = lax.dynamic_slice_in_dim(piece, index * size, size, 0)
        key_blocks = lax.dynamic_slice_in_dim(sequence_blocks, index * size, size, 0)
        return lax.cond(
            jnp.min(key_blocks) <= top_block,
            lambda inner: attend(inner, head_queries, own_blocks, key_rows, key_blocks, scale),
            lambda inner: inner,
            state,
        )

    best, total, accum = lax.fori_loop(0, rows // size, visit, start_state)
    mixed = accum / jnp.transpose(total)[:, :, None]
    log_total = best + jnp.log(total)
    mixed_low = mixed.reshape(stride, width).astype(jnp.bfloat16)
    branch = project(mixed_low, full_out)
    hidden = tokens + layer_norm(branch, gains[1])
    inner = layer_norm(hidden, gains[2]).astype(jnp.bfloat16)
    lifted = project(inner, full_up)
    active = gelu_exact(lifted).astype(jnp.bfloat16)
    lowered = project(active, full_down)
    layer_out = (hidden + layer_norm(lowered, gains[3])).astype(jnp.bfloat16)[None]
    regathered = (
        lax.all_gather(shards[0], ("fsdp", "ctx"), axis=0, tiled=True),
        lax.all_gather(shards[1], ("fsdp", "ctx"), axis=0, tiled=True),
        lax.all_gather(shards[2], ("fsdp", "ctx"), axis=0, tiled=True),
        lax.all_gather(shards[3], ("fsdp", "ctx"), axis=0, tiled=True),
        lax.all_gather(shards[4], ("fsdp", "ctx"), axis=0, tiled=True),
        lax.all_gather(shards[5], ("fsdp", "ctx"), axis=0, tiled=True),
        lax.all_gather(shards[6], ("fsdp", "ctx"), axis=1, tiled=True),
    )
    back_query, back_key, back_value, back_out, back_up, back_down, back_gain = regathered
    back_gains = back_gain.astype(jnp.float32)
    upstream = cotangent[0].astype(jnp.float32)
    unused_four, pull_four = jax.vjp(layer_norm, lowered, back_gains[3])
    grad_lowered, gain_four = pull_four(upstream)
    grad_lowered = grad_lowered.astype(jnp.bfloat16)
    grad_down = outer_sum(active, grad_lowered)
    grad_active = back_project(grad_lowered, back_down)
    unused_gelu, pull_gelu = jax.vjp(gelu_exact, lifted)
    grad_lifted = pull_gelu(grad_active)[0].astype(jnp.bfloat16)
    grad_up = outer_sum(inner, grad_lifted)
    grad_inner = back_project(grad_lifted, back_up)
    unused_three, pull_three = jax.vjp(layer_norm, hidden, back_gains[2])
    grad_hidden_branch, gain_three = pull_three(grad_inner)
    grad_hidden = upstream + grad_hidden_branch
    unused_two, pull_two = jax.vjp(layer_norm, branch, back_gains[1])
    grad_branch, gain_two = pull_two(grad_hidden)
    grad_branch = grad_branch.astype(jnp.bfloat16)
    grad_out = outer_sum(mixed_low, grad_branch)
    grad_mixed = back_project(grad_branch, back_out).astype(jnp.bfloat16)
    head_grads = split_heads(grad_mixed)
    delta = jnp.transpose(jnp.sum(head_grads.astype(jnp.float32) * mixed, axis=2))
    query_grad, kv_grad = guarded(
        head_queries, head_grads, log_total, delta, own_blocks, key_value, own_blocks, scale
    )

    def pass_grads(values):
        return from_behind(values.astype(jnp.bfloat16), "ctx", 1).astype(values.dtype)

    def cycle_keys(step, state):
        travel, kv_accum, query_accum = state
        travel = from_behind(travel, "ctx", 1)
        kv_accum = pass_grads(kv_accum)
        source = (place - step) % cycle_size
        key_blocks = lax.dynamic_slice_in_dim(sequence_blocks, source * stride, stride, 0)
        part_query, part_kv = guarded(
            head_queries, head_grads, log_total, delta, own_blocks, travel, key_blocks, scale
        )
        return (travel, kv_accum + part_kv, query_accum + part_query)

    unused_travel, kv_accum, query_grad = lax.fori_loop(
        1, cycle_size, cycle_keys, (key_value, kv_grad, query_grad)
    )
    kv_grad = pass_grads(kv_accum)
    query_low = query_grad.astype(jnp.bfloat16)
    kv_low = kv_grad.astype(jnp.bfloat16)
    key_low = kv_low[:, :width]
    value_low = kv_low[:, width:]
    grad_query = outer_sum(normed, query_low)
    grad_key = outer_sum(normed, key_low)
    grad_value = outer_sum(normed, value_low)
    grad_normed = (
        back_project(query_low, back_query)
        + back_project(key_low, back_key)
        + back_project(value_low, back_value)
    )
    unused_one, pull_one = jax.vjp(layer_norm, tokens, back_gains[0])
    grad_norm_in, gain_one = pull_one(grad_normed)
    grad_tokens = (grad_hidden + grad_norm_in).astype(jnp.bfloat16)[None]
    gain_grads = jnp.stack([gain_one, gain_two, gain_three, gain_four])
    summed = (
        lax.psum_scatter(grad_query, ("fsdp", "ctx"), scatter_dimension=0, tiled=True),
        lax.psum_scatter(grad_key, ("fsdp", "ctx"), scatter_dimension=0, tiled=True),
        lax.psum_scatter(grad_value, ("fsdp", "ctx"), scatter_dimension=0, tiled=True),
        lax.psum_scatter(grad_out, ("fsdp", "ctx"), scatter_dimension=0, tiled=True),
        lax.psum_scatter(grad_up, ("fsdp", "ctx"), scatter_dimension=0, tiled=True),
        lax.psum_scatter(grad_down, ("fsdp", "ctx"), scatter_dimension=0, tiled=True),
        lax.psum_scatter(gain_grads, ("fsdp", "ctx"), scatter_dimension=1, tiled=True),
    )
    return (
        layer_out,
        grad_tokens,
        summed[0],
        summed[1],
        summed[2],
        summed[3],
        summed[4],
        summed[5],
        summed[6],
    )


MESH = pl.DeviceIdType.MESH
SLAB = 16
LANES = 1024
SUM_LAG = 2


def places():
    fsdp, ctx = lax.axis_index("fsdp"), lax.axis_index("ctx")
    return lax.div(fsdp, 2), lax.rem(fsdp, 2), lax.div(ctx, 2), lax.rem(ctx, 2)


def at_place(y, core, z, x):
    return (y * 2 + core, z * 2 + x)


def meet(devices):
    barrier = pltpu.get_barrier_semaphore()
    for device in devices:
        pl.semaphore_signal(barrier, inc=1, device_id=device, device_id_type=MESH)
    pl.semaphore_wait(barrier, len(devices))


def sum_kernel(views, lines, *refs):
    grads, gain_ref = refs[:lines], refs[lines]
    out_ref, gain_out, own, zero, first_x, first_y, second, third = refs[lines + 1 : lines + 9]
    g_own, g_zero, g_first, g_second, g_third, load, send, arrive = refs[lines + 9 :]
    y, core, z, x = places()
    partner = at_place(y, 1 - core, z, x)
    beside = at_place(y, core, z, 1 - x)
    across = at_place(1 - y, core, z, x)
    rank = [lax.rem(z + d, 4) for d in (1, 2, 3)]
    others = [at_place(y, core, r, x) for r in rank]
    meet([partner, beside, across] + others)
    count = len(views) + 1
    last = len(views)

    def pick(k, side):
        if k == last:
            return gain_ref.at[:, side]
        ref, part = views[k]
        return grads[ref].at[(slice(None), side, slice(None), slice(None)) + part]

    def remote(src, dst, k, phase, device):
        return pltpu.make_async_remote_copy(
            src_ref=src,
            dst_ref=dst,
            send_sem=send.at[k, phase],
            recv_sem=arrive.at[k, phase],
            device_id=device,
            device_id_type=MESH,
        )

    def add(total, landed, pairs, rows):
        def one(i, unused):
            into, out_of = pairs(i)
            total[into] = total[into] + landed[out_of]
            return unused

        lax.fori_loop(0, rows, one, 0)

    def steps(k):
        if k == last:
            return g_own, g_zero, g_first, g_second, g_third
        return own.at[k], zero.at[k], (first_y if k % 2 else first_x).at[k // 2], second.at[k], third.at[k]

    def phase_zero(k):
        return remote(pick(k, 1 - core), steps(k)[1], k, 0, partner)

    def loading(k):
        return pltpu.make_async_copy(pick(k, core), steps(k)[0], load.at[k])

    def phase_one(k):
        total = steps(k)[0]
        if k % 2:
            return remote(total.at[1 - y], steps(k)[2], k, 1, across)
        return remote(total.at[:, :, 1 - x], steps(k)[2], k, 1, beside)

    def phase_two(k):
        total = steps(k)[0]
        if k % 2:
            return remote(total.at[y, :, 1 - x], steps(k)[3], k, 2, beside)
        return remote(total.at[1 - y, :, x], steps(k)[3], k, 2, across)

    def phase_three(k):
        total = steps(k)[0]
        return [
            remote(total.at[y, r, x], steps(k)[4].at[2 - d], k, 3 + d, others[d])
            for d, r in enumerate(rank)
        ]

    def after_zero(k):
        loading(k).wait()
        phase_zero(k).wait()
        total, landed = steps(k)[:2]
        split = lambda i: (lax.div(i, 8), lax.rem(lax.div(i, 2), 4), lax.rem(i, 2))
        add(total, landed, lambda i: (split(i), split(i)), 16)
        phase_one(k).start()

    def after_one(k):
        phase_one(k).wait()
        total, landed = steps(k)[0], steps(k)[2]
        if k % 2:
            add(total, landed, lambda i: ((y, lax.div(i, 2), lax.rem(i, 2)), (lax.div(i, 2), lax.rem(i, 2))), 8)
        else:
            add(total, landed, lambda i: ((lax.div(i, 4), lax.rem(i, 4), x), (lax.div(i, 4), lax.rem(i, 4))), 8)
        phase_two(k).start()

    def after_two(k):
        phase_two(k).wait()
        total, landed = steps(k)[0], steps(k)[3]
        add(total, landed, lambda i: ((y, i, x), (i,)), 4)
        for copy in phase_three(k):
            copy.start()

    def after_three(k):
        for copy in phase_three(k):
            copy.wait()
        total, landed = steps(k)[0], steps(k)[4]
        value = total[y, z, x].astype(jnp.float32)
        for d in range(3):
            value = value + landed[d].astype(jnp.float32)
        if k == last:
            gain_out[...] = value
        else:
            out_ref[k] = value

    for k in range(count):
        loading(k).start()
        phase_zero(k).start()
    for step in range(count + 3 * SUM_LAG):
        for stage, run in enumerate((after_zero, after_one, after_two, after_three)):
            if 0 <= step - SUM_LAG * stage < count:
                run(step - SUM_LAG * stage)


def sum_over_devices(grads, gain, collective_id):
    shaped, views = [], []
    for ref, grad in enumerate(grads):
        rows, columns = grad.shape
        parts = rows // (32 * SLAB)
        shaped.append(grad.reshape(2, 2, 4, 2, parts, SLAB, columns))
        views += [
            (ref, (part, slice(None), pl.ds(left, LANES)))
            for left in range(0, columns, LANES)
            for part in range(parts)
        ]
    count = len(views)
    low = jnp.bfloat16
    slab = (SLAB, LANES)
    any_spec = pl.BlockSpec(memory_space=pl.ANY)
    out, gain_out = pl.pallas_call(
        functools.partial(sum_kernel, views, len(grads)),
        out_shape=(
            jax.ShapeDtypeStruct((count,) + slab, jnp.float32),
            jax.ShapeDtypeStruct((8, 128), jnp.float32),
        ),
        in_specs=[any_spec] * (len(grads) + 1),
        out_specs=(pl.BlockSpec(memory_space=pltpu.VMEM), pl.BlockSpec(memory_space=pltpu.VMEM)),
        scratch_shapes=[
            pltpu.VMEM((count, 2, 4, 2) + slab, low),
            pltpu.VMEM((count, 2, 4, 2) + slab, low),
            pltpu.VMEM(((count + 1) // 2, 2, 4) + slab, low),
            pltpu.VMEM(((count + 1) // 2, 4, 2) + slab, low),
            pltpu.VMEM((count, 4) + slab, low),
            pltpu.VMEM((count, 3) + slab, low),
            pltpu.VMEM((2, 4, 2, 8, 128), jnp.float32),
            pltpu.VMEM((2, 4, 2, 8, 128), jnp.float32),
            pltpu.VMEM(((4, 2) if count % 2 else (2, 4)) + (8, 128), jnp.float32),
            pltpu.VMEM((4, 8, 128), jnp.float32),
            pltpu.VMEM((3, 8, 128), jnp.float32),
            pltpu.SemaphoreType.DMA((count + 1,)),
            pltpu.SemaphoreType.DMA((count + 1, 6)),
            pltpu.SemaphoreType.DMA((count + 1, 6)),
        ],
        compiler_params=pltpu.CompilerParams(
            collective_id=collective_id, has_side_effects=True, vmem_limit_bytes=60 * 2**20
        ),
        name="sum_over_devices",
    )(*shaped, gain)
    return out, gain_out


WINDOW = 8
LAG = 2
ORDERS = ("zxy", "zyx")


def gather_schedule(chunks, send, arrive, keep):
    here = dict(zip(("y", "core", "z", "x"), places()))
    count = len(chunks)
    slots = {"x": 0, "y": 1, "core": 2, "z": 3}

    def copies(k, stage):
        own, whole = chunks[k]
        order = tuple(ORDERS[k % len(ORDERS)]) + ("core",)
        axis, done = order[stage], order[:stage]
        part = whole(*(slice(None) if a in done else here[a] for a in here))
        made = []
        for distance in range(1, 4 if axis == "z" else 2):
            there = dict(here)
            there[axis] = lax.rem(here[axis] + distance, 4 if axis == "z" else 2)
            made.append(
                pltpu.make_async_remote_copy(
                    src_ref=part if stage else own,
                    dst_ref=part,
                    send_sem=send.at[k, slots[axis] + distance - 1],
                    recv_sem=arrive.at[k, slots[axis] + distance - 1],
                    device_id=at_place(*there.values()),
                    device_id_type=MESH,
                )
            )
        return made

    def keeping(k):
        own, whole = chunks[k]
        return pltpu.make_async_copy(own, whole(*here.values()), keep.at[k])

    def enter(k):
        keeping(k).start()
        for copy in copies(k, 0):
            copy.start()

    def begin():
        for k in range(min(WINDOW, count)):
            enter(k)

    def after(k, stage):
        if stage == 0:
            if k + WINDOW < count:
                enter(k + WINDOW)
            keeping(k).wait()
        for copy in copies(k, stage):
            copy.wait()
        if stage < 3:
            for copy in copies(k, stage + 1):
                copy.start()

    steps = [begin]
    for step in range(count + 3 * LAG):
        for stage in range(4):
            if 0 <= step - LAG * stage < count:
                steps.append(functools.partial(after, step - LAG * stage, stage))
    return steps


def weight_chunks(shards, wholes):
    chunks = []
    for own, whole in zip(shards, wholes):
        rows, columns = own.shape
        if len(whole.shape) < 7:
            chunks.append((own, lambda *p, w=whole: w.at[p]))
            continue
        for left in range(0, columns, LANES):
            for part in range(rows // SLAB):
                lanes = pl.ds(left, LANES)
                chunks.append(
                    (
                        own.at[pl.ds(part * SLAB, SLAB), lanes],
                        lambda *p, w=whole, n=(part, slice(None), lanes): w.at[p + n],
                    )
                )
    return chunks


def whole_shape(shard):
    rows, columns = shard.shape
    if rows % SLAB == 0:
        return jax.ShapeDtypeStruct((2, 2, 4, 2, rows // SLAB, SLAB, columns), shard.dtype)
    return jax.ShapeDtypeStruct((2, 2, 4, 2, rows, columns), shard.dtype)


def gather_kernel(count, *refs):
    shards, wholes = refs[:count], refs[count : 2 * count]
    send, arrive, keep = refs[2 * count :]
    y, core, z, x = places()
    meet(
        [at_place(y, 1 - core, z, x), at_place(y, core, z, 1 - x), at_place(1 - y, core, z, x)]
        + [at_place(y, core, lax.rem(z + d, 4), x) for d in (1, 2, 3)]
    )
    for step in gather_schedule(weight_chunks(shards, wholes), send, arrive, keep):
        step()


def gather_over_devices(shards, collective_id):
    shapes = [whole_shape(shard) for shard in shards]
    count = sum(max(1, shard.size // (SLAB * LANES)) for shard in shards)
    any_spec = pl.BlockSpec(memory_space=pl.ANY)
    wholes = pl.pallas_call(
        functools.partial(gather_kernel, len(shards)),
        out_shape=shapes,
        in_specs=[pl.BlockSpec(memory_space=pltpu.VMEM)] * len(shards),
        out_specs=[any_spec] * len(shards),
        scratch_shapes=[
            pltpu.SemaphoreType.DMA((count, 6)),
            pltpu.SemaphoreType.DMA((count, 6)),
            pltpu.SemaphoreType.DMA((count,)),
        ],
        compiler_params=pltpu.CompilerParams(
            collective_id=collective_id, has_side_effects=True, vmem_limit_bytes=60 * 2**20
        ),
        name="gather_over_devices",
    )(*shards)
    return [whole.reshape(-1, whole.shape[-1]) for whole in wholes]


SEND_ORDER = (1, 2, 3, 4, 5, 6, 7, 0)
def same_column(offset):
    return lax.rem(lax.axis_index("ctx") + offset, lax.axis_size("ctx"))


def greet():
    meet([(lax.axis_index("fsdp"), same_column(o)) for o in range(1, 8)])


def to_column(src, dst, send, arrive, place):
    return pltpu.make_async_remote_copy(
        src_ref=src,
        dst_ref=dst,
        send_sem=send,
        recv_sem=arrive,
        device_id=(lax.axis_index("fsdp"), place),
        device_id_type=MESH,
    )


def rows_of(index):
    return pl.ds(pl.multiple_of(index * TILE, TILE), TILE)


def lanes_of(index, start=0):
    return pl.ds(pl.multiple_of(start + index * 2 * HD, 2 * HD), 2 * HD)


def forward_kernel(
    joined_in, row_ref, col_ref, joined, mixed_ref, log_ref, mixed_in,
    score_ref, low_ref, q_send, q_arrive, m_send, m_arrive,
):
    me = lax.axis_index("ctx")
    tiles = 8
    wide = 2 * HD
    width = HEADS * HD
    greet()

    def outward(offset, part):
        place = same_column(offset)
        src = joined_in.at[:, lanes_of(place, part * width)]
        dst = joined.at[part, rows_of(me)]
        if offset == 0:
            return pltpu.make_async_copy(src, dst, q_arrive.at[0, part])
        return to_column(src, dst, q_send.at[offset, part], q_arrive.at[offset, part], place)

    for offset in SEND_ORDER:
        for part in range(3):
            outward(offset, part).start()
    def receive(source, parts):
        offset = lax.rem(me + 8 - source, 8)
        for part in parts:
            dst = joined.at[part, rows_of(source)]

            @pl.when(offset == 0)
            def _():
                outward(0, part).wait()

            @pl.when(offset != 0)
            def _():
                to_column(
                    dst, dst, q_send.at[offset, part], q_arrive.at[offset, part], source
                ).wait_recv()

    def back(tile):
        return to_column(
            low_ref.at[tile], mixed_in.at[:, lanes_of(me)], m_send.at[tile], m_arrive.at[me], tile
        )

    def back_here():
        return pltpu.make_async_copy(
            low_ref.at[me], mixed_in.at[:, lanes_of(me)], m_arrive.at[me]
        )

    receive(jnp.int32(0), (0, 1, 2))

    def one_tile(tile, unused):
        @pl.when(tile < tiles - 1)
        def _():
            receive(tile + 1, (0, 1, 2))

        scaled = both_heads(
            (joined[0, rows_of(tile)].astype(jnp.float32) * HD**-0.5).astype(jnp.bfloat16)
        )
        own = row_ref[rows_of(tile), :]
        own = jnp.concatenate([own, own], axis=0)

        def score(index, best, masked):
            here = rows_of(index)
            part = nt(scaled, joined[1, here])
            if masked:
                part = jnp.where(col_ref[:, here] <= own, part, MASKED)
            score_ref[:, here] = part
            for lane in range(0, TILE, wide):
                best = jnp.maximum(best, part[:, lane : lane + wide])
            return best

        best = jnp.full((2 * TILE, wide), MASKED, jnp.float32)
        best = lax.fori_loop(0, tile, lambda i, b: score(i, b, False), best)
        stop = jnp.minimum(tile + 2, tiles)
        best = lax.fori_loop(tile, stop, lambda i, b: score(i, b, True), best)
        best = jnp.max(best, axis=1, keepdims=True)

        def weigh(index, carry):
            total, accum = carry
            here = rows_of(index)
            weights = jnp.exp(score_ref[:, here] - best)
            for lane in range(0, TILE, wide):
                total = total + weights[:, lane : lane + wide]
            return (total, accum + nn(weights.astype(jnp.bfloat16), joined[2, here]))

        zero = jnp.zeros((2 * TILE, wide), jnp.float32)
        total, accum = lax.fori_loop(0, stop, weigh, (zero, zero))
        total = jnp.sum(total, axis=1, keepdims=True)
        mixed = own_lanes(accum / total)
        mixed_ref[rows_of(tile), :] = mixed
        low_ref[tile] = mixed.astype(jnp.bfloat16)
        log_total = jnp.broadcast_to(best + jnp.log(total), (2 * TILE, wide))
        log_ref[tile] = jnp.transpose(log_total)[:8]

        @pl.when(tile != me)
        def _():
            back(tile).start()

        @pl.when(tile == me)
        def _():
            back_here().start()

        return unused

    lax.fori_loop(0, tiles, one_tile, 0)
    for offset in range(1, 8):
        for part in range(3):
            outward(offset, part).wait_send()
        place = same_column(offset)
        back(place).wait_send()
        lane = mixed_in.at[:, lanes_of(place)]
        to_column(lane, lane, m_send.at[place], m_arrive.at[place], place).wait_recv()
    back_here().wait()


def attention_forward(joined, blocks, collective_id):
    tokens = joined.shape[0]
    rows = tokens * 8
    wide = 2 * HD
    low = jnp.bfloat16
    vmem = pl.BlockSpec(memory_space=pltpu.VMEM)
    return pl.pallas_call(
        forward_kernel,
        out_shape=[
            jax.ShapeDtypeStruct((3, rows, wide), low),
            jax.ShapeDtypeStruct((rows, wide), jnp.float32),
            jax.ShapeDtypeStruct((8, 8, 2 * TILE), jnp.float32),
            jax.ShapeDtypeStruct((tokens, HEADS * HD), low),
        ],
        in_specs=[vmem] * 3,
        out_specs=[vmem] * 4,
        scratch_shapes=[
            pltpu.VMEM((2 * TILE, rows), jnp.float32),
            pltpu.VMEM((8, TILE, wide), low),
            pltpu.SemaphoreType.DMA((8, 3)),
            pltpu.SemaphoreType.DMA((8, 3)),
            pltpu.SemaphoreType.DMA((8,)),
            pltpu.SemaphoreType.DMA((8,)),
        ],
        compiler_params=pltpu.CompilerParams(
            collective_id=collective_id, has_side_effects=True, vmem_limit_bytes=60 * 2**20
        ),
        name="attention_forward",
    )(joined, blocks.reshape(rows, 1), blocks.reshape(1, rows))


def backward_kernel(
    grad_in, joined, mixed_ref, log_ref, row_ref, col_ref, out_ref,
    grad_ref, scaled_ref, pair_ref, delta_ref, query_sum, low_ref, g_send, g_arrive, o_send, o_arrive,
):
    me = lax.axis_index("ctx")
    tiles = 8
    wide = 2 * HD
    width = HEADS * HD
    greet()

    def outward(offset):
        place = same_column(offset)
        src, dst = grad_in.at[:, lanes_of(place)], grad_ref.at[rows_of(me)]
        if offset == 0:
            return pltpu.make_async_copy(src, dst, g_arrive.at[0])
        return to_column(src, dst, g_send.at[offset], g_arrive.at[offset], place)

    for offset in range(8):
        outward(offset).start()
    query_sum[...] = jnp.zeros_like(query_sum)

    def receive(source):
        offset = lax.rem(me + 8 - source, 8)

        @pl.when(offset == 0)
        def _():
            outward(0).wait()

        @pl.when(offset != 0)
        def _():
            dst = grad_ref.at[rows_of(source)]
            to_column(dst, dst, g_send.at[offset], g_arrive.at[offset], source).wait_recv()

    def back(tile, part):
        return to_column(
            low_ref.at[part, tile],
            out_ref.at[:, lanes_of(me, part * width)],
            o_send.at[part, tile],
            o_arrive.at[part, me],
            tile,
        )

    def back_here(part):
        return pltpu.make_async_copy(
            low_ref.at[part, me], out_ref.at[:, lanes_of(me, part * width)], o_arrive.at[part, me]
        )

    def deliver(tile, parts):
        @pl.when(tile != me)
        def _():
            for part in parts:
                back(tile, part).start()

        @pl.when(tile == me)
        def _():
            for part in parts:
                back_here(part).start()

    def prepare(turn, unused):
        tile = lax.rem(me + turn, tiles)
        receive(tile)
        scaled_ref[tile] = both_heads(
            (joined[0, rows_of(tile)].astype(jnp.float32) * HD**-0.5).astype(jnp.bfloat16)
        )
        pair_ref[tile] = both_heads(grad_ref[rows_of(tile), :])
        products = grad_ref[rows_of(tile), :].astype(jnp.float32) * mixed_ref[rows_of(tile), :]
        products = jnp.transpose(products)
        delta_ref[tile] = jnp.concatenate(
            [
                jnp.sum(products[:HD], axis=0, keepdims=True),
                jnp.sum(products[HD:], axis=0, keepdims=True),
            ],
            axis=1,
        )
        return unused

    lax.fori_loop(0, tiles, prepare, 0)

    def one_tile(turn, unused):
        tile = lax.rem(me + turn, tiles)
        keys, values = joined[1, rows_of(tile)], joined[2, rows_of(tile)]
        ids = row_ref[rows_of(tile), :]

        def step(index, sums, masked):
            key_sum, value_sum = sums
            scaled, pair = scaled_ref[index], pair_ref[index]
            scores = nt(keys, scaled)
            if masked:
                own = col_ref[:, rows_of(index)]
                own = jnp.concatenate([own, own], axis=1)
                scores = jnp.where(ids <= own, scores, MASKED)
            probs = jnp.exp(scores - log_ref[index, :1])
            value_sum = value_sum + nn(probs.astype(jnp.bfloat16), pair)
            grad_scores = (probs * (nt(values, pair) - delta_ref[index])).astype(jnp.bfloat16)
            query_sum[index] += tn(grad_scores, keys)
            return (key_sum + nn(grad_scores, scaled), value_sum)

        zero = jnp.zeros((TILE, wide), jnp.float32)
        first = jnp.maximum(tile - 1, 0)
        sums = lax.fori_loop(first, tile + 1, lambda i, s: step(i, s, True), (zero, zero))
        sums = lax.fori_loop(tile + 1, tiles, lambda i, s: step(i, s, False), sums)
        low_ref[1, tile] = sums[0].astype(jnp.bfloat16)
        low_ref[2, tile] = sums[1].astype(jnp.bfloat16)
        deliver(tile, (1, 2))
        return unused

    lax.fori_loop(0, tiles, one_tile, 0)

    def finish(turn, unused):
        tile = lax.rem(me + turn, tiles)
        low_ref[0, tile] = (own_lanes(query_sum[tile]) * HD**-0.5).astype(jnp.bfloat16)
        deliver(tile, (0,))
        return unused

    lax.fori_loop(0, tiles, finish, 0)
    for offset in range(1, 8):
        outward(offset).wait_send()
        place = same_column(offset)
        for part in range(3):
            back(place, part).wait_send()
            lane = out_ref.at[:, lanes_of(place, part * width)]
            to_column(
                lane, lane, o_send.at[part, place], o_arrive.at[part, place], place
            ).wait_recv()
    for part in range(3):
        back_here(part).wait()


def attention_backward(grad_mixed, joined, mixed, log_total, blocks, collective_id):
    tokens, width = grad_mixed.shape
    rows = joined.shape[1]
    wide = 2 * HD
    low = jnp.bfloat16
    vmem = pl.BlockSpec(memory_space=pltpu.VMEM)
    return pl.pallas_call(
        backward_kernel,
        out_shape=jax.ShapeDtypeStruct((tokens, 3 * width), low),
        in_specs=[vmem] * 6,
        out_specs=vmem,
        scratch_shapes=[
            pltpu.VMEM((rows, wide), low),
            pltpu.VMEM((8, 2 * TILE, wide), low),
            pltpu.VMEM((8, 2 * TILE, wide), low),
            pltpu.VMEM((8, 1, 2 * TILE), jnp.float32),
            pltpu.VMEM((8, 2 * TILE, wide), jnp.float32),
            pltpu.VMEM((3, 8, TILE, wide), low),
            pltpu.SemaphoreType.DMA((8,)),
            pltpu.SemaphoreType.DMA((8,)),
            pltpu.SemaphoreType.DMA((3, 8)),
            pltpu.SemaphoreType.DMA((3, 8)),
        ],
        compiler_params=pltpu.CompilerParams(
            collective_id=collective_id, has_side_effects=True, vmem_limit_bytes=60 * 2**20
        ),
        name="attention_backward",
    )(grad_mixed, joined, mixed, log_total, blocks.reshape(rows, 1), blocks.reshape(1, rows))


FF_BLOCK = 512


def feed_kernel(
    inner_ref, hidden_ref, upstream_ref, gain_ref, up_ref, down_ref,
    out_ref, grad_inner_ref, gain_grad_ref, grad_up_ref, grad_down_ref,
    turned_ref, slope_ref, active_ref, lowered_ref, grad_ref,
):
    step = pl.program_id(0)
    blocks = slope_ref.shape[0]

    @pl.when(step == 0)
    def _():
        lowered_ref[...] = jnp.zeros_like(lowered_ref)
        grad_inner_ref[...] = jnp.zeros_like(grad_inner_ref)
        turned_ref[...] = jnp.transpose(inner_ref[...])

    @pl.when(step < blocks)
    def _():
        lifted = nn(inner_ref[...], up_ref[...])
        share = 0.5 + 0.5 * lax.erf(lifted * 0.5**0.5)
        slope_ref[step] = share + lifted * jnp.exp(lifted * lifted * -0.5) * (2 * math.pi) ** -0.5
        active = (lifted * share).astype(jnp.bfloat16)
        active_ref[step] = active
        lowered_ref[...] += nn(active, down_ref[...])

    @pl.when(step == blocks - 1)
    def _():
        lowered = lowered_ref[...]
        centre = lowered - jnp.mean(lowered, axis=-1, keepdims=True)
        inverse = lax.rsqrt(jnp.mean(centre * centre, axis=-1, keepdims=True) + EPS)
        unit = centre * inverse
        gain = gain_ref[...]
        out_ref[...] = (hidden_ref[...] + unit * gain).astype(jnp.bfloat16)
        upstream = upstream_ref[...].astype(jnp.float32)
        gain_grad_ref[...] = jnp.sum(upstream * unit, axis=0, keepdims=True)
        scaled = upstream * gain
        mean = jnp.mean(scaled, axis=-1, keepdims=True)
        along = jnp.mean(scaled * unit, axis=-1, keepdims=True)
        grad_ref[...] = ((scaled - mean - unit * along) * inverse).astype(jnp.bfloat16)

    @pl.when(step >= blocks)
    def _():
        block = step - blocks
        grad = grad_ref[...]
        grad_lifted = (nt(grad, down_ref[...]) * slope_ref[block]).astype(jnp.bfloat16)
        grad_up_ref[...] = nn(turned_ref[...], grad_lifted).astype(jnp.bfloat16)
        grad_down_ref[...] = tn(active_ref[block], grad).astype(jnp.bfloat16)
        grad_inner_ref[...] += nt(grad_lifted, up_ref[...])


def feed_forward(inner, hidden, upstream, gain, full_up, full_down):
    tokens, width = inner.shape
    blocks = full_up.shape[1] // FF_BLOCK
    low = jnp.bfloat16
    whole = pl.BlockSpec((tokens, width), lambda i: (0, 0))
    row = pl.BlockSpec((1, width), lambda i: (0, 0))
    at = lambda i: lax.rem(i, blocks)
    late = lambda i: jnp.maximum(i - blocks, 0)
    return pl.pallas_call(
        feed_kernel,
        grid=(2 * blocks,),
        out_shape=(
            jax.ShapeDtypeStruct((tokens, width), low),
            jax.ShapeDtypeStruct((tokens, width), jnp.float32),
            jax.ShapeDtypeStruct((1, width), jnp.float32),
            jax.ShapeDtypeStruct(full_up.shape, low),
            jax.ShapeDtypeStruct(full_down.shape, low),
        ),
        in_specs=[
            whole,
            whole,
            whole,
            row,
            pl.BlockSpec((width, FF_BLOCK), lambda i: (0, at(i))),
            pl.BlockSpec((FF_BLOCK, width), lambda i: (at(i), 0)),
        ],
        out_specs=(
            whole,
            whole,
            row,
            pl.BlockSpec((width, FF_BLOCK), lambda i: (0, late(i))),
            pl.BlockSpec((FF_BLOCK, width), lambda i: (late(i), 0)),
        ),
        scratch_shapes=[
            pltpu.VMEM((width, tokens), low),
            pltpu.VMEM((blocks, tokens, FF_BLOCK), jnp.float32),
            pltpu.VMEM((blocks, tokens, FF_BLOCK), low),
            pltpu.VMEM((tokens, width), jnp.float32),
            pltpu.VMEM((tokens, width), low),
        ],
        compiler_params=pltpu.CompilerParams(vmem_limit_bytes=60 * 2**20),
        name="feed_forward",
    )(inner, hidden, upstream, gain, full_up, full_down)


TILE = 256


def nt(left, right):
    return lax.dot_general(
        left, right, (((1,), (1,)), ((), ())), preferred_element_type=jnp.float32
    )


def nn(left, right):
    return lax.dot_general(
        left, right, (((1,), (0,)), ((), ())), preferred_element_type=jnp.float32
    )


def tn(left, right):
    return lax.dot_general(
        left, right, (((0,), (0,)), ((), ())), preferred_element_type=jnp.float32
    )


def both_heads(rows):
    lane = lax.broadcasted_iota(jnp.int32, rows.shape, 1)
    zero = jnp.zeros_like(rows)
    return jnp.concatenate(
        [jnp.where(lane < HD, rows, zero), jnp.where(lane < HD, zero, rows)], axis=0
    )


def own_lanes(pair):
    half = pair.shape[0] // 2
    lane = lax.broadcasted_iota(jnp.int32, (half, pair.shape[1]), 1)
    return jnp.where(lane < HD, pair[:half], pair[half:])


def fast_body(
    tokens_in, block_ids, w_query, w_key, w_value, w_out, w_up, w_down, norm_gain, cotangent
):
    width = tokens_in.shape[2]
    groups = lax.axis_size("ctx")
    kinds = norm_gain.shape[0]
    small = jnp.concatenate(
        [norm_gain.astype(jnp.float32).reshape(1, -1), block_ids.astype(jnp.float32).reshape(-1, 128)]
    )
    small = jnp.pad(small, ((0, 8 - small.shape[0]), (0, 0)))
    smalls, full_query, full_key, full_value, full_out, full_up, full_down = gather_over_devices(
        [small, w_query, w_key, w_value, w_out, w_up, w_down], 1
    )
    smalls = smalls.reshape(32, 8, 128)
    gains = smalls[:, 0].reshape(32, kinds, -1).transpose(1, 0, 2).reshape(kinds, width)
    blocks = lax.dynamic_slice_in_dim(smalls, lax.axis_index("fsdp") * groups, groups, 0)
    blocks = blocks[:, 1:3].reshape(-1).astype(jnp.int32)
    tokens = tokens_in[0].astype(jnp.float32)
    normed = layer_norm(tokens, gains[0]).astype(jnp.bfloat16)
    queries = jnp.concatenate(
        [project(normed, w).astype(jnp.bfloat16) for w in (full_query, full_key, full_value)], axis=1
    )
    joined, mixed, log_total, mixed_low = attention_forward(queries, blocks, 2)
    branch = project(mixed_low, full_out)
    hidden = tokens + layer_norm(branch, gains[1])
    inner = layer_norm(hidden, gains[2]).astype(jnp.bfloat16)
    upstream = cotangent[0].astype(jnp.float32)
    layer_out, grad_inner, gain_four, grad_up, grad_down = feed_forward(
        inner, hidden, cotangent[0], gains[3:], full_up, full_down
    )
    layer_out, gain_four = layer_out[None], gain_four[0]
    unused_three, pull_three = jax.vjp(layer_norm, hidden, gains[2])
    grad_hidden_branch, gain_three = pull_three(grad_inner)
    grad_hidden = upstream + grad_hidden_branch
    unused_two, pull_two = jax.vjp(layer_norm, branch, gains[1])
    grad_branch, gain_two = pull_two(grad_hidden)
    grad_branch = grad_branch.astype(jnp.bfloat16)
    grad_out = outer_sum(mixed_low, grad_branch).astype(jnp.bfloat16)
    grad_mixed = back_project(grad_branch, full_out).astype(jnp.bfloat16)
    grad_qkv = attention_backward(grad_mixed, joined, mixed, log_total, blocks, 4)
    grad_three = outer_sum(normed, grad_qkv).astype(jnp.bfloat16)
    grad_normed = (
        back_project(grad_qkv[:, :width], full_query)
        + back_project(grad_qkv[:, width : 2 * width], full_key)
        + back_project(grad_qkv[:, 2 * width :], full_value)
    )
    unused_one, pull_one = jax.vjp(layer_norm, tokens, gains[0])
    grad_norm_in, gain_one = pull_one(grad_normed)
    grad_tokens = (grad_hidden + grad_norm_in).astype(jnp.bfloat16)[None]
    gain_grads = jnp.stack([gain_one, gain_two, gain_three, gain_four])
    sums, gain_sum = sum_over_devices(
        [grad_three, grad_out, grad_up, grad_down], by_owner(gain_grads), 3
    )
    return (
        layer_out,
        grad_tokens,
        *(sums[2 * k : 2 * k + 2].reshape(w_out.shape) for k in range(4)),
        sums[8:16].reshape(-1, w_up.shape[0], LANES).transpose(1, 0, 2).reshape(w_up.shape),
        sums[16:].reshape(w_down.shape),
        gain_sum[0].reshape(norm_gain.shape),
    )


def by_owner(gain_grads):
    kinds, width = gain_grads.shape
    rows = gain_grads.reshape(kinds, 32, width // 32).transpose(1, 0, 2).reshape(32, 1, -1)
    return jnp.pad(rows, ((0, 0), (0, 7), (0, 0))).reshape(2, 2, 4, 2, 8, rows.shape[-1])


def pick(mesh):
    return fast_body if mesh.shape["ctx"] * 2 == HEADS else body


def solution(mesh):
    placed = (
        P("fsdp", "ctx", None),
        P("fsdp", "ctx"),
        P(("fsdp", "ctx"), None),
        P(("fsdp", "ctx"), None),
        P(("fsdp", "ctx"), None),
        P(("fsdp", "ctx"), None),
        P(("fsdp", "ctx"), None),
        P(("fsdp", "ctx"), None),
        P(None, ("fsdp", "ctx")),
        P("fsdp", "ctx", None),
    )
    return jax.shard_map(
        pick(mesh),
        mesh=mesh,
        in_specs=placed,
        out_specs=(
            P("fsdp", "ctx", None),
            P("fsdp", "ctx", None),
            P(("fsdp", "ctx"), None),
            P(("fsdp", "ctx"), None),
            P(("fsdp", "ctx"), None),
            P(("fsdp", "ctx"), None),
            P(("fsdp", "ctx"), None),
            P(("fsdp", "ctx"), None),
            P(None, ("fsdp", "ctx")),
        ),
        check_vma=False,
    )
```
